512 devices in a mesh: gx: 64 (over y, z_lo, core), gy: 8 (over z_hi, x).
Axes of the slice: x: 4, y: 8, z: 8 (z_hi: 2, z_lo: 4; z = z_hi * 4 + z_lo), core: 2. Of those that a mesh axis runs over, the one named last changes fastest.
Arguments:
- pops: float32 [19, 256, 64, 128], P(None, 'gx', 'gy'), may hold values from 0.005 to 0.5, as said below
- label: int32 [256, 64, 128], P('gx', 'gy'), may hold values from 0 to 2, as said below
- drive: float32 [3, 256, 64, 128], P(None, 'gx', 'gy'), may hold values from -0.3 to 0.3
Outputs:
- momentum: float32 [3, 256, 64, 128], P(None, 'gx', 'gy')
- running: float32 [3, 64, 16, 32], P(None, 'gx', 'gy')
The draws below stay inside these ranges and needn't reach their ends.
Inputs may be any that keep to these rules, and one draw needn't show every extreme that they name: `pops`: populations near a local equilibrium with density 0.8 to 1.2 and each velocity component within 0.1. `label`: 2 marks walls: every cell with z index 0 or 127, and scattered obstacle cells; elsewhere 1 marks the second solution, 0 the first.
All inputs are finite; a program needn't handle non-finite values.
Results may differ from the reference program's by a relative error of at most 0.0003.
Values sent between devices are 32-bit elements; how exact they have to be, the bound alone decides.
No kernel may reach another device: no remote copies, remote signals or barrier semaphores. Data moves between devices by JAX's collectives and lax.ppermute only.
A program may use at most 64 MiB of HBM per device.

```python
import math
import jax
import jax.numpy as jnp

NZ = 128
STEPS = 4
NX = 256
NY = 64
SX = 64
SY = 16
SZ = 32


VELOCITY = [[0, 0, 0], [1, 0, 0], [-1, 0, 0], [0, 1, 0], [0, -1, 0], [0, 0, 1], [0, 0, -1], [1, 1, 0], [-1, -1, 0], [1, -1, 0], [-1, 1, 0], [1, 0, 1], [-1, 0, -1], [1, 0, -1], [-1, 0, 1], [0, 1, 1], [0, -1, -1], [0, 1, -1], [0, -1, 1]]


WEIGHTS = [1.0 / 3.0] + [1.0 / 18.0] * 6 + [1.0 / 36.0] * 12


def draw_pops(key, part):
    density = 1.0 + 0.2 * jax.random.uniform(jax.random.fold_in(key, 11), (NX, NY, NZ), jnp.float32, -1.0, 1.0)
    rough = 0.1 * jax.random.uniform(jax.random.fold_in(key, 12), (3, NX, NY, NZ), jnp.float32, -1.0, 1.0)
    speed = rough
    columns = [jnp.array([row[axis_id] for row in VELOCITY], jnp.float32).reshape(19, 1, 1, 1) for axis_id in range(3)]
    weights = jnp.array(WEIGHTS, jnp.float32).reshape(19, 1, 1, 1)
    along = columns[0] * speed[0] + columns[1] * speed[1] + columns[2] * speed[2]
    square = speed[0] * speed[0] + speed[1] * speed[1] + speed[2] * speed[2]
    balance = weights * density * (1.0 + 3.0 * along + 4.5 * along * along - 1.5 * square)
    noise = 1.0 + 0.1 * jax.random.uniform(jax.random.fold_in(key, 13), (19, NX, NY, NZ), jnp.float32, -1.0, 1.0)
    return (balance * noise).astype(jnp.float32)


def draw_label(key, part):
    offsets = jax.random.randint(jax.random.fold_in(key, 21), (NX, 1, 1), -(NY // 4), NY // 4 + 1)
    rows = jnp.arange(NY, dtype=jnp.int32).reshape(1, NY, 1)
    depth = jnp.arange(NZ, dtype=jnp.int32).reshape(1, 1, NZ)
    second = (rows >= NY // 2 + offsets).astype(jnp.int32) + jnp.zeros((NX, NY, NZ), jnp.int32)
    obstacle = jax.random.randint(jax.random.fold_in(key, 22), (NX, NY, NZ), 0, 64) == 0
    wall = jnp.logical_or(jnp.logical_or(depth == 0, depth == NZ - 1), obstacle)
    return jnp.where(wall, 2, second).astype(jnp.int32)


def levels(stream_key, dims, cuts, least, high):
    def one(axis_at, shards_of):
        heights = jax.random.uniform(jax.random.fold_in(jax.random.fold_in(stream_key, 6), axis_at), (shards_of,), jnp.float32, least / len(cuts), high / len(cuts))
        return jnp.repeat(jnp.exp(heights), dims[axis_at] // shards_of).reshape((-1,) + (1,) * (len(dims) - axis_at - 1))

    gain = one(*cuts[0])
    for cut in cuts[1:]:
        gain = gain * one(*cut)
    return gain


def bell_draw(rng, dims, width, limit, cuts=(), kind=jnp.bfloat16):
    values = width * jax.random.normal(rng, dims, jnp.float32)
    if cuts:
        values = values * levels(rng, dims, cuts, -0.22, 0.18)
    return jnp.clip(values, -limit, limit).astype(kind)


def setup_inputs(seed: int = 0) -> dict:
    arg_keys = jax.random.split(jax.random.key(seed), 4)
    pops = draw_pops(jax.random.fold_in(arg_keys[3], 71), 0)
    label = draw_label(jax.random.fold_in(arg_keys[3], 71), 0)
    drive = bell_draw(arg_keys[2], (3, NX, NY, NZ), 0.05, 0.3, ((1, 64), (2, 8)), jnp.float32)
    return {"pops": pops, "label": label, "drive": drive}


VELOCITY = [[0, 0, 0], [1, 0, 0], [-1, 0, 0], [0, 1, 0], [0, -1, 0], [0, 0, 1], [0, 0, -1],
            [1, 1, 0], [-1, -1, 0], [1, -1, 0], [-1, 1, 0], [1, 0, 1], [-1, 0, -1], [1, 0, -1], [-1, 0, 1],
            [0, 1, 1], [0, -1, -1], [0, 1, -1], [0, -1, 1]]
OPPOSITE = [0, 2, 1, 4, 3, 6, 5, 8, 7, 10, 9, 12, 11, 14, 13, 16, 15, 18, 17]
WEIGHTS = [1.0 / 3.0] + [1.0 / 18.0] * 6 + [1.0 / 36.0] * 12
PAIRS = [(0, 0), (1, 1), (2, 2), (0, 1), (0, 2), (1, 2)]
COMPONENT = [[0, 3, 4], [3, 1, 5], [4, 5, 2]]
SLOW_VISCOSITY = 0.0004


def collide(pops, label, drive, phase):
    columns = [jnp.array([row[axis_id] for row in VELOCITY], jnp.float32).reshape(19, 1, 1, 1) for axis_id in range(3)]
    weights = jnp.array(WEIGHTS, jnp.float32).reshape(19, 1, 1, 1)
    density = jnp.sum(pops, axis=0)
    moment = [jnp.sum(columns[axis_id] * pops, axis=0) for axis_id in range(3)]
    speed = [moment[axis_id] / density for axis_id in range(3)]
    along = columns[0] * speed[0] + columns[1] * speed[1] + columns[2] * speed[2]
    square = speed[0] * speed[0] + speed[1] * speed[1] + speed[2] * speed[2]
    balance = weights * density * (1.0 + 3.0 * along + 4.5 * along * along - 1.5 * square)
    second = label == 1
    solid = label == 2
    omega = jnp.where(second, 1.1, 1.6)
    strength = jnp.where(second, 0.6, 1.0) * phase
    push = columns[0] * drive[0] + columns[1] * drive[1] + columns[2] * drive[2]
    relaxed = pops - omega * (pops - balance) + 3.0 * weights * strength * push
    bounced = jnp.stack([pops[other] for other in OPPOSITE])
    post = jnp.where(solid, bounced, relaxed)
    fluid = jnp.where(solid, 0.0, 1.0)
    stress = jnp.stack([moment[first] * moment[later] / density * fluid for first, later in PAIRS])
    return post, stress


def momentum_of(pops):
    columns = [jnp.array([row[axis_id] for row in VELOCITY], jnp.float32).reshape(19, 1, 1, 1) for axis_id in range(3)]
    return jnp.stack([jnp.sum(columns[axis_id] * pops, axis=0) for axis_id in range(3)])


def reference(pops, label, drive):
    state = pops
    total = jnp.zeros((6,) + pops.shape[1:], jnp.float32)
    for step in range(STEPS):
        phase = math.cos(2.0 * math.pi * (step + 0.5) / STEPS)
        post, stress = collide(state, label, drive, phase)
        total = total + stress
        state = jnp.stack([jnp.roll(post[index], (VELOCITY[index][0], VELOCITY[index][1], VELOCITY[index][2]), axis=(0, 1, 2)) for index in range(19)])
    momentum = momentum_of(state)
    slow = (total / STEPS).reshape(6, SX, 4, SY, 4, SZ, 4).mean(axis=(2, 4, 6))
    spectrum = jnp.fft.fftn(slow, axes=(1, 2, 3))
    wave_x = (2.0 * math.pi * jnp.fft.fftfreq(SX)).reshape(SX, 1, 1)
    wave_y = (2.0 * math.pi * jnp.fft.fftfreq(SY)).reshape(1, SY, 1)
    wave_z = (2.0 * math.pi * jnp.fft.fftfreq(SZ)).reshape(1, 1, SZ)
    waves = [wave_x, wave_y, wave_z]
    force = [-1j * (waves[0] * spectrum[COMPONENT[first][0]] + waves[1] * spectrum[COMPONENT[first][1]] + waves[2] * spectrum[COMPONENT[first][2]]) for first in range(3)]
    wave_sq = wave_x * wave_x + wave_y * wave_y + wave_z * wave_z
    positive = wave_sq > 0
    safe = jnp.where(positive, wave_sq, 1.0)
    inner = waves[0] * force[0] + waves[1] * force[1] + waves[2] * force[2]
    velocity = jnp.stack([jnp.where(positive, (force[first] - waves[first] * inner / safe) / (SLOW_VISCOSITY * safe), 0.0) for first in range(3)])
    running = jnp.real(jnp.fft.ifftn(velocity, axes=(1, 2, 3))).astype(jnp.float32)
    return momentum, running
```

```python
import functools
import math

import jax
import jax.numpy as jnp
import numpy as np
from jax import lax
from jax.experimental import pallas as pl
from jax.experimental.pallas import tpu as pltpu
from jax.sharding import PartitionSpec as P

NZ = 128
STEPS = 4
SZ = 32
LX = 4
LY = 8
VELOCITY = [
    [0, 0, 0],
    [1, 0, 0],
    [-1, 0, 0],
    [0, 1, 0],
    [0, -1, 0],
    [0, 0, 1],
    [0, 0, -1],
    [1, 1, 0],
    [-1, -1, 0],
    [1, -1, 0],
    [-1, 1, 0],
    [1, 0, 1],
    [-1, 0, -1],
    [1, 0, -1],
    [-1, 0, 1],
    [0, 1, 1],
    [0, -1, -1],
    [0, 1, -1],
    [0, -1, 1],
]
OPPOSITE = [0, 2, 1, 4, 3, 6, 5, 8, 7, 10, 9, 12, 11, 14, 13, 16, 15, 18, 17]
WEIGHTS = [1.0 / 3.0] + [1.0 / 18.0] * 6 + [1.0 / 36.0] * 12
PAIRS = [(0, 0), (1, 1), (2, 2), (0, 1), (0, 2), (1, 2)]
COMPONENT = [[0, 3, 4], [3, 1, 5], [4, 5, 2]]
SLOW_VISCOSITY = 0.0004
PHASES = [math.cos(2.0 * math.pi * (step + 0.5) / STEPS) for step in range(STEPS)]

CHANNELS = 23
CX = [v[0] for v in VELOCITY] + [0] * 4
CY = [v[1] for v in VELOCITY] + [0] * 4
HIGHEST = lax.Precision.HIGHEST


def pack_y(sign):
    out, at = [], 0
    for x in range(LX):
        for ch in range(CHANNELS):
            n = 3 if CY[ch] == sign else 2
            out.append((ch, x, LY - n if sign > 0 else 0, n, at))
            at += n
    return out, -(-at // 8) * 8


def pack_x(sign):
    out, at = [], 0
    layers = (3, 2, 1) if sign > 0 else (0, 1, 2)
    for depth, x in enumerate(layers):
        for ch in range(CHANNELS):
            if depth == 2 and CX[ch] != sign:
                continue
            low = 3 if CY[ch] == 1 else 2
            high = 3 if CY[ch] == -1 else 2
            out.append((ch, x, low, high, at))
            at += low + LY + high
    return out, -(-at // 8) * 8


Y_UP, Y_ROWS = pack_y(1)
Y_DOWN, _ = pack_y(-1)
X_RIGHT, X_ROWS = pack_x(1)
X_LEFT, _ = pack_x(-1)
Y_UP_AT = {(ch, x): (n, at) for ch, x, _, n, at in Y_UP}
Y_DOWN_AT = {(ch, x): (n, at) for ch, x, _, n, at in Y_DOWN}
UP = [i for i in range(19) if CY[i] == 1]
DOWN = [i for i in range(19) if CY[i] == -1]
RIGHT = [i for i in range(19) if CX[i] == 1]
LEFT = [i for i in range(19) if CX[i] == -1]
EDGE_Y_ROWS = 24
EDGE_X_ROWS = 40


def collide(f, label, drive, phase):
    rho = f[0]
    for i in range(1, 19):
        rho = rho + f[i]
    j = []
    for axis in range(3):
        total = None
        for i in range(1, 19, 2):
            c = VELOCITY[i][axis]
            if c == 0:
                continue
            term = f[i] - f[i + 1] if c > 0 else f[i + 1] - f[i]
            total = term if total is None else total + term
        j.append(total)
    second = label == 1.0
    solid = label == 2.0
    omega = jnp.where(second, 1.1, 1.6)
    keep = 1.0 - omega
    strength = jnp.where(second, 0.6 * phase, phase)
    inverse = 1.0 / rho
    mix = [omega * j[axis] + strength * drive[axis] for axis in range(3)]
    base = omega * (rho - 1.5 * (j[0] * j[0] + j[1] * j[1] + j[2] * j[2]) * inverse)
    curve = 4.5 * omega * inverse

    def along(vector, c):
        total = None
        for axis in range(3):
            if c[axis] == 0:
                continue
            if total is None:
                total = vector[axis] if c[axis] > 0 else -vector[axis]
            else:
                total = total + vector[axis] if c[axis] > 0 else total - vector[axis]
        return total

    post = [None] * 19
    post[0] = jnp.where(solid, f[0], keep * f[0] + WEIGHTS[0] * base)
    for i in range(1, 19, 2):
        w = WEIGHTS[i]
        cj = along(j, VELOCITY[i])
        even = w * (base + curve * (cj * cj))
        odd = (3.0 * w) * along(mix, VELOCITY[i])
        post[i] = jnp.where(solid, f[i + 1], keep * f[i] + (even + odd))
        post[i + 1] = jnp.where(solid, f[i], keep * f[i + 1] + (even - odd))
    fluid = jnp.where(solid, 0.0, inverse)
    stress = [j[a] * j[b] * fluid for a, b in PAIRS]
    return post, stress


def first_kernel(pops, label, drive, cells, total, send_a, send_b, box):
    up = lax.rem(lax.axis_index("gy"), 2)
    down = 1 - up
    sums = [jnp.zeros((LY, NZ), jnp.float32)] * 6
    for x in range(LX):
        f = [pops[i, x] for i in range(19)]
        lab = label[x].astype(jnp.float32)
        force = [drive[axis, x] for axis in range(3)]
        post, stress = collide(f, lab, force, PHASES[0])
        for i in range(19):
            cells[i, x] = post[i]
        cells[19, x] = lab
        for axis in range(3):
            cells[20 + axis, x] = force[axis]
        sums = [sums[k] + stress[k] for k in range(6)]
    for k in range(6):
        total[k] = sums[k]
    for ch, x, row, n, at in Y_UP:
        box[up, at : at + n, :] = cells[ch, x, row : row + n, :]
    for ch, x, row, n, at in Y_DOWN:
        box[down, at : at + n, :] = cells[ch, x, row : row + n, :]
    send_a[...] = box[0]
    send_b[...] = box[1]


def second_kernel(cells, got_a, got_b, send_a, send_b, rows, box):
    odd_y = lax.rem(lax.axis_index("gy"), 2)
    low_slot, high_slot = 1 - odd_y, odd_y
    right = lax.rem(lax.axis_index("gx"), 2)
    rows[0] = got_a[...]
    rows[1] = got_b[...]
    for slot, entries in ((right, X_RIGHT), (1 - right, X_LEFT)):
        for ch, x, low, high, at in entries:
            n, source = Y_UP_AT[ch, x]
            box[slot, at : at + n, :] = rows[low_slot, source : source + n, :]
            box[slot, at + low : at + low + LY, :] = cells[ch, x]
            n, source = Y_DOWN_AT[ch, x]
            box[slot, at + low + LY : at + low + LY + n, :] = rows[high_slot, source : source + n, :]
    send_a[...] = box[0]
    send_b[...] = box[1]


ROW0 = 12
COL0 = 3


def third_kernel(
    cells, total, ya, yb, xa, xb, post3, spread, edge_a, edge_b, rows, cols, one, two, aux, sums, box
):
    odd_y = lax.rem(lax.axis_index("gy"), 2)
    odd_x = lax.rem(lax.axis_index("gx"), 2)
    low_slot, high_slot = 1 - odd_y, odd_y
    left_slot, right_slot = 1 - odd_x, odd_x
    rows[0] = ya[...]
    rows[1] = yb[...]
    cols[0] = xa[...]
    cols[1] = xb[...]

    def place(ch, x, row, values):
        n = values.shape[0]
        if ch < 19:
            one[ch, x + COL0, row + ROW0 : row + ROW0 + n, :] = values
        else:
            aux[ch - 19, x + COL0, row + ROW0 : row + ROW0 + n, :] = values

    for ch in range(CHANNELS):
        for x in range(LX):
            place(ch, x, 0, cells[ch, x])
    for ch, x, row, n, at in Y_UP:
        place(ch, x, row - LY, rows[low_slot, at : at + n, :])
    for ch, x, row, n, at in Y_DOWN:
        place(ch, x, row + LY, rows[high_slot, at : at + n, :])
    for ch, x, low, high, at in X_RIGHT:
        place(ch, x - LX, -low, cols[left_slot, at : at + low + LY + high, :])
    for ch, x, low, high, at in X_LEFT:
        place(ch, x + LX, -low, cols[right_slot, at : at + low + LY + high, :])

    def arrive(source, x, row, n):
        f = []
        for i in range(19):
            cx, cy, cz = VELOCITY[i]
            value = source[i, x - cx, row - cy : row - cy + n, :]
            f.append(pltpu.roll(value, cz % NZ, 1) if cz else value)
        lab = aux[0, x, row : row + n, :]
        force = [aux[1 + axis, x, row : row + n, :] for axis in range(3)]
        return f, lab, force

    wide = 16
    start = ROW0 - 4
    sums[...] = jnp.zeros(sums.shape, jnp.float32)
    for step, source, target, least, most in ((1, one, two, 1, 9), (2, two, one, 2, 8)):

        def layer(x, carry, step=step, source=source, target=target):
            f, lab, force = arrive(source, x, start, wide)
            post, stress = collide(f, lab, force, PHASES[step])
            for i in range(19):
                target[i, x, start : start + wide, :] = post[i]
            own = jnp.logical_and(x >= COL0, x < COL0 + LX)
            for k in range(6):
                sums[k] += jnp.where(own, stress[k], 0.0)
            return carry

        lax.fori_loop(least, most, layer, 0)
    last = [total[k] + sums[k, 4:12, :] for k in range(6)]
    for x in range(LX):
        f, lab, force = arrive(one, x + COL0, ROW0, LY)
        post, stress = collide(f, lab, force, PHASES[3])
        for i in range(19):
            post3[i, x] = post[i]
        last = [last[k] + stress[k] for k in range(6)]
    stacked = jnp.concatenate(last, axis=0)
    r = lax.broadcasted_iota(jnp.int32, (16, 48), 0)
    c = lax.broadcasted_iota(jnp.int32, (16, 48), 1)
    chosen = jnp.logical_and((r & 7) == (c >> 3), (r >> 3) == ((c & 7) >> 2))
    left = jnp.where(chosen, 1.0, 0.0)
    halves = jnp.dot(left, stacked, precision=HIGHEST, preferred_element_type=jnp.float32)
    z = lax.broadcasted_iota(jnp.int32, (NZ, NZ), 0)
    lane = lax.broadcasted_iota(jnp.int32, (NZ, NZ), 1)
    mean = 1.0 / (STEPS * 64)
    slow = jnp.zeros((8, NZ), jnp.float32)
    for half in range(2):
        table = jnp.where(lane == (z >> 2) + half * SZ, mean, 0.0)
        slow = slow + jnp.dot(
            halves[half * 8 : half * 8 + 8],
            table,
            precision=HIGHEST,
            preferred_element_type=jnp.float32,
        )
    for d in range(spread.shape[0]):
        spread[d] = slow
    for k, i in enumerate(UP):
        for x in range(LX):
            box[odd_y, k * LX + x : k * LX + x + 1, :] = post3[i, x, LY - 1 : LY, :]
    for k, i in enumerate(DOWN):
        for x in range(LX):
            box[1 - odd_y, k * LX + x : k * LX + x + 1, :] = post3[i, x, 0:1, :]
    edge_a[...] = box[0]
    edge_b[...] = box[1]


def edge_kernel(post3, ya, yb, send_a, send_b, rows, box):
    odd_y = lax.rem(lax.axis_index("gy"), 2)
    low_slot, high_slot = 1 - odd_y, odd_y
    right = lax.rem(lax.axis_index("gx"), 2)
    rows[0] = ya[...]
    rows[1] = yb[...]
    for slot, comps, x in ((right, RIGHT, LX - 1), (1 - right, LEFT, 0)):
        for k, i in enumerate(comps):
            at = k * LY
            if CY[i] == 0:
                box[slot, at : at + LY, :] = post3[i, x]
            elif CY[i] == 1:
                source = UP.index(i) * LX + x
                box[slot, at : at + 1, :] = rows[low_slot, source : source + 1, :]
                box[slot, at + 1 : at + LY, :] = post3[i, x, 0 : LY - 1, :]
            else:
                source = DOWN.index(i) * LX + x
                box[slot, at : at + LY - 1, :] = post3[i, x, 1:LY, :]
                box[slot, at + LY - 1 : at + LY, :] = rows[high_slot, source : source + 1, :]
    send_a[...] = box[0]
    send_b[...] = box[1]


def momentum_kernel(post3, ya, yb, xa, xb, out, rows, cols, work):
    odd_y = lax.rem(lax.axis_index("gy"), 2)
    odd_x = lax.rem(lax.axis_index("gx"), 2)
    rows[0] = ya[...]
    rows[1] = yb[...]
    cols[0] = xa[...]
    cols[1] = xb[...]
    for i in range(1, 19):
        for x in range(LX):
            work[i, x + 1, 8:16, :] = post3[i, x]
    for k, i in enumerate(UP):
        for x in range(LX):
            at = k * LX + x
            work[i, x + 1, 7:8, :] = rows[1 - odd_y, at : at + 1, :]
    for k, i in enumerate(DOWN):
        for x in range(LX):
            at = k * LX + x
            work[i, x + 1, 16:17, :] = rows[odd_y, at : at + 1, :]
    for k, i in enumerate(RIGHT):
        work[i, 0, 8 - CY[i] : 16 - CY[i], :] = cols[1 - odd_x, k * LY : k * LY + LY, :]
    for k, i in enumerate(LEFT):
        work[i, LX + 1, 8 - CY[i] : 16 - CY[i], :] = cols[odd_x, k * LY : k * LY + LY, :]
    for x in range(LX):
        f = [None]
        for i in range(1, 19):
            cx, cy, cz = VELOCITY[i]
            value = work[i, x + 1 - cx, 8 - cy : 16 - cy, :]
            f.append(pltpu.roll(value, cz % NZ, 1) if cz else value)
        for axis in range(3):
            total = None
            for i in range(1, 19, 2):
                c = VELOCITY[i][axis]
                if c == 0:
                    continue
                term = f[i] - f[i + 1] if c > 0 else f[i + 1] - f[i]
                total = term if total is None else total + term
            out[axis, x] = total


LANES = 384


@functools.cache
def operator_tables(sx, sy):
    waves = [2.0 * math.pi * np.fft.fftfreq(n) for n in (sx, sy, SZ)]
    k = np.meshgrid(*waves, indexing="ij")
    square = k[0] ** 2 + k[1] ** 2 + k[2] ** 2
    positive = square > 0
    safe = np.where(positive, square, 1.0)
    half = SZ // 2 + 1
    modes = sy * half
    table = np.zeros((18, sx, LANES))
    twist = np.zeros((24, LANES))
    imaginary = []
    for a in range(3):
        for c in range(6):
            force = [
                -1j * sum(k[b] for b in range(3) if COMPONENT[first][b] == c) + 0.0 * k[0]
                for first in range(3)
            ]
            inner = k[0] * force[0] + k[1] * force[1] + k[2] * force[2]
            gain = np.where(positive, (force[a] - k[a] * inner / safe) / (SLOW_VISCOSITY * safe), 0.0)
            flipped = gain
            for axis in range(3):
                flipped = np.roll(np.flip(flipped, axis), 1, axis)
            gain = 0.5 * (gain + np.conj(flipped))
            line = np.fft.ifft(gain, axis=0)[:, :, :half].reshape(sx, modes)
            odd_x = (int(a == 0) + sum(int(d == 0) for d in PAIRS[c])) % 2
            imaginary.append(not odd_x)
            table[a * 6 + c, :, :modes] = line.real if odd_x else line.imag
            if odd_x:
                twist[a * 8 + c, :modes] = line.imag[0]
    ky = np.repeat(np.arange(sy), half)
    kz = np.tile(np.arange(half), sy)
    y = np.repeat(np.arange(2), SZ)
    z = np.tile(np.arange(SZ), 2)
    angle = 2.0 * math.pi * (np.outer(y, ky) / sy + np.outer(z, kz) / SZ)
    forward = np.zeros((128, 2 * LANES))
    forward[:64, :modes] = np.cos(angle)
    forward[:64, LANES : LANES + modes] = -np.sin(angle)
    weight = np.where((kz == 0) | (kz == SZ // 2), 1.0, 2.0) / (sy * SZ)
    backward = np.zeros((2 * LANES, 128))
    backward[:modes, :64] = (weight * np.cos(angle)).T
    backward[LANES : LANES + modes, :64] = (-weight * np.sin(angle)).T
    shift = 2.0 * math.pi * np.outer(2 * np.arange(sy // 2), ky) / sy
    turn = np.zeros((sy // 2, 2, LANES))
    turn[:, 0, :modes] = np.cos(shift)
    turn[:, 1, :modes] = np.sin(shift)
    return (
        forward.astype(np.float32),
        turn.astype(np.float32),
        table.astype(np.float32),
        twist.astype(np.float32),
        backward.astype(np.float32),
        tuple(imaginary),
    )


def solve_kernel(imaginary, blocks, forward, turn, table, twist, backward, out, part, hat, field, ring):
    devices = blocks.shape[0]
    sx = table.shape[1]
    me = lax.axis_index("gy")
    here = lax.axis_index("gx")
    part[...] = jnp.dot(
        blocks[...].reshape(devices * 8, NZ),
        forward[...],
        precision=HIGHEST,
        preferred_element_type=jnp.float32,
    ).reshape(devices, 8, 2 * LANES)
    real = jnp.zeros((8, LANES), jnp.float32)
    imag = jnp.zeros((8, LANES), jnp.float32)
    for d in range(devices):
        owner = lax.rem(me + d, devices)
        value = part[owner]
        re, im = value[:, :LANES], value[:, LANES:]
        cosine, sine = turn[d, 0:1, :], turn[d, 1:2, :]
        real = real + re * cosine + im * sine
        imag = imag + im * cosine - re * sine
    for c in range(6):
        hat[c] = jnp.broadcast_to(real[c : c + 1], (8, LANES))
        hat[6 + c] = jnp.broadcast_to(imag[c : c + 1], (8, LANES))
    alternate = jnp.where(lax.broadcasted_iota(jnp.int32, (8, LANES), 0) % 2 == 0, 1.0, -1.0)
    for a in range(3):
        wave = twist[a * 8 : a * 8 + 8, :]
        first_re = -alternate * jnp.sum(wave * imag, axis=0, keepdims=True)
        first_im = alternate * jnp.sum(wave * real, axis=0, keepdims=True)
        for at in range(0, sx, 8):
            re, im = first_re, first_im
            for c in range(6):
                gain = table[a * 6 + c, at : at + 8, :]
                if imaginary[a * 6 + c]:
                    re = re - gain * hat[6 + c]
                    im = im + gain * hat[c]
                else:
                    re = re + gain * hat[c]
                    im = im + gain * hat[6 + c]
            field[at : at + 8, :LANES] = re
            field[at : at + 8, LANES:] = im
        result = jnp.dot(
            field[...], backward[...], precision=HIGHEST, preferred_element_type=jnp.float32
        )[:, :64]
        lane = (a % 2) * 64
        ring[a // 2, 0:sx, lane : lane + 64] = result
        ring[a // 2, sx : 2 * sx, lane : lane + 64] = result
    ring[1, :, 64:128] = jnp.zeros((2 * sx, 64), jnp.float32)
    for t in range(sx):
        for half in range(2):
            out[t, half : half + 1, :] = ring[half, pl.ds(sx - here + t, 1), :]


def last_kernel(parts, out):
    total = jnp.sum(parts[...], axis=0)
    for a in range(3):
        row = total[a // 2 : a // 2 + 1, :]
        for y in range(2):
            lane = (a % 2) * 64 + y * SZ
            value = pltpu.roll(row, (NZ - lane) % NZ, 1) if lane else row
            out[a, 0, y : y + 1, :] = value[:, :SZ]


def call(body, outs, scratch, cost, limit=32):
    spec = pl.BlockSpec(memory_space=pltpu.VMEM)
    shapes = [jax.ShapeDtypeStruct(s, jnp.float32) for s in outs]
    def run(*args):
        return pl.pallas_call(
            body,
            out_shape=shapes,
            in_specs=[spec] * len(args),
            out_specs=[spec] * len(shapes),
            scratch_shapes=[pltpu.VMEM(s, jnp.float32) for s in scratch],
            compiler_params=pltpu.CompilerParams(vmem_limit_bytes=limit << 20),
            cost_estimate=pl.CostEstimate(flops=cost, bytes_accessed=cost, transcendentals=0),
        )(*args)

    return run


def swap(values, axis):
    count = lax.axis_size(axis)
    near = [(i, i ^ 1) for i in range(count)]
    far = [(i, (i + 1) % count if i % 2 else (i - 1) % count) for i in range(count)]
    second = lax.ppermute(values[1], axis, far)
    first = lax.ppermute(values[0], axis, near)
    return first, second


def local(pops, label, drive):
    nx = lax.axis_size("gx")
    ny = lax.axis_size("gy")
    cells, total, ya, yb = call(
        first_kernel,
        [(CHANNELS, LX, LY, NZ), (6, LY, NZ), (Y_ROWS, NZ), (Y_ROWS, NZ)],
        [(2, Y_ROWS, NZ)],
        2_000_000,
    )(pops, label, drive)
    ya, yb = swap((ya, yb), "gy")
    xa, xb = call(
        second_kernel,
        [(X_ROWS, NZ), (X_ROWS, NZ)],
        [(2, Y_ROWS, NZ), (2, X_ROWS, NZ)],
        2_000_000,
    )(cells, ya, yb)
    xa, xb = swap((xa, xb), "gx")
    post3, spread, ea, eb = call(
        third_kernel,
        [(19, LX, LY, NZ), (ny, 8, NZ), (EDGE_Y_ROWS, NZ), (EDGE_Y_ROWS, NZ)],
        [
            (2, Y_ROWS, NZ),
            (2, X_ROWS, NZ),
            (19, LX + 6, 32, NZ),
            (19, LX + 6, 32, NZ),
            (4, LX + 6, 32, NZ),
            (6, 16, NZ),
            (2, EDGE_Y_ROWS, NZ),
        ],
        20_000_000,
    )(cells, total, ya, yb, xa, xb)
    blocks = lax.all_to_all(spread, "gy", 0, 0, tiled=False)
    ea, eb = swap((ea, eb), "gy")
    fa, fb = call(
        edge_kernel,
        [(EDGE_X_ROWS, NZ), (EDGE_X_ROWS, NZ)],
        [(2, EDGE_Y_ROWS, NZ), (2, EDGE_X_ROWS, NZ)],
        200_000,
    )(post3, ea, eb)
    fa, fb = swap((fa, fb), "gx")
    (momentum,) = call(
        momentum_kernel,
        [(3, LX, LY, NZ)],
        [(2, EDGE_Y_ROWS, NZ), (2, EDGE_X_ROWS, NZ), (19, LX + 2, 24, NZ)],
        1_000_000,
    )(post3, ea, eb, fa, fb)
    forward, turn, table, twist, backward, imaginary = operator_tables(nx, 2 * ny)
    (parts,) = call(
        functools.partial(solve_kernel, imaginary),
        [(nx, 2, NZ)],
        [
            (ny, 8, 2 * LANES),
            (12, 8, LANES),
            (nx, 2 * LANES),
            (2, 2 * nx, NZ),
        ],
        10_000_000,
    )(blocks, forward, turn, table, twist, backward)
    parts = lax.all_to_all(parts, "gx", 0, 0, tiled=False)
    (running,) = call(last_kernel, [(3, 1, 2, SZ)], [], 100_000)(parts)
    return momentum, running


def solution(mesh):
    in_specs = (P(None, "gx", "gy", None), P("gx", "gy", None), P(None, "gx", "gy", None))
    out_specs = (P(None, "gx", "gy", None), P(None, "gx", "gy", None))
    return jax.shard_map(local, mesh=mesh, in_specs=in_specs, out_specs=out_specs, check_vma=False)
```

```python
import functools
import math

import jax
import jax.numpy as jnp
import numpy as np
from jax import lax
from jax.experimental import pallas as pl
from jax.experimental.pallas import tpu as pltpu
from jax.sharding import PartitionSpec as P

NZ = 128
STEPS = 4
SZ = 32
LX = 4
LY = 8
VELOCITY = [
    [0, 0, 0],
    [1, 0, 0],
    [-1, 0, 0],
    [0, 1, 0],
    [0, -1, 0],
    [0, 0, 1],
    [0, 0, -1],
    [1, 1, 0],
    [-1, -1, 0],
    [1, -1, 0],
    [-1, 1, 0],
    [1, 0, 1],
    [-1, 0, -1],
    [1, 0, -1],
    [-1, 0, 1],
    [0, 1, 1],
    [0, -1, -1],
    [0, 1, -1],
    [0, -1, 1],
]
OPPOSITE = [0, 2, 1, 4, 3, 6, 5, 8, 7, 10, 9, 12, 11, 14, 13, 16, 15, 18, 17]
WEIGHTS = [1.0 / 3.0] + [1.0 / 18.0] * 6 + [1.0 / 36.0] * 12
PAIRS = [(0, 0), (1, 1), (2, 2), (0, 1), (0, 2), (1, 2)]
COMPONENT = [[0, 3, 4], [3, 1, 5], [4, 5, 2]]
SLOW_VISCOSITY = 0.0004
PHASES = [math.cos(2.0 * math.pi * (step + 0.5) / STEPS) for step in range(STEPS)]

CHANNELS = 23
CX = [v[0] for v in VELOCITY] + [0] * 4
CY = [v[1] for v in VELOCITY] + [0] * 4
HIGHEST = lax.Precision.HIGHEST
GX = ("cy", "zl", "core")
GY = ("zh", "cx")
GROUP = 8


REACH = STEPS - 1


def pack_y(sign):
    out, at = [], 0
    for x in range(LX):
        for ch in range(CHANNELS):
            n = REACH + sign * CY[ch]
            out.append((ch, x, LY - n if sign > 0 else 0, n, at))
            at += n
    return out, -(-at // 8) * 8


def pack_x(sign):
    out, at = [], 0
    for ch in range(CHANNELS):
        n = REACH + sign * CX[ch]
        for x in range(LX - n, LX) if sign > 0 else range(n):
            out.append((ch, x, REACH + CY[ch], REACH - CY[ch], at))
            at += 2 * REACH + LY
    return out, -(-at // 8) * 8


Y_UP, Y_ROWS = pack_y(1)
Y_DOWN, _ = pack_y(-1)
X_RIGHT, X_ROWS = pack_x(1)
X_LEFT, _ = pack_x(-1)
Y_UP_AT = {(ch, x): (n, at) for ch, x, _, n, at in Y_UP}
Y_DOWN_AT = {(ch, x): (n, at) for ch, x, _, n, at in Y_DOWN}


def collide(f, label, drive, phase):
    rho = f[0]
    for i in range(1, 19):
        rho = rho + f[i]
    j = []
    for axis in range(3):
        total = None
        for i in range(1, 19, 2):
            c = VELOCITY[i][axis]
            if c == 0:
                continue
            term = f[i] - f[i + 1] if c > 0 else f[i + 1] - f[i]
            total = term if total is None else total + term
        j.append(total)
    second = label == 1.0
    solid = label == 2.0
    omega = jnp.where(second, 1.1, 1.6)
    keep = 1.0 - omega
    strength = jnp.where(second, 0.6 * phase, phase)
    inverse = 1.0 / rho
    mix = [omega * j[axis] + strength * drive[axis] for axis in range(3)]
    base = omega * (rho - 1.5 * (j[0] * j[0] + j[1] * j[1] + j[2] * j[2]) * inverse)
    curve = 4.5 * omega * inverse

    def along(vector, c):
        total = None
        for axis in range(3):
            if c[axis] == 0:
                continue
            if total is None:
                total = vector[axis] if c[axis] > 0 else -vector[axis]
            else:
                total = total + vector[axis] if c[axis] > 0 else total - vector[axis]
        return total

    post = [None] * 19
    post[0] = jnp.where(solid, f[0], keep * f[0] + WEIGHTS[0] * base)
    for i in range(1, 19, 2):
        w = WEIGHTS[i]
        cj = along(j, VELOCITY[i])
        even = w * (base + curve * (cj * cj))
        odd = (3.0 * w) * along(mix, VELOCITY[i])
        post[i] = jnp.where(solid, f[i + 1], keep * f[i] + (even + odd))
        post[i + 1] = jnp.where(solid, f[i], keep * f[i + 1] + (even - odd))
    fluid = jnp.where(solid, 0.0, inverse)
    stress = [j[a] * j[b] * fluid for a, b in PAIRS]
    return post, stress


def first_kernel(pops_in, label_in, drive_in, cells, total, far, near, box, pops, label, drive, sems):
    copies = [
        pltpu.make_async_copy(source, target, sems.at[k])
        for k, (source, target) in enumerate(((pops_in, pops), (label_in, label), (drive_in, drive)))
    ]
    for copy in copies:
        copy.start()
    for copy in copies:
        copy.wait()
    up = lax.rem(lax.axis_index(GY), 2)
    down = 1 - up
    sums = [jnp.zeros((LY, NZ), jnp.float32)] * 6
    for x in range(LX):
        f = [pops[i, x] for i in range(19)]
        lab = label[x].astype(jnp.float32)
        force = [drive[axis, x] for axis in range(3)]
        post, stress = collide(f, lab, force, PHASES[0])
        for i in range(19):
            cells[i, x] = post[i]
        cells[19, x] = lab
        for axis in range(3):
            cells[20 + axis, x] = force[axis]
        sums = [sums[k] + stress[k] for k in range(6)]
    for k in range(6):
        total[k] = sums[k]
    for ch, x, row, n, at in Y_UP:
        box[up, at : at + n, :] = cells[ch, x, row : row + n, :]
    for ch, x, row, n, at in Y_DOWN:
        box[down, at : at + n, :] = cells[ch, x, row : row + n, :]
    near[...] = box[0]
    far[...] = box[1]


def second_kernel(cells, got_far, got_near, far, near, rows, box):
    odd_y = lax.rem(lax.axis_index(GY), 2)
    low_slot, high_slot = 1 - odd_y, odd_y
    right = lax.rem(lax.axis_index(GX), 2)
    rows[0] = got_near[...]
    rows[1] = got_far[...]
    for slot, entries in ((right, X_RIGHT), (1 - right, X_LEFT)):
        for ch, x, low, high, at in entries:
            n, source = Y_UP_AT[ch, x]
            box[slot, at : at + n, :] = rows[low_slot, source : source + n, :]
            box[slot, at + low : at + low + LY, :] = cells[ch, x]
            n, source = Y_DOWN_AT[ch, x]
            box[slot, at + low + LY : at + low + LY + n, :] = rows[high_slot, source : source + n, :]
    near[...] = box[0]
    far[...] = box[1]


ROW0 = 12
COL0 = 4
WORK_ROWS = 32
WORK_COLS = LX + 8
STATE_ROW0 = 8
STATE_COL0 = 2
STATE_ROWS = 24
STATE_COLS = LX + 4


def arrive(source, x, row, n):
    f = []
    for i in range(19):
        cx, cy, cz = VELOCITY[i]
        value = source[i, x - cx, row - cy : row - cy + n, :]
        f.append(pltpu.roll(value, cz % NZ, 1) if cz else value)
    return f


def around(aux, x, row, n):
    return aux[0, x, row : row + n, :], [aux[1 + axis, x, row : row + n, :] for axis in range(3)]


def third_kernel(
    cells, total, y_far, y_near, x_far, x_near, state, aux, spread, rows, cols, one, mid, sums, two, sem
):
    odd_y = lax.rem(lax.axis_index(GY), 2)
    odd_x = lax.rem(lax.axis_index(GX), 2)
    low_slot, high_slot = 1 - odd_y, odd_y
    left_slot, right_slot = 1 - odd_x, odd_x
    rows[0] = y_near[...]
    rows[1] = y_far[...]
    cols[0] = x_near[...]
    cols[1] = x_far[...]

    def place(ch, x, row, values):
        n = values.shape[0]
        if ch < 19:
            one[ch, x + COL0, row + ROW0 : row + ROW0 + n, :] = values
        else:
            aux[ch - 19, x + COL0, row + ROW0 : row + ROW0 + n, :] = values

    for ch in range(CHANNELS):
        for x in range(LX):
            place(ch, x, 0, cells[ch, x])
    for ch, x, row, n, at in Y_UP:
        place(ch, x, row - LY, rows[low_slot, at : at + n, :])
    for ch, x, row, n, at in Y_DOWN:
        place(ch, x, row + LY, rows[high_slot, at : at + n, :])
    for ch, x, low, high, at in X_RIGHT:
        place(ch, x - LX, -low, cols[left_slot, at : at + low + LY + high, :])
    for ch, x, low, high, at in X_LEFT:
        place(ch, x + LX, -low, cols[right_slot, at : at + low + LY + high, :])

    wide = 16
    start = ROW0 - 4
    sums[...] = jnp.zeros(sums.shape, jnp.float32)
    for step, source, target, back, to in ((1, one, mid, 0, start), (2, mid, two, 2, STATE_ROW0 - 4)):

        def layer(x, carry, step=step, source=source, target=target, back=back, to=to):
            f = arrive(source, x, start, wide)
            lab, force = around(aux, x, start, wide)
            post, stress = collide(f, lab, force, PHASES[step])
            for i in range(19):
                target[i, x - back, to : to + wide, :] = post[i]
            own = jnp.logical_and(x >= COL0, x < COL0 + LX)
            for k in range(6):
                sums[k] += jnp.where(own, stress[k], 0.0)
            return carry

        lax.fori_loop(COL0 + step - STEPS, COL0 + LX + STEPS - step, layer, 0)
    save = pltpu.make_async_copy(two, state, sem)
    save.start()
    last = [total[k] + sums[k, 4:12, :] for k in range(6)]
    for x in range(LX):
        f = arrive(two, x + STATE_COL0, STATE_ROW0, LY)
        lab, force = around(aux, x + COL0, ROW0, LY)
        _, stress = collide(f, lab, force, PHASES[3])
        last = [last[k] + stress[k] for k in range(6)]
    stacked = jnp.concatenate(last, axis=0)
    r = lax.broadcasted_iota(jnp.int32, (16, 48), 0)
    c = lax.broadcasted_iota(jnp.int32, (16, 48), 1)
    chosen = jnp.logical_and((r & 7) == (c >> 3), (r >> 3) == ((c & 7) >> 2))
    left = jnp.where(chosen, 1.0, 0.0)
    halves = jnp.dot(left, stacked, precision=HIGHEST, preferred_element_type=jnp.float32)
    z = lax.broadcasted_iota(jnp.int32, (NZ, NZ), 0)
    lane = lax.broadcasted_iota(jnp.int32, (NZ, NZ), 1)
    mean = 1.0 / (STEPS * 64)
    slow = jnp.zeros((8, NZ), jnp.float32)
    for half in range(2):
        table = jnp.where(lane == (z >> 2) + half * SZ, mean, 0.0)
        slow = slow + jnp.dot(
            halves[half * 8 : half * 8 + 8],
            table,
            precision=HIGHEST,
            preferred_element_type=jnp.float32,
        )
    for d in range(spread.shape[0]):
        spread[d] = slow
    save.wait()


def momentum_kernel(state, aux, out, work):
    wide = 16

    def layer(x, carry):
        f = arrive(state, x, STATE_ROW0 - 4, wide)
        lab, force = around(aux, x + (COL0 - STATE_COL0), ROW0 - 4, wide)
        post, _ = collide(f, lab, force, PHASES[3])
        for i in range(1, 19):
            work[i, x, STATE_ROW0 - 4 : STATE_ROW0 - 4 + wide, :] = post[i]
        return carry

    lax.fori_loop(STATE_COL0 - 1, STATE_COL0 + LX + 1, layer, 0)
    for x in range(LX):
        f = arrive(work, x + STATE_COL0, STATE_ROW0, LY)
        for axis in range(3):
            total = None
            for i in range(1, 19, 2):
                c = VELOCITY[i][axis]
                if c == 0:
                    continue
                term = f[i] - f[i + 1] if c > 0 else f[i + 1] - f[i]
                total = term if total is None else total + term
            out[axis, x] = total


TILES = 3


@functools.cache
def operator_table(sx, sy):
    waves = [2.0 * math.pi * np.fft.fftfreq(n) for n in (sx, sy, SZ)]
    k = np.meshgrid(*waves, indexing="ij")
    square = k[0] ** 2 + k[1] ** 2 + k[2] ** 2
    positive = square > 0
    safe = np.where(positive, square, 1.0)
    half = SZ // 2 + 1
    modes = sy * half
    lanes = TILES * NZ
    ky = np.repeat(np.arange(sy), half)
    kz = np.tile(np.arange(half), sy)
    weight = np.where((kz == 0) | (kz == SZ // 2), 1.0, 2.0) / (sy * SZ)
    gains = np.zeros((3, 6, sx, lanes))
    twists = np.zeros((3, 8, lanes))
    imaginary = []
    for a in range(3):
        for c in range(6):
            force = [
                -1j * sum(k[b] for b in range(3) if COMPONENT[first][b] == c) + 0.0 * k[0]
                for first in range(3)
            ]
            inner = k[0] * force[0] + k[1] * force[1] + k[2] * force[2]
            gain = np.where(positive, (force[a] - k[a] * inner / safe) / (SLOW_VISCOSITY * safe), 0.0)
            flipped = gain
            for axis in range(3):
                flipped = np.roll(np.flip(flipped, axis), 1, axis)
            gain = 0.5 * (gain + np.conj(flipped))
            line = weight * np.fft.ifft(gain, axis=0)[:, :, :half].reshape(sx, modes)
            odd_x = (int(a == 0) + sum(int(d == 0) for d in PAIRS[c])) % 2
            imaginary.append(not odd_x)
            gains[a, c, :, :modes] = line.real if odd_x else line.imag
            if odd_x:
                twists[a, c, :modes] = line.imag[0]
    gains = np.concatenate([gains, gains[:, :, :GROUP]], axis=2)
    gains = gains.reshape(3, 6, sx + GROUP, TILES, NZ).transpose(0, 1, 3, 2, 4)
    twists = twists.reshape(3, 8, TILES, NZ).transpose(0, 2, 1, 3)
    y = np.repeat(np.arange(2), SZ)
    z = np.tile(np.arange(SZ), 2)
    angle = 2.0 * math.pi * (np.outer(y, ky) / sy + np.outer(z, kz) / SZ)
    forward = np.zeros((2, NZ, lanes))
    forward[0, :64, :modes] = np.cos(angle)
    forward[1, :64, :modes] = -np.sin(angle)
    forward = forward.reshape(2, NZ, TILES, NZ).transpose(0, 2, 1, 3)
    shift = 2.0 * math.pi * np.outer(2 * np.arange(sy // 2), ky) / sy
    turns = np.zeros((sy // 2, 2, lanes))
    turns[:, 0, :modes] = np.cos(shift)
    turns[:, 1, :modes] = np.sin(shift)
    turns = np.concatenate([turns.reshape(-1, NZ), np.zeros((-turns.size // NZ % 8, NZ))])
    sections = [gains.reshape(-1, NZ), twists.reshape(-1, NZ), turns, forward.reshape(-1, NZ)]
    starts = np.cumsum([0] + [len(section) for section in sections])
    table = np.concatenate(sections).astype(np.float32)
    return table, tuple(int(start) for start in starts[:4]), tuple(imaginary)


def solve_kernel(starts, imaginary, pairs, blocks, table, out, part, field):
    groups = blocks.shape[0]
    sx = groups * GROUP
    at_gain, at_twist, at_turn, at_forward = starts
    me = lax.axis_index("cy")
    mine = lax.rem(lax.axis_index(GX), GROUP)
    pair = lax.axis_index(GY)
    forward = jnp.concatenate(
        [table[at_forward + k * NZ : at_forward + (k + 1) * NZ, :] for k in range(2 * TILES)], axis=1
    )
    part[...] = jnp.dot(
        blocks[...].reshape(groups * 8, NZ),
        forward,
        precision=HIGHEST,
        preferred_element_type=jnp.float32,
    ).reshape(groups, 8, 2 * TILES * NZ)

    row = lax.broadcasted_iota(jnp.int32, (GROUP, NZ), 0)
    alternate = jnp.where(lax.rem(row + mine, 2) == 0, 1.0, -1.0)
    starts_x = [lax.rem(GROUP * (me + groups - g) + sx - mine, sx) for g in range(groups)]
    for k in range(TILES):
        re_lanes = slice(k * NZ, (k + 1) * NZ)
        im_lanes = slice((TILES + k) * NZ, (TILES + k + 1) * NZ)
        all_re = part[0, :, re_lanes]
        all_im = part[0, :, im_lanes]
        for g in range(1, groups):
            all_re = all_re + part[g, :, re_lanes]
            all_im = all_im + part[g, :, im_lanes]
        re, im = [], []
        for a in range(3):
            at = at_twist + (a * TILES + k) * 8
            wave = table[at : at + 8, :]
            re.append(-alternate * jnp.sum(wave * all_im, axis=0, keepdims=True))
            im.append(alternate * jnp.sum(wave * all_re, axis=0, keepdims=True))
        for g in range(groups):
            for c in range(6):
                hat_re = jnp.broadcast_to(part[g, c : c + 1, re_lanes], (GROUP, NZ))
                hat_im = jnp.broadcast_to(part[g, c : c + 1, im_lanes], (GROUP, NZ))
                for a in range(3):
                    at = at_gain + ((a * 6 + c) * TILES + k) * (sx + GROUP)
                    gain = table[pl.ds(at + starts_x[g], GROUP), :]
                    if imaginary[a * 6 + c]:
                        re[a] = re[a] - gain * hat_im
                        im[a] = im[a] + gain * hat_re
                    else:
                        re[a] = re[a] + gain * hat_re
                        im[a] = im[a] + gain * hat_im
        for j in range(pairs):
            d = lax.rem(pairs + j - pair, pairs)
            cosine = table[pl.ds(at_turn + k + d * (2 * TILES), 1), :]
            sine = table[pl.ds(at_turn + TILES + k + d * (2 * TILES), 1), :]
            for a in range(3):
                at = (a * pairs + j) * GROUP
                field[at : at + GROUP, re_lanes] = re[a] * cosine - im[a] * sine
                field[at : at + GROUP, im_lanes] = re[a] * sine + im[a] * cosine
    result = lax.dot_general(
        field[...],
        forward,
        (((1,), (1,)), ((), ())),
        precision=HIGHEST,
        preferred_element_type=jnp.float32,
    )
    for j in range(pairs):
        first, second, third = [
            result[(a * pairs + j) * GROUP : (a * pairs + j + 1) * GROUP] for a in range(3)
        ]
        both = first + pltpu.roll(second, 64, 1)
        for r in range(GROUP):
            out[r * pairs + j, 0:1, :] = both[r : r + 1]
            out[r * pairs + j, 1:2, :] = third[r : r + 1]


def last_kernel(parts, out):
    total = jnp.sum(parts[...], axis=0)
    for a in range(3):
        row = total[a // 2 : a // 2 + 1, :]
        for y in range(2):
            lane = (a % 2) * 64 + y * SZ
            value = pltpu.roll(row, (NZ - lane) % NZ, 1) if lane else row
            out[a, 0, y : y + 1, :] = value[:, :SZ]


def call(body, outs, scratch, cost, limit=16, place=pltpu.VMEM, more=(), far=0):
    shapes = [
        pltpu.HBM(s, jnp.float32) if k < far else jax.ShapeDtypeStruct(s, jnp.float32) for k, s in enumerate(outs)
    ]

    def run(*args):
        return pl.pallas_call(
            body,
            out_shape=shapes,
            in_specs=[pl.BlockSpec(memory_space=place)] * len(args),
            out_specs=[
                pl.BlockSpec(memory_space=pltpu.HBM if k < far else pltpu.VMEM) for k in range(len(shapes))
            ],
            scratch_shapes=[pltpu.VMEM(s, jnp.float32) for s in scratch] + list(more),
            compiler_params=pltpu.CompilerParams(vmem_limit_bytes=limit << 20),
            cost_estimate=pl.CostEstimate(flops=cost, bytes_accessed=cost, transcendentals=0),
        )(*args)

    return run


def swap(far, near, axis):
    count = lax.axis_size(axis)
    near_pairs = [(i, i ^ 1) for i in range(count)]
    far_pairs = [(i, (i + 1) % count if i % 2 else (i - 1) % count) for i in range(count)]
    return lax.ppermute(far, axis, far_pairs), lax.ppermute(near, axis, near_pairs)


def local(pops, label, drive):
    nx = lax.axis_size(GX)
    ny = lax.axis_size(GY)
    groups = lax.axis_size("cy")
    cells, total, far, near = call(
        first_kernel,
        [(CHANNELS, LX, LY, NZ), (6, LY, NZ), (Y_ROWS, NZ), (Y_ROWS, NZ)],
        [(2, Y_ROWS, NZ), pops.shape],
        2_000_000,
        place=pltpu.HBM,
        more=[
            pltpu.VMEM(label.shape, jnp.int32),
            pltpu.VMEM(drive.shape, jnp.float32),
            pltpu.SemaphoreType.DMA((3,)),
        ],
    )(*[pltpu.with_memory_space_constraint(value, pltpu.HBM) for value in (pops, label, drive)])
    y_far, y_near = swap(far, near, GY)
    far, near = call(
        second_kernel,
        [(X_ROWS, NZ), (X_ROWS, NZ)],
        [(2, Y_ROWS, NZ), (2, X_ROWS, NZ)],
        2_000_000,
    )(cells, y_far, y_near)
    x_far, x_near = swap(far, near, GX)
    state, aux, spread = call(
        third_kernel,
        [(19, STATE_COLS, STATE_ROWS, NZ), (4, WORK_COLS, WORK_ROWS, NZ), (groups, 8, NZ)],
        [
            (2, Y_ROWS, NZ),
            (2, X_ROWS, NZ),
            (19, WORK_COLS, WORK_ROWS, NZ),
            (19, WORK_COLS, WORK_ROWS, NZ),
            (6, 16, NZ),
            (19, STATE_COLS, STATE_ROWS, NZ),
        ],
        20_000_000,
        more=[pltpu.SemaphoreType.DMA(())],
        far=1,
    )(cells, total, y_far, y_near, x_far, x_near)
    blocks = lax.all_to_all(spread, "cy", 0, 0, tiled=False)
    (momentum,) = call(
        momentum_kernel,
        [(3, LX, LY, NZ)],
        [(19, STATE_COLS, STATE_ROWS, NZ)],
        10_000_000,
    )(state, aux)
    blocks, momentum = lax.optimization_barrier((blocks, momentum))
    table, starts, imaginary = operator_table(nx, 2 * ny)
    (parts,) = call(
        functools.partial(solve_kernel, starts, imaginary, ny),
        [(GROUP * ny, 2, NZ)],
        [(groups, 8, 2 * TILES * NZ), (3 * ny * GROUP, 2 * TILES * NZ)],
        10_000_000,
    )(blocks, table)
    parts = lax.all_to_all(parts, ("zl", "core", "zh", "cx"), 0, 0, tiled=False)
    (running,) = call(last_kernel, [(3, 1, 2, SZ)], [], 100_000)(parts)
    return momentum, running


def solution(mesh):
    nx, ny = mesh.devices.shape
    devices = mesh.devices.reshape(nx // GROUP, 4, 2, 2, ny // 2)
    mesh = jax.sharding.Mesh(devices, GX + GY)
    in_specs = (P(None, GX, GY, None), P(GX, GY, None), P(None, GX, GY, None))
    out_specs = (P(None, GX, GY, None), P(None, GX, GY, None))
    return jax.shard_map(local, mesh=mesh, in_specs=in_specs, out_specs=out_specs, check_vma=False)
```

```python
import functools
import math

import jax
import jax.numpy as jnp
import numpy as np
from jax import lax
from jax.experimental import pallas as pl
from jax.experimental.pallas import tpu as pltpu
from jax.sharding import PartitionSpec as P

NZ = 128
STEPS = 4
SZ = 32
LX = 4
LY = 8
VELOCITY = [
    [0, 0, 0],
    [1, 0, 0],
    [-1, 0, 0],
    [0, 1, 0],
    [0, -1, 0],
    [0, 0, 1],
    [0, 0, -1],
    [1, 1, 0],
    [-1, -1, 0],
    [1, -1, 0],
    [-1, 1, 0],
    [1, 0, 1],
    [-1, 0, -1],
    [1, 0, -1],
    [-1, 0, 1],
    [0, 1, 1],
    [0, -1, -1],
    [0, 1, -1],
    [0, -1, 1],
]
OPPOSITE = [0, 2, 1, 4, 3, 6, 5, 8, 7, 10, 9, 12, 11, 14, 13, 16, 15, 18, 17]
WEIGHTS = [1.0 / 3.0] + [1.0 / 18.0] * 6 + [1.0 / 36.0] * 12
PAIRS = [(0, 0), (1, 1), (2, 2), (0, 1), (0, 2), (1, 2)]
COMPONENT = [[0, 3, 4], [3, 1, 5], [4, 5, 2]]
SLOW_VISCOSITY = 0.0004
PHASES = [math.cos(2.0 * math.pi * (step + 0.5) / STEPS) for step in range(STEPS)]

CHANNELS = 23
CX = [v[0] for v in VELOCITY] + [0] * 4
CY = [v[1] for v in VELOCITY] + [0] * 4
HIGHEST = lax.Precision.HIGHEST
GX = ("cy", "zl", "core")
GY = ("zh", "cx")
GROUP = 8


REACH = STEPS - 2


def pack_y(sign):
    out, at = [], 0
    for x in range(LX):
        for ch in range(CHANNELS):
            n = REACH + sign * CY[ch]
            out.append((ch, x, LY - n if sign > 0 else 0, n, at))
            at += n
    return out, -(-at // 8) * 8


def pack_x(sign):
    out, at = [], 0
    for ch in range(CHANNELS):
        n = REACH + sign * CX[ch]
        for x in range(LX - n, LX) if sign > 0 else range(n):
            out.append((ch, x, REACH + CY[ch], REACH - CY[ch], at))
            at += 2 * REACH + LY
    return out, -(-at // 8) * 8


SPAN = 2 * REACH + LY
Y_UP, Y_ROWS = pack_y(1)
Y_DOWN, _ = pack_y(-1)
X_RIGHT, X_ROWS = pack_x(1)
X_LEFT, _ = pack_x(-1)
Y_UP_AT = {(ch, x): (n, at) for ch, x, _, n, at in Y_UP}
Y_DOWN_AT = {(ch, x): (n, at) for ch, x, _, n, at in Y_DOWN}
X_RIGHT_AT = {(ch, x): at for ch, x, _, _, at in X_RIGHT}
X_LEFT_AT = {(ch, x): at for ch, x, _, _, at in X_LEFT}
UP = [i for i in range(19) if CY[i] == 1]
DOWN = [i for i in range(19) if CY[i] == -1]
RIGHT = [i for i in range(19) if CX[i] == 1]
LEFT = [i for i in range(19) if CX[i] == -1]
EDGE_Y_ROWS = 24
EDGE_X_ROWS = 40


def collide(f, label, drive, phase):
    rho = f[0]
    for i in range(1, 19):
        rho = rho + f[i]
    j = []
    for axis in range(3):
        total = None
        for i in range(1, 19, 2):
            c = VELOCITY[i][axis]
            if c == 0:
                continue
            term = f[i] - f[i + 1] if c > 0 else f[i + 1] - f[i]
            total = term if total is None else total + term
        j.append(total)
    second = label == 1.0
    solid = label == 2.0
    omega = jnp.where(second, 1.1, 1.6)
    keep = 1.0 - omega
    strength = jnp.where(second, 0.6 * phase, phase)
    inverse = 1.0 / rho
    mix = [omega * j[axis] + strength * drive[axis] for axis in range(3)]
    base = omega * (rho - 1.5 * (j[0] * j[0] + j[1] * j[1] + j[2] * j[2]) * inverse)
    curve = 4.5 * omega * inverse

    def along(vector, c):
        total = None
        for axis in range(3):
            if c[axis] == 0:
                continue
            if total is None:
                total = vector[axis] if c[axis] > 0 else -vector[axis]
            else:
                total = total + vector[axis] if c[axis] > 0 else total - vector[axis]
        return total

    post = [None] * 19
    post[0] = jnp.where(solid, f[0], keep * f[0] + WEIGHTS[0] * base)
    for i in range(1, 19, 2):
        w = WEIGHTS[i]
        cj = along(j, VELOCITY[i])
        even = w * (base + curve * (cj * cj))
        odd = (3.0 * w) * along(mix, VELOCITY[i])
        post[i] = jnp.where(solid, f[i + 1], keep * f[i] + (even + odd))
        post[i + 1] = jnp.where(solid, f[i], keep * f[i + 1] + (even - odd))
    fluid = jnp.where(solid, 0.0, inverse)
    stress = [j[a] * j[b] * fluid for a, b in PAIRS]
    return post, stress


def first_kernel(pops_in, label_in, drive_in, cells, total, far, near, box, pops, label, drive, sems):
    copies = [
        pltpu.make_async_copy(source, target, sems.at[k])
        for k, (source, target) in enumerate(((pops_in, pops), (label_in, label), (drive_in, drive)))
    ]
    for copy in copies:
        copy.start()
    for copy in copies:
        copy.wait()
    up = lax.rem(lax.axis_index(GY), 2)
    down = 1 - up
    sums = [jnp.zeros((LY, NZ), jnp.float32)] * 6
    for x in range(LX):
        f = [pops[i, x] for i in range(19)]
        lab = label[x].astype(jnp.float32)
        force = [drive[axis, x] for axis in range(3)]
        post, stress = collide(f, lab, force, PHASES[0])
        for i in range(19):
            cells[i, x] = post[i]
        cells[19, x] = lab
        for axis in range(3):
            cells[20 + axis, x] = force[axis]
        sums = [sums[k] + stress[k] for k in range(6)]
    for k in range(6):
        total[k] = sums[k]
    for ch, x, row, n, at in Y_UP:
        box[up, at : at + n, :] = cells[ch, x, row : row + n, :]
    for ch, x, row, n, at in Y_DOWN:
        box[down, at : at + n, :] = cells[ch, x, row : row + n, :]
    near[...] = box[0]
    far[...] = box[1]


def second_kernel(cells, got_far, got_near, far, near, rows, box):
    odd_y = lax.rem(lax.axis_index(GY), 2)
    low_slot, high_slot = 1 - odd_y, odd_y
    right = lax.rem(lax.axis_index(GX), 2)
    rows[0] = got_near[...]
    rows[1] = got_far[...]
    for slot, entries in ((right, X_RIGHT), (1 - right, X_LEFT)):
        for ch, x, low, high, at in entries:
            n, source = Y_UP_AT[ch, x]
            box[slot, at : at + n, :] = rows[low_slot, source : source + n, :]
            box[slot, at + low : at + low + LY, :] = cells[ch, x]
            n, source = Y_DOWN_AT[ch, x]
            box[slot, at + low + LY : at + low + LY + n, :] = rows[high_slot, source : source + n, :]
    near[...] = box[0]
    far[...] = box[1]


PACK = 16
ROW0 = 8
WORK_ROWS = 24


def own_kernel(cells, got_far, got_near, packs, rows):
    odd_y = lax.rem(lax.axis_index(GY), 2)
    rows[0] = got_near[...]
    rows[1] = got_far[...]
    for ch in range(CHANNELS):
        for x in range(LX):
            low, source = Y_UP_AT[ch, x]
            packs[ch, x, 0:low, :] = rows[1 - odd_y, source : source + low, :]
            packs[ch, x, low : low + LY, :] = cells[ch, x]
            high, source = Y_DOWN_AT[ch, x]
            packs[ch, x, low + LY : low + LY + high, :] = rows[odd_y, source : source + high, :]


def spin(value, i):
    cz = VELOCITY[i][2]
    return pltpu.roll(value, cz % NZ, 1) if cz else value


def arrive(source, x, row, n):
    return [
        spin(source[i, x - CX[i], row - CY[i] : row - CY[i] + n, :], i) for i in range(19)
    ]


def third_kernel(
    cells, total, packs, x_far, x_near, post3, spread, edge_far, edge_near, cols, one, two, sums, box
):
    odd_y = lax.rem(lax.axis_index(GY), 2)
    odd_x = lax.rem(lax.axis_index(GX), 2)
    left_slot, right_slot = 1 - odd_x, odd_x
    cols[0] = x_near[...]
    cols[1] = x_far[...]

    def packed(ch, x):
        if x < 0:
            at = X_RIGHT_AT[ch, x + LX]
            return cols[left_slot, at : at + SPAN, :]
        if x >= LX:
            at = X_LEFT_AT[ch, x - LX]
            return cols[right_slot, at : at + SPAN, :]
        return packs[ch, x, 0:SPAN, :]

    def add(first, second):
        return second if first is None else [a + b for a, b in zip(first, second)]

    low = ROW0 - REACH
    kept = None
    for x in range(-REACH, LX + REACH):
        f = [spin(packed(i, x - CX[i]), i) for i in range(19)]
        post, stress = collide(f, packed(19, x), [packed(20 + axis, x) for axis in range(3)], PHASES[1])
        for i in range(19):
            one[i, x + REACH, low : low + SPAN, :] = post[i]
        if 0 <= x < LX:
            kept = add(kept, stress)
    for k in range(6):
        sums[k, 0:SPAN, :] = kept[k]
    low, n = ROW0 - 1, LY + 2
    kept = None
    for x in range(-1, LX + 1):
        f = arrive(one, x + REACH, low, n)
        lab, *force = [packed(ch, x)[REACH - 1 : REACH - 1 + n] for ch in range(19, CHANNELS)]
        post, stress = collide(f, lab, force, PHASES[2])
        for i in range(19):
            two[i, x + 1, low : low + n, :] = post[i]
        if 0 <= x < LX:
            kept = add(kept, stress)
    for k in range(6):
        sums[6 + k, 0:n, :] = kept[k]
    last = [
        total[k] + sums[k, REACH : REACH + LY, :] + sums[6 + k, 1 : 1 + LY, :] for k in range(6)
    ]
    for x in range(LX):
        f = arrive(two, x + 1, ROW0, LY)
        post, stress = collide(f, cells[19, x], [cells[20 + axis, x] for axis in range(3)], PHASES[3])
        for i in range(19):
            post3[i, x] = post[i]
        last = add(last, stress)
    stacked = jnp.concatenate(last, axis=0)
    r = lax.broadcasted_iota(jnp.int32, (16, 48), 0)
    c = lax.broadcasted_iota(jnp.int32, (16, 48), 1)
    chosen = jnp.logical_and((r & 7) == (c >> 3), (r >> 3) == ((c & 7) >> 2))
    left = jnp.where(chosen, 1.0, 0.0)
    halves = jnp.dot(left, stacked, precision=HIGHEST, preferred_element_type=jnp.float32)
    z = lax.broadcasted_iota(jnp.int32, (NZ, NZ), 0)
    lane = lax.broadcasted_iota(jnp.int32, (NZ, NZ), 1)
    mean = 1.0 / (STEPS * 64)
    slow = jnp.zeros((8, NZ), jnp.float32)
    for half in range(2):
        table = jnp.where(lane == (z >> 2) + half * SZ, mean, 0.0)
        slow = slow + jnp.dot(
            halves[half * 8 : half * 8 + 8],
            table,
            precision=HIGHEST,
            preferred_element_type=jnp.float32,
        )
    for d in range(spread.shape[0]):
        spread[d] = slow
    for slot, comps, row in ((odd_y, UP, LY - 1), (1 - odd_y, DOWN, 0)):
        for k, i in enumerate(comps):
            for x in range(LX):
                at = k * LX + x
                box[slot, at : at + 1, :] = post3[i, x, row : row + 1, :]
    edge_near[...] = box[0]
    edge_far[...] = box[1]


def edge_kernel(post3, y_far, y_near, far, near, rows, box):
    odd_y = lax.rem(lax.axis_index(GY), 2)
    low_slot, high_slot = 1 - odd_y, odd_y
    right = lax.rem(lax.axis_index(GX), 2)
    rows[0] = y_near[...]
    rows[1] = y_far[...]
    for slot, comps, x in ((right, RIGHT, LX - 1), (1 - right, LEFT, 0)):
        for k, i in enumerate(comps):
            at = k * LY
            if CY[i] == 0:
                box[slot, at : at + LY, :] = post3[i, x]
            elif CY[i] == 1:
                source = UP.index(i) * LX + x
                box[slot, at : at + 1, :] = rows[low_slot, source : source + 1, :]
                box[slot, at + 1 : at + LY, :] = post3[i, x, 0 : LY - 1, :]
            else:
                source = DOWN.index(i) * LX + x
                box[slot, at : at + LY - 1, :] = post3[i, x, 1:LY, :]
                box[slot, at + LY - 1 : at + LY, :] = rows[high_slot, source : source + 1, :]
    near[...] = box[0]
    far[...] = box[1]


def momentum_kernel(post3, y_far, y_near, x_far, x_near, out, rows, cols, work):
    odd_y = lax.rem(lax.axis_index(GY), 2)
    odd_x = lax.rem(lax.axis_index(GX), 2)
    rows[0] = y_near[...]
    rows[1] = y_far[...]
    cols[0] = x_near[...]
    cols[1] = x_far[...]
    for i in range(1, 19):
        for x in range(LX):
            work[i, x + 1, ROW0 : ROW0 + LY, :] = post3[i, x]
    for k, i in enumerate(UP):
        for x in range(LX):
            at = k * LX + x
            work[i, x + 1, ROW0 - 1 : ROW0, :] = rows[1 - odd_y, at : at + 1, :]
    for k, i in enumerate(DOWN):
        for x in range(LX):
            at = k * LX + x
            work[i, x + 1, ROW0 + LY : ROW0 + LY + 1, :] = rows[odd_y, at : at + 1, :]
    for k, i in enumerate(RIGHT):
        work[i, 0, ROW0 - CY[i] : ROW0 - CY[i] + LY, :] = cols[1 - odd_x, k * LY : k * LY + LY, :]
    for k, i in enumerate(LEFT):
        work[i, LX + 1, ROW0 - CY[i] : ROW0 - CY[i] + LY, :] = cols[odd_x, k * LY : k * LY + LY, :]
    for x in range(LX):
        f = [None] + [
            spin(work[i, x + 1 - CX[i], ROW0 - CY[i] : ROW0 - CY[i] + LY, :], i) for i in range(1, 19)
        ]
        for axis in range(3):
            total = None
            for i in range(1, 19, 2):
                c = VELOCITY[i][axis]
                if c == 0:
                    continue
                term = f[i] - f[i + 1] if c > 0 else f[i + 1] - f[i]
                total = term if total is None else total + term
            out[axis, x] = total


TILES = 3


@functools.cache
def operator_table(sx, sy):
    waves = [2.0 * math.pi * np.fft.fftfreq(n) for n in (sx, sy, SZ)]
    k = np.meshgrid(*waves, indexing="ij")
    square = k[0] ** 2 + k[1] ** 2 + k[2] ** 2
    positive = square > 0
    safe = np.where(positive, square, 1.0)
    half = SZ // 2 + 1
    modes = sy * half
    lanes = TILES * NZ
    ky = np.repeat(np.arange(sy), half)
    kz = np.tile(np.arange(half), sy)
    weight = np.where((kz == 0) | (kz == SZ // 2), 1.0, 2.0) / (sy * SZ)
    gains = np.zeros((3, 6, sx, lanes))
    twists = np.zeros((3, 8, lanes))
    imaginary = []
    for a in range(3):
        for c in range(6):
            force = [
                -1j * sum(k[b] for b in range(3) if COMPONENT[first][b] == c) + 0.0 * k[0]
                for first in range(3)
            ]
            inner = k[0] * force[0] + k[1] * force[1] + k[2] * force[2]
            gain = np.where(positive, (force[a] - k[a] * inner / safe) / (SLOW_VISCOSITY * safe), 0.0)
            flipped = gain
            for axis in range(3):
                flipped = np.roll(np.flip(flipped, axis), 1, axis)
            gain = 0.5 * (gain + np.conj(flipped))
            line = weight * np.fft.ifft(gain, axis=0)[:, :, :half].reshape(sx, modes)
            odd_x = (int(a == 0) + sum(int(d == 0) for d in PAIRS[c])) % 2
            imaginary.append(not odd_x)
            gains[a, c, :, :modes] = line.real if odd_x else line.imag
            if odd_x:
                twists[a, c, :modes] = line.imag[0]
    gains = np.concatenate([gains, gains[:, :, :GROUP]], axis=2)
    gains = gains.reshape(3, 6, sx + GROUP, TILES, NZ).transpose(0, 1, 3, 2, 4)
    twists = twists.reshape(3, 8, TILES, NZ).transpose(0, 2, 1, 3)
    y = np.repeat(np.arange(2), SZ)
    z = np.tile(np.arange(SZ), 2)
    angle = 2.0 * math.pi * (np.outer(y, ky) / sy + np.outer(z, kz) / SZ)
    forward = np.zeros((2, NZ, lanes))
    forward[0, :64, :modes] = np.cos(angle)
    forward[1, :64, :modes] = -np.sin(angle)
    forward = forward.reshape(2, NZ, TILES, NZ).transpose(0, 2, 1, 3)
    shift = 2.0 * math.pi * np.outer(2 * np.arange(sy // 2), ky) / sy
    turns = np.zeros((sy // 2, 2, lanes))
    turns[:, 0, :modes] = np.cos(shift)
    turns[:, 1, :modes] = np.sin(shift)
    turns = np.concatenate([turns.reshape(-1, NZ), np.zeros((-turns.size // NZ % 8, NZ))])
    sections = [gains.reshape(-1, NZ), twists.reshape(-1, NZ), turns, forward.reshape(-1, NZ)]
    starts = np.cumsum([0] + [len(section) for section in sections])
    table = np.concatenate(sections).astype(np.float32)
    return table, tuple(int(start) for start in starts[:4]), tuple(imaginary)


def solve_kernel(starts, imaginary, pairs, blocks, table, out, part, field):
    groups = blocks.shape[0]
    sx = groups * GROUP
    at_gain, at_twist, at_turn, at_forward = starts
    me = lax.axis_index("cy")
    mine = lax.rem(lax.axis_index(GX), GROUP)
    pair = lax.axis_index(GY)
    forward = jnp.concatenate(
        [table[at_forward + k * NZ : at_forward + (k + 1) * NZ, :] for k in range(2 * TILES)], axis=1
    )
    part[...] = jnp.dot(
        blocks[...].reshape(groups * 8, NZ),
        forward,
        precision=HIGHEST,
        preferred_element_type=jnp.float32,
    ).reshape(groups, 8, 2 * TILES * NZ)

    row = lax.broadcasted_iota(jnp.int32, (GROUP, NZ), 0)
    alternate = jnp.where(lax.rem(row + mine, 2) == 0, 1.0, -1.0)
    starts_x = [lax.rem(GROUP * (me + groups - g) + sx - mine, sx) for g in range(groups)]
    for k in range(TILES):
        re_lanes = slice(k * NZ, (k + 1) * NZ)
        im_lanes = slice((TILES + k) * NZ, (TILES + k + 1) * NZ)
        all_re = part[0, :, re_lanes]
        all_im = part[0, :, im_lanes]
        for g in range(1, groups):
            all_re = all_re + part[g, :, re_lanes]
            all_im = all_im + part[g, :, im_lanes]
        re, im = [], []
        for a in range(3):
            at = at_twist + (a * TILES + k) * 8
            wave = table[at : at + 8, :]
            re.append(-alternate * jnp.sum(wave * all_im, axis=0, keepdims=True))
            im.append(alternate * jnp.sum(wave * all_re, axis=0, keepdims=True))
        for g in range(groups):
            for c in range(6):
                hat_re = jnp.broadcast_to(part[g, c : c + 1, re_lanes], (GROUP, NZ))
                hat_im = jnp.broadcast_to(part[g, c : c + 1, im_lanes], (GROUP, NZ))
                for a in range(3):
                    at = at_gain + ((a * 6 + c) * TILES + k) * (sx + GROUP)
                    gain = table[pl.ds(at + starts_x[g], GROUP), :]
                    if imaginary[a * 6 + c]:
                        re[a] = re[a] - gain * hat_im
                        im[a] = im[a] + gain * hat_re
                    else:
                        re[a] = re[a] + gain * hat_re
                        im[a] = im[a] + gain * hat_im
        for j in range(pairs):
            d = lax.rem(pairs + j - pair, pairs)
            cosine = table[pl.ds(at_turn + k + d * (2 * TILES), 1), :]
            sine = table[pl.ds(at_turn + TILES + k + d * (2 * TILES), 1), :]
            for a in range(3):
                at = (a * pairs + j) * GROUP
                field[at : at + GROUP, re_lanes] = re[a] * cosine - im[a] * sine
                field[at : at + GROUP, im_lanes] = re[a] * sine + im[a] * cosine
    result = lax.dot_general(
        field[...],
        forward,
        (((1,), (1,)), ((), ())),
        precision=HIGHEST,
        preferred_element_type=jnp.float32,
    )
    for j in range(pairs):
        first, second, third = [
            result[(a * pairs + j) * GROUP : (a * pairs + j + 1) * GROUP] for a in range(3)
        ]
        both = first + pltpu.roll(second, 64, 1)
        for r in range(GROUP):
            out[r * pairs + j, 0:1, :] = both[r : r + 1]
            out[r * pairs + j, 1:2, :] = third[r : r + 1]


def last_kernel(parts, out):
    total = jnp.sum(parts[...], axis=0)
    for a in range(3):
        row = total[a // 2 : a // 2 + 1, :]
        for y in range(2):
            lane = (a % 2) * 64 + y * SZ
            value = pltpu.roll(row, (NZ - lane) % NZ, 1) if lane else row
            out[a, 0, y : y + 1, :] = value[:, :SZ]


def call(body, outs, scratch, cost, limit=16, place=pltpu.VMEM, more=()):
    shapes = [jax.ShapeDtypeStruct(s, jnp.float32) for s in outs]
    spec = pl.BlockSpec(memory_space=pltpu.VMEM)

    def run(*args):
        return pl.pallas_call(
            body,
            out_shape=shapes,
            in_specs=[pl.BlockSpec(memory_space=place)] * len(args),
            out_specs=[spec] * len(shapes),
            scratch_shapes=[pltpu.VMEM(s, jnp.float32) for s in scratch] + list(more),
            compiler_params=pltpu.CompilerParams(vmem_limit_bytes=limit << 20),
            cost_estimate=pl.CostEstimate(flops=cost, bytes_accessed=cost, transcendentals=0),
        )(*args)

    return run


def swap(far, near, axis):
    count = lax.axis_size(axis)
    near_pairs = [(i, i ^ 1) for i in range(count)]
    far_pairs = [(i, (i + 1) % count if i % 2 else (i - 1) % count) for i in range(count)]
    return lax.ppermute(far, axis, far_pairs), lax.ppermute(near, axis, near_pairs)


def local(pops, label, drive):
    nx = lax.axis_size(GX)
    ny = lax.axis_size(GY)
    groups = lax.axis_size("cy")
    cells, total, far, near = call(
        first_kernel,
        [(CHANNELS, LX, LY, NZ), (6, LY, NZ), (Y_ROWS, NZ), (Y_ROWS, NZ)],
        [(2, Y_ROWS, NZ), pops.shape],
        2_000_000,
        place=pltpu.HBM,
        more=[
            pltpu.VMEM(label.shape, jnp.int32),
            pltpu.VMEM(drive.shape, jnp.float32),
            pltpu.SemaphoreType.DMA((3,)),
        ],
    )(*[pltpu.with_memory_space_constraint(value, pltpu.HBM) for value in (pops, label, drive)])
    y_far, y_near = swap(far, near, GY)
    far, near = call(
        second_kernel,
        [(X_ROWS, NZ), (X_ROWS, NZ)],
        [(2, Y_ROWS, NZ), (2, X_ROWS, NZ)],
        2_000_000,
    )(cells, y_far, y_near)
    x_far, x_near = swap(far, near, GX)
    (packs,) = call(
        own_kernel, [(CHANNELS, LX, PACK, NZ)], [(2, Y_ROWS, NZ)], 2_000_000
    )(cells, y_far, y_near)
    post3, spread, far, near = call(
        third_kernel,
        [(19, LX, LY, NZ), (groups, 8, NZ), (EDGE_Y_ROWS, NZ), (EDGE_Y_ROWS, NZ)],
        [
            (2, X_ROWS, NZ),
            (19, LX + 2 * REACH, WORK_ROWS, NZ),
            (19, LX + 2, WORK_ROWS, NZ),
            (12, 16, NZ),
            (2, EDGE_Y_ROWS, NZ),
        ],
        20_000_000,
    )(cells, total, packs, x_far, x_near)
    blocks = lax.all_to_all(spread, "cy", 0, 0, tiled=False)
    ey_far, ey_near = swap(far, near, GY)
    blocks, ey_far, ey_near = lax.optimization_barrier((blocks, ey_far, ey_near))
    table, starts, imaginary = operator_table(nx, 2 * ny)
    (parts,) = call(
        functools.partial(solve_kernel, starts, imaginary, ny),
        [(GROUP * ny, 2, NZ)],
        [(groups, 8, 2 * TILES * NZ), (3 * ny * GROUP, 2 * TILES * NZ)],
        10_000_000,
    )(blocks, table)
    parts = lax.all_to_all(parts, ("zl", "core", "zh", "cx"), 0, 0, tiled=False)
    far, near = call(
        edge_kernel,
        [(EDGE_X_ROWS, NZ), (EDGE_X_ROWS, NZ)],
        [(2, EDGE_Y_ROWS, NZ), (2, EDGE_X_ROWS, NZ)],
        200_000,
    )(post3, ey_far, ey_near)
    ex_far, ex_near = swap(far, near, GX)
    (momentum,) = call(
        momentum_kernel,
        [(3, LX, LY, NZ)],
        [(2, EDGE_Y_ROWS, NZ), (2, EDGE_X_ROWS, NZ), (19, LX + 2, WORK_ROWS, NZ)],
        1_000_000,
    )(post3, ey_far, ey_near, ex_far, ex_near)
    (running,) = call(last_kernel, [(3, 1, 2, SZ)], [], 100_000)(parts)
    return momentum, running


def solution(mesh):
    nx, ny = mesh.devices.shape
    devices = mesh.devices.reshape(nx // GROUP, 4, 2, 2, ny // 2)
    mesh = jax.sharding.Mesh(devices, GX + GY)
    in_specs = (P(None, GX, GY, None), P(GX, GY, None), P(None, GX, GY, None))
    out_specs = (P(None, GX, GY, None), P(None, GX, GY, None))
    return jax.shard_map(local, mesh=mesh, in_specs=in_specs, out_specs=out_specs, check_vma=False)
```

```python
import functools
import math

import jax
import jax.numpy as jnp
import numpy as np
from jax import lax
from jax.experimental import pallas as pl
from jax.experimental.pallas import tpu as pltpu
from jax.sharding import PartitionSpec as P

NZ = 128
STEPS = 4
SZ = 32
LX = 4
LY = 8
VELOCITY = [
    [0, 0, 0],
    [1, 0, 0],
    [-1, 0, 0],
    [0, 1, 0],
    [0, -1, 0],
    [0, 0, 1],
    [0, 0, -1],
    [1, 1, 0],
    [-1, -1, 0],
    [1, -1, 0],
    [-1, 1, 0],
    [1, 0, 1],
    [-1, 0, -1],
    [1, 0, -1],
    [-1, 0, 1],
    [0, 1, 1],
    [0, -1, -1],
    [0, 1, -1],
    [0, -1, 1],
]
OPPOSITE = [0, 2, 1, 4, 3, 6, 5, 8, 7, 10, 9, 12, 11, 14, 13, 16, 15, 18, 17]
WEIGHTS = [1.0 / 3.0] + [1.0 / 18.0] * 6 + [1.0 / 36.0] * 12
PAIRS = [(0, 0), (1, 1), (2, 2), (0, 1), (0, 2), (1, 2)]
COMPONENT = [[0, 3, 4], [3, 1, 5], [4, 5, 2]]
SLOW_VISCOSITY = 0.0004
PHASES = [math.cos(2.0 * math.pi * (step + 0.5) / STEPS) for step in range(STEPS)]

CHANNELS = 23
CX = [v[0] for v in VELOCITY] + [0] * 4
CY = [v[1] for v in VELOCITY] + [0] * 4
HIGHEST = lax.Precision.HIGHEST
GX = ("cy", "zl", "core")
GY = ("zh", "cx")
GROUP = 8


REACH = STEPS - 1


def pack_y(sign):
    out, at = [], 0
    for x in range(LX):
        for ch in range(CHANNELS):
            n = REACH + sign * CY[ch]
            out.append((ch, x, LY - n if sign > 0 else 0, n, at))
            at += n
    return out, -(-at // 8) * 8


def pack_x(sign):
    out, at = [], 0
    for ch in range(CHANNELS):
        n = REACH + sign * CX[ch]
        for x in range(LX - n, LX) if sign > 0 else range(n):
            out.append((ch, x, REACH + CY[ch], REACH - CY[ch], at))
            at += 2 * REACH + LY
    return out, -(-at // 8) * 8


SPAN = 2 * REACH + LY
Y_UP, Y_ROWS = pack_y(1)
Y_DOWN, _ = pack_y(-1)
X_RIGHT, X_ROWS = pack_x(1)
X_LEFT, _ = pack_x(-1)
Y_UP_AT = {(ch, x): (n, at) for ch, x, _, n, at in Y_UP}
Y_DOWN_AT = {(ch, x): (n, at) for ch, x, _, n, at in Y_DOWN}
X_RIGHT_AT = {(ch, x): at for ch, x, _, _, at in X_RIGHT}
X_LEFT_AT = {(ch, x): at for ch, x, _, _, at in X_LEFT}


def collide(f, label, drive, phase):
    rho = f[0]
    for i in range(1, 19):
        rho = rho + f[i]
    j = []
    for axis in range(3):
        total = None
        for i in range(1, 19, 2):
            c = VELOCITY[i][axis]
            if c == 0:
                continue
            term = f[i] - f[i + 1] if c > 0 else f[i + 1] - f[i]
            total = term if total is None else total + term
        j.append(total)
    second = label == 1.0
    solid = label == 2.0
    omega = jnp.where(second, 1.1, 1.6)
    keep = 1.0 - omega
    strength = jnp.where(second, 0.6 * phase, phase)
    inverse = 1.0 / rho
    mix = [omega * j[axis] + strength * drive[axis] for axis in range(3)]
    base = omega * (rho - 1.5 * (j[0] * j[0] + j[1] * j[1] + j[2] * j[2]) * inverse)
    curve = 4.5 * omega * inverse

    def along(vector, c):
        total = None
        for axis in range(3):
            if c[axis] == 0:
                continue
            if total is None:
                total = vector[axis] if c[axis] > 0 else -vector[axis]
            else:
                total = total + vector[axis] if c[axis] > 0 else total - vector[axis]
        return total

    post = [None] * 19
    post[0] = jnp.where(solid, f[0], keep * f[0] + WEIGHTS[0] * base)
    for i in range(1, 19, 2):
        w = WEIGHTS[i]
        cj = along(j, VELOCITY[i])
        even = w * (base + curve * (cj * cj))
        odd = (3.0 * w) * along(mix, VELOCITY[i])
        post[i] = jnp.where(solid, f[i + 1], keep * f[i] + (even + odd))
        post[i + 1] = jnp.where(solid, f[i], keep * f[i + 1] + (even - odd))
    fluid = jnp.where(solid, 0.0, inverse)
    stress = [j[a] * j[b] * fluid for a, b in PAIRS]
    return post, stress


def first_kernel(pops_in, label_in, drive_in, cells, total, far, near, box, pops, label, drive, sems):
    copies = [
        pltpu.make_async_copy(source, target, sems.at[k])
        for k, (source, target) in enumerate(((pops_in, pops), (label_in, label), (drive_in, drive)))
    ]
    for copy in copies:
        copy.start()
    for copy in copies:
        copy.wait()
    up = lax.rem(lax.axis_index(GY), 2)
    down = 1 - up
    sums = [jnp.zeros((LY, NZ), jnp.float32)] * 6
    for x in range(LX):
        f = [pops[i, x] for i in range(19)]
        lab = label[x].astype(jnp.float32)
        force = [drive[axis, x] for axis in range(3)]
        post, stress = collide(f, lab, force, PHASES[0])
        for i in range(19):
            cells[i, x] = post[i]
        cells[19, x] = lab
        for axis in range(3):
            cells[20 + axis, x] = force[axis]
        sums = [sums[k] + stress[k] for k in range(6)]
    for k in range(6):
        total[k] = sums[k]
    for ch, x, row, n, at in Y_UP:
        box[up, at : at + n, :] = cells[ch, x, row : row + n, :]
    for ch, x, row, n, at in Y_DOWN:
        box[down, at : at + n, :] = cells[ch, x, row : row + n, :]
    near[...] = box[0]
    far[...] = box[1]


def second_kernel(cells, got_far, got_near, far, near, rows, box):
    odd_y = lax.rem(lax.axis_index(GY), 2)
    low_slot, high_slot = 1 - odd_y, odd_y
    right = lax.rem(lax.axis_index(GX), 2)
    rows[0] = got_near[...]
    rows[1] = got_far[...]
    for slot, entries in ((right, X_RIGHT), (1 - right, X_LEFT)):
        for ch, x, low, high, at in entries:
            n, source = Y_UP_AT[ch, x]
            box[slot, at : at + n, :] = rows[low_slot, source : source + n, :]
            box[slot, at + low : at + low + LY, :] = cells[ch, x]
            n, source = Y_DOWN_AT[ch, x]
            box[slot, at + low + LY : at + low + LY + n, :] = rows[high_slot, source : source + n, :]
    near[...] = box[0]
    far[...] = box[1]


PACK = 16
ROW0 = 8
WORK_ROWS = 24
STATE_ROW0 = 4
STATE_ROWS = 16


def own_kernel(cells, got_far, got_near, packs, rows):
    odd_y = lax.rem(lax.axis_index(GY), 2)
    rows[0] = got_near[...]
    rows[1] = got_far[...]
    for ch in range(CHANNELS):
        for x in range(LX):
            low, source = Y_UP_AT[ch, x]
            packs[ch, x, 0:low, :] = rows[1 - odd_y, source : source + low, :]
            packs[ch, x, low : low + LY, :] = cells[ch, x]
            high, source = Y_DOWN_AT[ch, x]
            packs[ch, x, low + LY : low + LY + high, :] = rows[odd_y, source : source + high, :]


def spin(value, i):
    cz = VELOCITY[i][2]
    return pltpu.roll(value, cz % NZ, 1) if cz else value


def arrive(source, x, row, n):
    return [
        spin(source[i, x - CX[i], row - CY[i] : row - CY[i] + n, :], i) for i in range(19)
    ]


def third_kernel(
    cells, total, packs, x_far, x_near, state, near_aux, spread, cols, one, two, sums, sem
):
    odd_x = lax.rem(lax.axis_index(GX), 2)
    left_slot, right_slot = 1 - odd_x, odd_x
    cols[0] = x_near[...]
    cols[1] = x_far[...]

    def packed(ch, x):
        if x < 0:
            at = X_RIGHT_AT[ch, x + LX]
            return cols[left_slot, at : at + SPAN, :]
        if x >= LX:
            at = X_LEFT_AT[ch, x - LX]
            return cols[right_slot, at : at + SPAN, :]
        return packs[ch, x, 0:SPAN, :]

    def add(first, second):
        return second if first is None else [a + b for a, b in zip(first, second)]

    low = ROW0 - REACH
    kept = None
    for x in range(-REACH, LX + REACH):
        f = [spin(packed(i, x - CX[i]), i) for i in range(19)]
        post, stress = collide(f, packed(19, x), [packed(20 + axis, x) for axis in range(3)], PHASES[1])
        for i in range(19):
            one[i, x + REACH, low : low + SPAN, :] = post[i]
        if 0 <= x < LX:
            kept = add(kept, stress)
    for k in range(6):
        sums[k, 0:SPAN, :] = kept[k]
    low, n = ROW0 - (REACH - 1), LY + 2 * (REACH - 1)
    to = STATE_ROW0 - (REACH - 1)
    kept = None
    for x in range(1 - REACH, LX + REACH - 1):
        f = arrive(one, x + REACH, low, n)
        lab, *force = [packed(ch, x)[1 : 1 + n] for ch in range(19, CHANNELS)]
        post, stress = collide(f, lab, force, PHASES[2])
        for i in range(19):
            two[i, x + REACH - 1, to : to + n, :] = post[i]
        if 0 <= x < LX:
            kept = add(kept, stress)
    save = pltpu.make_async_copy(two, state, sem)
    save.start()
    for k in range(6):
        sums[6 + k, 0:n, :] = kept[k]
    last = [
        total[k] + sums[k, REACH : REACH + LY, :] + sums[6 + k, REACH - 1 : REACH - 1 + LY, :]
        for k in range(6)
    ]
    for x in range(LX):
        f = arrive(two, x + REACH - 1, STATE_ROW0, LY)
        _, stress = collide(f, cells[19, x], [cells[20 + axis, x] for axis in range(3)], PHASES[3])
        last = add(last, stress)
    stacked = jnp.concatenate(last, axis=0)
    r = lax.broadcasted_iota(jnp.int32, (16, 48), 0)
    c = lax.broadcasted_iota(jnp.int32, (16, 48), 1)
    chosen = jnp.logical_and((r & 7) == (c >> 3), (r >> 3) == ((c & 7) >> 2))
    left = jnp.where(chosen, 1.0, 0.0)
    halves = jnp.dot(left, stacked, precision=HIGHEST, preferred_element_type=jnp.float32)
    z = lax.broadcasted_iota(jnp.int32, (NZ, NZ), 0)
    lane = lax.broadcasted_iota(jnp.int32, (NZ, NZ), 1)
    mean = 1.0 / (STEPS * 64)
    slow = jnp.zeros((8, NZ), jnp.float32)
    for half in range(2):
        table = jnp.where(lane == (z >> 2) + half * SZ, mean, 0.0)
        slow = slow + jnp.dot(
            halves[half * 8 : half * 8 + 8],
            table,
            precision=HIGHEST,
            preferred_element_type=jnp.float32,
        )
    for d in range(spread.shape[0]):
        spread[d] = slow
    for ch in range(19, CHANNELS):
        for x in range(-1, LX + 1):
            near_aux[ch - 19, x + 1, 0 : LY + 2, :] = packed(ch, x)[REACH - 1 : REACH + 1 + LY]
    save.wait()


def momentum_kernel(state, aux, out, work):
    n = LY + 2
    for x in range(-1, LX + 1):
        f = arrive(state, x + REACH - 1, STATE_ROW0 - 1, n)
        lab, *force = [aux[ch, x + 1, 0:n, :] for ch in range(4)]
        post, _ = collide(f, lab, force, PHASES[3])
        for i in range(1, 19):
            work[i, x + 1, 0:n, :] = post[i]
    for x in range(LX):
        f = [None] + [spin(work[i, x + 1 - CX[i], 1 - CY[i] : 1 - CY[i] + LY, :], i) for i in range(1, 19)]
        for axis in range(3):
            total = None
            for i in range(1, 19, 2):
                c = VELOCITY[i][axis]
                if c == 0:
                    continue
                term = f[i] - f[i + 1] if c > 0 else f[i + 1] - f[i]
                total = term if total is None else total + term
            out[axis, x] = total


TILES = 3


@functools.cache
def operator_table(sx, sy):
    waves = [2.0 * math.pi * np.fft.fftfreq(n) for n in (sx, sy, SZ)]
    k = np.meshgrid(*waves, indexing="ij")
    square = k[0] ** 2 + k[1] ** 2 + k[2] ** 2
    positive = square > 0
    safe = np.where(positive, square, 1.0)
    half = SZ // 2 + 1
    modes = sy * half
    lanes = TILES * NZ
    ky = np.repeat(np.arange(sy), half)
    kz = np.tile(np.arange(half), sy)
    weight = np.where((kz == 0) | (kz == SZ // 2), 1.0, 2.0) / (sy * SZ)
    gains = np.zeros((3, 6, sx, lanes))
    twists = np.zeros((3, 8, lanes))
    imaginary = []
    for a in range(3):
        for c in range(6):
            force = [
                -1j * sum(k[b] for b in range(3) if COMPONENT[first][b] == c) + 0.0 * k[0]
                for first in range(3)
            ]
            inner = k[0] * force[0] + k[1] * force[1] + k[2] * force[2]
            gain = np.where(positive, (force[a] - k[a] * inner / safe) / (SLOW_VISCOSITY * safe), 0.0)
            flipped = gain
            for axis in range(3):
                flipped = np.roll(np.flip(flipped, axis), 1, axis)
            gain = 0.5 * (gain + np.conj(flipped))
            line = weight * np.fft.ifft(gain, axis=0)[:, :, :half].reshape(sx, modes)
            odd_x = (int(a == 0) + sum(int(d == 0) for d in PAIRS[c])) % 2
            imaginary.append(not odd_x)
            gains[a, c, :, :modes] = line.real if odd_x else line.imag
            if odd_x:
                twists[a, c, :modes] = line.imag[0]
    gains = np.concatenate([gains, gains[:, :, :GROUP]], axis=2)
    gains = gains.reshape(3, 6, sx + GROUP, TILES, NZ).transpose(0, 1, 3, 2, 4)
    twists = twists.reshape(3, 8, TILES, NZ).transpose(0, 2, 1, 3)
    y = np.repeat(np.arange(2), SZ)
    z = np.tile(np.arange(SZ), 2)
    angle = 2.0 * math.pi * (np.outer(y, ky) / sy + np.outer(z, kz) / SZ)
    forward = np.zeros((2, NZ, lanes))
    forward[0, :64, :modes] = np.cos(angle)
    forward[1, :64, :modes] = -np.sin(angle)
    forward = forward.reshape(2, NZ, TILES, NZ).transpose(0, 2, 1, 3)
    shift = 2.0 * math.pi * np.outer(2 * np.arange(sy // 2), ky) / sy
    turns = np.zeros((sy // 2, 2, lanes))
    turns[:, 0, :modes] = np.cos(shift)
    turns[:, 1, :modes] = np.sin(shift)
    turns = np.concatenate([turns.reshape(-1, NZ), np.zeros((-turns.size // NZ % 8, NZ))])
    sections = [gains.reshape(-1, NZ), twists.reshape(-1, NZ), turns, forward.reshape(-1, NZ)]
    starts = np.cumsum([0] + [len(section) for section in sections])
    table = np.concatenate(sections).astype(np.float32)
    return table, tuple(int(start) for start in starts[:4]), tuple(imaginary)


def solve_kernel(starts, imaginary, pairs, blocks, table, out, part, field):
    groups = blocks.shape[0]
    sx = groups * GROUP
    at_gain, at_twist, at_turn, at_forward = starts
    me = lax.axis_index("cy")
    mine = lax.rem(lax.axis_index(GX), GROUP)
    pair = lax.axis_index(GY)
    forward = jnp.concatenate(
        [table[at_forward + k * NZ : at_forward + (k + 1) * NZ, :] for k in range(2 * TILES)], axis=1
    )
    part[...] = jnp.dot(
        blocks[...].reshape(groups * 8, NZ),
        forward,
        precision=HIGHEST,
        preferred_element_type=jnp.float32,
    ).reshape(groups, 8, 2 * TILES * NZ)

    row = lax.broadcasted_iota(jnp.int32, (GROUP, NZ), 0)
    alternate = jnp.where(lax.rem(row + mine, 2) == 0, 1.0, -1.0)
    starts_x = [lax.rem(GROUP * (me + groups - g) + sx - mine, sx) for g in range(groups)]
    for k in range(TILES):
        re_lanes = slice(k * NZ, (k + 1) * NZ)
        im_lanes = slice((TILES + k) * NZ, (TILES + k + 1) * NZ)
        all_re = part[0, :, re_lanes]
        all_im = part[0, :, im_lanes]
        for g in range(1, groups):
            all_re = all_re + part[g, :, re_lanes]
            all_im = all_im + part[g, :, im_lanes]
        re, im = [], []
        for a in range(3):
            at = at_twist + (a * TILES + k) * 8
            wave = table[at : at + 8, :]
            re.append(-alternate * jnp.sum(wave * all_im, axis=0, keepdims=True))
            im.append(alternate * jnp.sum(wave * all_re, axis=0, keepdims=True))
        for g in range(groups):
            for c in range(6):
                hat_re = jnp.broadcast_to(part[g, c : c + 1, re_lanes], (GROUP, NZ))
                hat_im = jnp.broadcast_to(part[g, c : c + 1, im_lanes], (GROUP, NZ))
                for a in range(3):
                    at = at_gain + ((a * 6 + c) * TILES + k) * (sx + GROUP)
                    gain = table[pl.ds(at + starts_x[g], GROUP), :]
                    if imaginary[a * 6 + c]:
                        re[a] = re[a] - gain * hat_im
                        im[a] = im[a] + gain * hat_re
                    else:
                        re[a] = re[a] + gain * hat_re
                        im[a] = im[a] + gain * hat_im
        for j in range(pairs):
            d = lax.rem(pairs + j - pair, pairs)
            cosine = table[pl.ds(at_turn + k + d * (2 * TILES), 1), :]
            sine = table[pl.ds(at_turn + TILES + k + d * (2 * TILES), 1), :]
            for a in range(3):
                at = (a * pairs + j) * GROUP
                field[at : at + GROUP, re_lanes] = re[a] * cosine - im[a] * sine
                field[at : at + GROUP, im_lanes] = re[a] * sine + im[a] * cosine
    result = lax.dot_general(
        field[...],
        forward,
        (((1,), (1,)), ((), ())),
        precision=HIGHEST,
        preferred_element_type=jnp.float32,
    )
    for j in range(pairs):
        first, second, third = [
            result[(a * pairs + j) * GROUP : (a * pairs + j + 1) * GROUP] for a in range(3)
        ]
        both = first + pltpu.roll(second, 64, 1)
        for r in range(GROUP):
            out[r * pairs + j, 0:1, :] = both[r : r + 1]
            out[r * pairs + j, 1:2, :] = third[r : r + 1]


def last_kernel(parts, out):
    total = jnp.sum(parts[...], axis=0)
    for a in range(3):
        row = total[a // 2 : a // 2 + 1, :]
        for y in range(2):
            lane = (a % 2) * 64 + y * SZ
            value = pltpu.roll(row, (NZ - lane) % NZ, 1) if lane else row
            out[a, 0, y : y + 1, :] = value[:, :SZ]


def call(body, outs, scratch, cost, limit=16, place=pltpu.VMEM, more=(), outside=0):
    shapes = [
        pltpu.HBM(s, jnp.float32) if k < outside else jax.ShapeDtypeStruct(s, jnp.float32)
        for k, s in enumerate(outs)
    ]
    specs = [
        pl.BlockSpec(memory_space=pltpu.HBM if k < outside else pltpu.VMEM) for k in range(len(outs))
    ]

    def run(*args):
        return pl.pallas_call(
            body,
            out_shape=shapes,
            in_specs=[pl.BlockSpec(memory_space=place)] * len(args),
            out_specs=specs,
            scratch_shapes=[pltpu.VMEM(s, jnp.float32) for s in scratch] + list(more),
            compiler_params=pltpu.CompilerParams(vmem_limit_bytes=limit << 20),
            cost_estimate=pl.CostEstimate(flops=cost, bytes_accessed=cost, transcendentals=0),
        )(*args)

    return run


def swap(far, near, axis):
    count = lax.axis_size(axis)
    near_pairs = [(i, i ^ 1) for i in range(count)]
    far_pairs = [(i, (i + 1) % count if i % 2 else (i - 1) % count) for i in range(count)]
    return lax.ppermute(far, axis, far_pairs), lax.ppermute(near, axis, near_pairs)


def local(pops, label, drive):
    nx = lax.axis_size(GX)
    ny = lax.axis_size(GY)
    groups = lax.axis_size("cy")
    cells, total, far, near = call(
        first_kernel,
        [(CHANNELS, LX, LY, NZ), (6, LY, NZ), (Y_ROWS, NZ), (Y_ROWS, NZ)],
        [(2, Y_ROWS, NZ), pops.shape],
        2_000_000,
        place=pltpu.HBM,
        more=[
            pltpu.VMEM(label.shape, jnp.int32),
            pltpu.VMEM(drive.shape, jnp.float32),
            pltpu.SemaphoreType.DMA((3,)),
        ],
    )(*[pltpu.with_memory_space_constraint(value, pltpu.HBM) for value in (pops, label, drive)])
    y_far, y_near = swap(far, near, GY)
    far, near = call(
        second_kernel,
        [(X_ROWS, NZ), (X_ROWS, NZ)],
        [(2, Y_ROWS, NZ), (2, X_ROWS, NZ)],
        2_000_000,
    )(cells, y_far, y_near)
    x_far, x_near = swap(far, near, GX)
    (packs,) = call(
        own_kernel, [(CHANNELS, LX, PACK, NZ)], [(2, Y_ROWS, NZ)], 2_000_000
    )(cells, y_far, y_near)
    state_shape = (19, LX + 2 * REACH - 2, STATE_ROWS, NZ)
    state, aux, spread = call(
        third_kernel,
        [state_shape, (4, LX + 2, STATE_ROWS, NZ), (groups, 8, NZ)],
        [
            (2, X_ROWS, NZ),
            (19, LX + 2 * REACH, WORK_ROWS, NZ),
            state_shape,
            (12, 16, NZ),
        ],
        20_000_000,
        more=[pltpu.SemaphoreType.DMA(())],
        outside=1,
    )(cells, total, packs, x_far, x_near)
    blocks = lax.all_to_all(spread, "cy", 0, 0, tiled=False)
    (momentum,) = call(
        momentum_kernel, [(3, LX, LY, NZ)], [(19, LX + 2, STATE_ROWS, NZ)], 10_000_000
    )(state, aux)
    blocks, momentum = lax.optimization_barrier((blocks, momentum))
    table, starts, imaginary = operator_table(nx, 2 * ny)
    (parts,) = call(
        functools.partial(solve_kernel, starts, imaginary, ny),
        [(GROUP * ny, 2, NZ)],
        [(groups, 8, 2 * TILES * NZ), (3 * ny * GROUP, 2 * TILES * NZ)],
        10_000_000,
    )(blocks, table)
    parts = lax.all_to_all(parts, ("zl", "core", "zh", "cx"), 0, 0, tiled=False)
    (running,) = call(last_kernel, [(3, 1, 2, SZ)], [], 100_000)(parts)
    return momentum, running


def solution(mesh):
    nx, ny = mesh.devices.shape
    devices = mesh.devices.reshape(nx // GROUP, 4, 2, 2, ny // 2)
    mesh = jax.sharding.Mesh(devices, GX + GY)
    in_specs = (P(None, GX, GY, None), P(GX, GY, None), P(None, GX, GY, None))
    out_specs = (P(None, GX, GY, None), P(None, GX, GY, None))
    return jax.shard_map(local, mesh=mesh, in_specs=in_specs, out_specs=out_specs, check_vma=False)
```

```python
import functools
import math

import jax
import jax.numpy as jnp
import numpy as np
from jax import lax
from jax.experimental import pallas as pl
from jax.experimental.pallas import tpu as pltpu
from jax.sharding import PartitionSpec as P

NZ = 128
STEPS = 4
SZ = 32
LX = 4
LY = 8
VELOCITY = [
    [0, 0, 0],
    [1, 0, 0],
    [-1, 0, 0],
    [0, 1, 0],
    [0, -1, 0],
    [0, 0, 1],
    [0, 0, -1],
    [1, 1, 0],
    [-1, -1, 0],
    [1, -1, 0],
    [-1, 1, 0],
    [1, 0, 1],
    [-1, 0, -1],
    [1, 0, -1],
    [-1, 0, 1],
    [0, 1, 1],
    [0, -1, -1],
    [0, 1, -1],
    [0, -1, 1],
]
OPPOSITE = [0, 2, 1, 4, 3, 6, 5, 8, 7, 10, 9, 12, 11, 14, 13, 16, 15, 18, 17]
WEIGHTS = [1.0 / 3.0] + [1.0 / 18.0] * 6 + [1.0 / 36.0] * 12
PAIRS = [(0, 0), (1, 1), (2, 2), (0, 1), (0, 2), (1, 2)]
COMPONENT = [[0, 3, 4], [3, 1, 5], [4, 5, 2]]
SLOW_VISCOSITY = 0.0004
PHASES = [math.cos(2.0 * math.pi * (step + 0.5) / STEPS) for step in range(STEPS)]

CHANNELS = 23
CX = [v[0] for v in VELOCITY] + [0] * 4
CY = [v[1] for v in VELOCITY] + [0] * 4
HIGHEST = lax.Precision.HIGHEST
GX = ("cy", "zl", "core")
GY = ("zh", "cx")
GROUP = 8


REACH_X = STEPS - 2
REACH_Y = STEPS - 1


def pack_y(sign):
    out, at = [], 0
    for x in range(LX):
        for ch in range(CHANNELS):
            n = REACH_Y + sign * CY[ch]
            out.append((ch, x, LY - n if sign > 0 else 0, n, at))
            at += n
    return out, -(-at // 8) * 8


def pack_x(sign):
    out, at = [], 0
    for ch in range(CHANNELS):
        n = REACH_X + sign * CX[ch]
        for x in range(LX - n, LX) if sign > 0 else range(n):
            out.append((ch, x, REACH_Y + CY[ch], REACH_Y - CY[ch], at))
            at += 2 * REACH_Y + LY
    return out, -(-at // 8) * 8


SPAN = 2 * REACH_Y + LY
Y_UP, Y_ROWS = pack_y(1)
Y_DOWN, _ = pack_y(-1)
X_RIGHT, X_ROWS = pack_x(1)
X_LEFT, _ = pack_x(-1)
Y_UP_AT = {(ch, x): (n, at) for ch, x, _, n, at in Y_UP}
Y_DOWN_AT = {(ch, x): (n, at) for ch, x, _, n, at in Y_DOWN}
X_RIGHT_AT = {(ch, x): at for ch, x, _, _, at in X_RIGHT}
X_LEFT_AT = {(ch, x): at for ch, x, _, _, at in X_LEFT}
RIGHT = [i for i in range(19) if CX[i] == 1]
LEFT = [i for i in range(19) if CX[i] == -1]
EDGE_ROWS = len(RIGHT) * LY


def collide(f, label, drive, phase):
    rho = f[0]
    for i in range(1, 19):
        rho = rho + f[i]
    j = []
    for axis in range(3):
        total = None
        for i in range(1, 19, 2):
            c = VELOCITY[i][axis]
            if c == 0:
                continue
            term = f[i] - f[i + 1] if c > 0 else f[i + 1] - f[i]
            total = term if total is None else total + term
        j.append(total)
    second = label == 1.0
    solid = label == 2.0
    omega = jnp.where(second, 1.1, 1.6)
    keep = 1.0 - omega
    strength = jnp.where(second, 0.6 * phase, phase)
    inverse = 1.0 / rho
    mix = [omega * j[axis] + strength * drive[axis] for axis in range(3)]
    base = omega * (rho - 1.5 * (j[0] * j[0] + j[1] * j[1] + j[2] * j[2]) * inverse)
    curve = 4.5 * omega * inverse

    def along(vector, c):
        total = None
        for axis in range(3):
            if c[axis] == 0:
                continue
            if total is None:
                total = vector[axis] if c[axis] > 0 else -vector[axis]
            else:
                total = total + vector[axis] if c[axis] > 0 else total - vector[axis]
        return total

    post = [None] * 19
    post[0] = jnp.where(solid, f[0], keep * f[0] + WEIGHTS[0] * base)
    for i in range(1, 19, 2):
        w = WEIGHTS[i]
        cj = along(j, VELOCITY[i])
        even = w * (base + curve * (cj * cj))
        odd = (3.0 * w) * along(mix, VELOCITY[i])
        post[i] = jnp.where(solid, f[i + 1], keep * f[i] + (even + odd))
        post[i + 1] = jnp.where(solid, f[i], keep * f[i + 1] + (even - odd))
    fluid = jnp.where(solid, 0.0, inverse)
    stress = [j[a] * j[b] * fluid for a, b in PAIRS]
    return post, stress


def first_kernel(pops_in, label_in, drive_in, cells, total, far, near, box, pops, label, drive, sems):
    copies = [
        pltpu.make_async_copy(source, target, sems.at[k])
        for k, (source, target) in enumerate(((pops_in, pops), (label_in, label), (drive_in, drive)))
    ]
    for copy in copies:
        copy.start()
    for copy in copies:
        copy.wait()
    up = lax.rem(lax.axis_index(GY), 2)
    down = 1 - up
    sums = [jnp.zeros((LY, NZ), jnp.float32)] * 6
    for x in range(LX):
        f = [pops[i, x] for i in range(19)]
        lab = label[x].astype(jnp.float32)
        force = [drive[axis, x] for axis in range(3)]
        post, stress = collide(f, lab, force, PHASES[0])
        for i in range(19):
            cells[i, x] = post[i]
        cells[19, x] = lab
        for axis in range(3):
            cells[20 + axis, x] = force[axis]
        sums = [sums[k] + stress[k] for k in range(6)]
    for k in range(6):
        total[k] = sums[k]
    for ch, x, row, n, at in Y_UP:
        box[up, at : at + n, :] = cells[ch, x, row : row + n, :]
    for ch, x, row, n, at in Y_DOWN:
        box[down, at : at + n, :] = cells[ch, x, row : row + n, :]
    near[...] = box[0]
    far[...] = box[1]


def second_kernel(cells, got_far, got_near, far, near, rows, box):
    odd_y = lax.rem(lax.axis_index(GY), 2)
    low_slot, high_slot = 1 - odd_y, odd_y
    right = lax.rem(lax.axis_index(GX), 2)
    rows[0] = got_near[...]
    rows[1] = got_far[...]
    for slot, entries in ((right, X_RIGHT), (1 - right, X_LEFT)):
        for ch, x, low, high, at in entries:
            n, source = Y_UP_AT[ch, x]
            box[slot, at : at + n, :] = rows[low_slot, source : source + n, :]
            box[slot, at + low : at + low + LY, :] = cells[ch, x]
            n, source = Y_DOWN_AT[ch, x]
            box[slot, at + low + LY : at + low + LY + n, :] = rows[high_slot, source : source + n, :]
    near[...] = box[0]
    far[...] = box[1]


PACK = 16
ROW0 = 8
WORK_ROWS = 24


def own_kernel(cells, got_far, got_near, packs, rows):
    odd_y = lax.rem(lax.axis_index(GY), 2)
    rows[0] = got_near[...]
    rows[1] = got_far[...]
    for ch in range(CHANNELS):
        for x in range(LX):
            low, source = Y_UP_AT[ch, x]
            packs[ch, x, 0:low, :] = rows[1 - odd_y, source : source + low, :]
            packs[ch, x, low : low + LY, :] = cells[ch, x]
            high, source = Y_DOWN_AT[ch, x]
            packs[ch, x, low + LY : low + LY + high, :] = rows[odd_y, source : source + high, :]


def spin(value, i):
    cz = VELOCITY[i][2]
    return pltpu.roll(value, cz % NZ, 1) if cz else value


def arrive(source, x, row, n):
    return [
        spin(source[i, x - CX[i], row - CY[i] : row - CY[i] + n, :], i) for i in range(19)
    ]


def third_kernel(
    cells, total, packs, x_far, x_near, post3, spread, edge_far, edge_near, cols, one, two, sums, box
):
    odd_x = lax.rem(lax.axis_index(GX), 2)
    left_slot, right_slot = 1 - odd_x, odd_x
    cols[0] = x_near[...]
    cols[1] = x_far[...]

    def packed(ch, x):
        if x < 0:
            at = X_RIGHT_AT[ch, x + LX]
            return cols[left_slot, at : at + SPAN, :]
        if x >= LX:
            at = X_LEFT_AT[ch, x - LX]
            return cols[right_slot, at : at + SPAN, :]
        return packs[ch, x, 0:SPAN, :]

    def add(first, second):
        return second if first is None else [a + b for a, b in zip(first, second)]

    last = [total[k] for k in range(6)]
    for step, source, target in ((1, None, one), (2, one, two), (3, two, post3)):
        near, wide = REACH_X + 1 - step, REACH_Y + 1 - step
        n = LY + 2 * wide
        to = 0 if step == 3 else ROW0 - wide
        kept = None
        for x in range(-near, LX + near):
            if step == 1:
                f = [spin(packed(i, x - CX[i]), i) for i in range(19)]
            else:
                f = arrive(source, x + near + 1, ROW0 - wide, n)
            at = REACH_Y - wide
            lab, *force = [packed(ch, x)[at : at + n] for ch in range(19, CHANNELS)]
            post, stress = collide(f, lab, force, PHASES[step])
            for i in range(19):
                target[i, x + near, to : to + n, :] = post[i]
            if 0 <= x < LX:
                kept = add(kept, stress)
        for k in range(6):
            sums[6 * step - 6 + k, 0:n, :] = kept[k]
        last = [last[k] + sums[6 * step - 6 + k, wide : wide + LY, :] for k in range(6)]
    stacked = jnp.concatenate(last, axis=0)
    r = lax.broadcasted_iota(jnp.int32, (16, 48), 0)
    c = lax.broadcasted_iota(jnp.int32, (16, 48), 1)
    chosen = jnp.logical_and((r & 7) == (c >> 3), (r >> 3) == ((c & 7) >> 2))
    left = jnp.where(chosen, 1.0, 0.0)
    halves = jnp.dot(left, stacked, precision=HIGHEST, preferred_element_type=jnp.float32)
    z = lax.broadcasted_iota(jnp.int32, (NZ, NZ), 0)
    lane = lax.broadcasted_iota(jnp.int32, (NZ, NZ), 1)
    mean = 1.0 / (STEPS * 64)
    slow = jnp.zeros((8, NZ), jnp.float32)
    for half in range(2):
        table = jnp.where(lane == (z >> 2) + half * SZ, mean, 0.0)
        slow = slow + jnp.dot(
            halves[half * 8 : half * 8 + 8],
            table,
            precision=HIGHEST,
            preferred_element_type=jnp.float32,
        )
    for d in range(spread.shape[0]):
        spread[d] = slow
    for slot, comps, x in ((odd_x, RIGHT, LX - 1), (1 - odd_x, LEFT, 0)):
        for k, i in enumerate(comps):
            box[slot, k * LY : k * LY + LY, :] = post3[i, x, 1 - CY[i] : 1 - CY[i] + LY, :]
    edge_near[...] = box[0]
    edge_far[...] = box[1]


def momentum_kernel(post3, x_far, x_near, out, cols):
    odd_x = lax.rem(lax.axis_index(GX), 2)
    cols[0] = x_near[...]
    cols[1] = x_far[...]
    for x in range(LX):
        f = [None]
        for i in range(1, 19):
            source = x - CX[i]
            if source < 0:
                at = RIGHT.index(i) * LY
                value = cols[1 - odd_x, at : at + LY, :]
            elif source >= LX:
                at = LEFT.index(i) * LY
                value = cols[odd_x, at : at + LY, :]
            else:
                value = post3[i, source, 1 - CY[i] : 1 - CY[i] + LY, :]
            f.append(spin(value, i))
        for axis in range(3):
            total = None
            for i in range(1, 19, 2):
                c = VELOCITY[i][axis]
                if c == 0:
                    continue
                term = f[i] - f[i + 1] if c > 0 else f[i + 1] - f[i]
                total = term if total is None else total + term
            out[axis, x] = total


TILES = 3


@functools.cache
def operator_table(sx, sy):
    waves = [2.0 * math.pi * np.fft.fftfreq(n) for n in (sx, sy, SZ)]
    k = np.meshgrid(*waves, indexing="ij")
    square = k[0] ** 2 + k[1] ** 2 + k[2] ** 2
    positive = square > 0
    safe = np.where(positive, square, 1.0)
    half = SZ // 2 + 1
    modes = sy * half
    lanes = TILES * NZ
    ky = np.repeat(np.arange(sy), half)
    kz = np.tile(np.arange(half), sy)
    weight = np.where((kz == 0) | (kz == SZ // 2), 1.0, 2.0) / (sy * SZ)
    gains = np.zeros((3, 6, sx, lanes))
    twists = np.zeros((3, 8, lanes))
    imaginary = []
    for a in range(3):
        for c in range(6):
            force = [
                -1j * sum(k[b] for b in range(3) if COMPONENT[first][b] == c) + 0.0 * k[0]
                for first in range(3)
            ]
            inner = k[0] * force[0] + k[1] * force[1] + k[2] * force[2]
            gain = np.where(positive, (force[a] - k[a] * inner / safe) / (SLOW_VISCOSITY * safe), 0.0)
            flipped = gain
            for axis in range(3):
                flipped = np.roll(np.flip(flipped, axis), 1, axis)
            gain = 0.5 * (gain + np.conj(flipped))
            line = weight * np.fft.ifft(gain, axis=0)[:, :, :half].reshape(sx, modes)
            odd_x = (int(a == 0) + sum(int(d == 0) for d in PAIRS[c])) % 2
            imaginary.append(not odd_x)
            gains[a, c, :, :modes] = line.real if odd_x else line.imag
            if odd_x:
                twists[a, c, :modes] = line.imag[0]
    gains = np.concatenate([gains, gains[:, :, :GROUP]], axis=2)
    gains = gains.reshape(3, 6, sx + GROUP, TILES, NZ).transpose(0, 1, 3, 2, 4)
    twists = twists.reshape(3, 8, TILES, NZ).transpose(0, 2, 1, 3)
    y = np.repeat(np.arange(2), SZ)
    z = np.tile(np.arange(SZ), 2)
    angle = 2.0 * math.pi * (np.outer(y, ky) / sy + np.outer(z, kz) / SZ)
    forward = np.zeros((2, NZ, lanes))
    forward[0, :64, :modes] = np.cos(angle)
    forward[1, :64, :modes] = -np.sin(angle)
    forward = forward.reshape(2, NZ, TILES, NZ).transpose(0, 2, 1, 3)
    shift = 2.0 * math.pi * np.outer(2 * np.arange(sy // 2), ky) / sy
    turns = np.zeros((sy // 2, 2, lanes))
    turns[:, 0, :modes] = np.cos(shift)
    turns[:, 1, :modes] = np.sin(shift)
    turns = np.concatenate([turns.reshape(-1, NZ), np.zeros((-turns.size // NZ % 8, NZ))])
    sections = [gains.reshape(-1, NZ), twists.reshape(-1, NZ), turns, forward.reshape(-1, NZ)]
    starts = np.cumsum([0] + [len(section) for section in sections])
    table = np.concatenate(sections).astype(np.float32)
    return table, tuple(int(start) for start in starts[:4]), tuple(imaginary)


def solve_kernel(starts, imaginary, pairs, blocks, table, out, part, field):
    groups = blocks.shape[0]
    sx = groups * GROUP
    at_gain, at_twist, at_turn, at_forward = starts
    me = lax.axis_index("cy")
    mine = lax.rem(lax.axis_index(GX), GROUP)
    pair = lax.axis_index(GY)
    forward = jnp.concatenate(
        [table[at_forward + k * NZ : at_forward + (k + 1) * NZ, :] for k in range(2 * TILES)], axis=1
    )
    part[...] = jnp.dot(
        blocks[...].reshape(groups * 8, NZ),
        forward,
        precision=HIGHEST,
        preferred_element_type=jnp.float32,
    ).reshape(groups, 8, 2 * TILES * NZ)

    row = lax.broadcasted_iota(jnp.int32, (GROUP, NZ), 0)
    alternate = jnp.where(lax.rem(row + mine, 2) == 0, 1.0, -1.0)
    starts_x = [lax.rem(GROUP * (me + groups - g) + sx - mine, sx) for g in range(groups)]
    for k in range(TILES):
        re_lanes = slice(k * NZ, (k + 1) * NZ)
        im_lanes = slice((TILES + k) * NZ, (TILES + k + 1) * NZ)
        all_re = part[0, :, re_lanes]
        all_im = part[0, :, im_lanes]
        for g in range(1, groups):
            all_re = all_re + part[g, :, re_lanes]
            all_im = all_im + part[g, :, im_lanes]
        re, im = [], []
        for a in range(3):
            at = at_twist + (a * TILES + k) * 8
            wave = table[at : at + 8, :]
            re.append(-alternate * jnp.sum(wave * all_im, axis=0, keepdims=True))
            im.append(alternate * jnp.sum(wave * all_re, axis=0, keepdims=True))
        for g in range(groups):
            for c in range(6):
                hat_re = jnp.broadcast_to(part[g, c : c + 1, re_lanes], (GROUP, NZ))
                hat_im = jnp.broadcast_to(part[g, c : c + 1, im_lanes], (GROUP, NZ))
                for a in range(3):
                    at = at_gain + ((a * 6 + c) * TILES + k) * (sx + GROUP)
                    gain = table[pl.ds(at + starts_x[g], GROUP), :]
                    if imaginary[a * 6 + c]:
                        re[a] = re[a] - gain * hat_im
                        im[a] = im[a] + gain * hat_re
                    else:
                        re[a] = re[a] + gain * hat_re
                        im[a] = im[a] + gain * hat_im
        for j in range(pairs):
            d = lax.rem(pairs + j - pair, pairs)
            cosine = table[pl.ds(at_turn + k + d * (2 * TILES), 1), :]
            sine = table[pl.ds(at_turn + TILES + k + d * (2 * TILES), 1), :]
            for a in range(3):
                at = (a * pairs + j) * GROUP
                field[at : at + GROUP, re_lanes] = re[a] * cosine - im[a] * sine
                field[at : at + GROUP, im_lanes] = re[a] * sine + im[a] * cosine
    result = lax.dot_general(
        field[...],
        forward,
        (((1,), (1,)), ((), ())),
        precision=HIGHEST,
        preferred_element_type=jnp.float32,
    )
    for j in range(pairs):
        first, second, third = [
            result[(a * pairs + j) * GROUP : (a * pairs + j + 1) * GROUP] for a in range(3)
        ]
        both = first + pltpu.roll(second, 64, 1)
        for r in range(GROUP):
            out[r * pairs + j, 0:1, :] = both[r : r + 1]
            out[r * pairs + j, 1:2, :] = third[r : r + 1]


def last_kernel(parts, out):
    total = jnp.sum(parts[...], axis=0)
    for a in range(3):
        row = total[a // 2 : a // 2 + 1, :]
        for y in range(2):
            lane = (a % 2) * 64 + y * SZ
            value = pltpu.roll(row, (NZ - lane) % NZ, 1) if lane else row
            out[a, 0, y : y + 1, :] = value[:, :SZ]


def call(body, outs, scratch, cost, limit=16, place=pltpu.VMEM, more=()):
    shapes = [jax.ShapeDtypeStruct(s, jnp.float32) for s in outs]
    spec = pl.BlockSpec(memory_space=pltpu.VMEM)

    def run(*args):
        return pl.pallas_call(
            body,
            out_shape=shapes,
            in_specs=[pl.BlockSpec(memory_space=place)] * len(args),
            out_specs=[spec] * len(shapes),
            scratch_shapes=[pltpu.VMEM(s, jnp.float32) for s in scratch] + list(more),
            compiler_params=pltpu.CompilerParams(vmem_limit_bytes=limit << 20),
            cost_estimate=pl.CostEstimate(flops=cost, bytes_accessed=cost, transcendentals=0),
        )(*args)

    return run


def swap(far, near, axis):
    count = lax.axis_size(axis)
    near_pairs = [(i, i ^ 1) for i in range(count)]
    far_pairs = [(i, (i + 1) % count if i % 2 else (i - 1) % count) for i in range(count)]
    return lax.ppermute(far, axis, far_pairs), lax.ppermute(near, axis, near_pairs)


def local(pops, label, drive):
    nx = lax.axis_size(GX)
    ny = lax.axis_size(GY)
    groups = lax.axis_size("cy")
    cells, total, far, near = call(
        first_kernel,
        [(CHANNELS, LX, LY, NZ), (6, LY, NZ), (Y_ROWS, NZ), (Y_ROWS, NZ)],
        [(2, Y_ROWS, NZ), pops.shape],
        2_000_000,
        place=pltpu.HBM,
        more=[
            pltpu.VMEM(label.shape, jnp.int32),
            pltpu.VMEM(drive.shape, jnp.float32),
            pltpu.SemaphoreType.DMA((3,)),
        ],
    )(*[pltpu.with_memory_space_constraint(value, pltpu.HBM) for value in (pops, label, drive)])
    y_far, y_near = swap(far, near, GY)
    far, near = call(
        second_kernel,
        [(X_ROWS, NZ), (X_ROWS, NZ)],
        [(2, Y_ROWS, NZ), (2, X_ROWS, NZ)],
        2_000_000,
    )(cells, y_far, y_near)
    x_far, x_near = swap(far, near, GX)
    (packs,) = call(
        own_kernel, [(CHANNELS, LX, PACK, NZ)], [(2, Y_ROWS, NZ)], 2_000_000
    )(cells, y_far, y_near)
    post3, spread, far, near = call(
        third_kernel,
        [(19, LX, PACK, NZ), (groups, 8, NZ), (EDGE_ROWS, NZ), (EDGE_ROWS, NZ)],
        [
            (2, X_ROWS, NZ),
            (19, LX + 2 * REACH_X, WORK_ROWS, NZ),
            (19, LX + 2 * REACH_X - 2, WORK_ROWS, NZ),
            (18, 16, NZ),
            (2, EDGE_ROWS, NZ),
        ],
        20_000_000,
    )(cells, total, packs, x_far, x_near)
    blocks = lax.all_to_all(spread, "cy", 0, 0, tiled=False)
    edge_far, edge_near = swap(far, near, GX)
    blocks, edge_far, edge_near = lax.optimization_barrier((blocks, edge_far, edge_near))
    (momentum,) = call(
        momentum_kernel, [(3, LX, LY, NZ)], [(2, EDGE_ROWS, NZ)], 1_000_000
    )(post3, edge_far, edge_near)
    table, starts, imaginary = operator_table(nx, 2 * ny)
    (parts,) = call(
        functools.partial(solve_kernel, starts, imaginary, ny),
        [(GROUP * ny, 2, NZ)],
        [(groups, 8, 2 * TILES * NZ), (3 * ny * GROUP, 2 * TILES * NZ)],
        10_000_000,
    )(blocks, table)
    parts = lax.all_to_all(parts, ("zl", "core", "zh", "cx"), 0, 0, tiled=False)
    parts, momentum = lax.optimization_barrier((parts, momentum))
    (running,) = call(last_kernel, [(3, 1, 2, SZ)], [], 100_000)(parts)
    return momentum, running


def solution(mesh):
    nx, ny = mesh.devices.shape
    devices = mesh.devices.reshape(nx // GROUP, 4, 2, 2, ny // 2)
    mesh = jax.sharding.Mesh(devices, GX + GY)
    in_specs = (P(None, GX, GY, None), P(GX, GY, None), P(None, GX, GY, None))
    out_specs = (P(None, GX, GY, None), P(None, GX, GY, None))
    return jax.shard_map(local, mesh=mesh, in_specs=in_specs, out_specs=out_specs, check_vma=False)
```

```python
import functools
import math

import jax
import jax.numpy as jnp
import numpy as np
from jax import lax
from jax.experimental import pallas as pl
from jax.experimental.pallas import tpu as pltpu
from jax.sharding import PartitionSpec as P

NZ = 128
STEPS = 4
SZ = 32
LX = 4
LY = 8
VELOCITY = [
    [0, 0, 0],
    [1, 0, 0],
    [-1, 0, 0],
    [0, 1, 0],
    [0, -1, 0],
    [0, 0, 1],
    [0, 0, -1],
    [1, 1, 0],
    [-1, -1, 0],
    [1, -1, 0],
    [-1, 1, 0],
    [1, 0, 1],
    [-1, 0, -1],
    [1, 0, -1],
    [-1, 0, 1],
    [0, 1, 1],
    [0, -1, -1],
    [0, 1, -1],
    [0, -1, 1],
]
OPPOSITE = [0, 2, 1, 4, 3, 6, 5, 8, 7, 10, 9, 12, 11, 14, 13, 16, 15, 18, 17]
WEIGHTS = [1.0 / 3.0] + [1.0 / 18.0] * 6 + [1.0 / 36.0] * 12
PAIRS = [(0, 0), (1, 1), (2, 2), (0, 1), (0, 2), (1, 2)]
COMPONENT = [[0, 3, 4], [3, 1, 5], [4, 5, 2]]
SLOW_VISCOSITY = 0.0004
PHASES = [math.cos(2.0 * math.pi * (step + 0.5) / STEPS) for step in range(STEPS)]

CHANNELS = 23
CX = [v[0] for v in VELOCITY] + [0] * 4
CY = [v[1] for v in VELOCITY] + [0] * 4
HIGHEST = lax.Precision.HIGHEST
GX = ("cy", "zl", "core")
GY = ("zh", "cx")
GROUP = 8


REACH_X = STEPS - 2
REACH_Y = STEPS - 1


def pack_y(sign):
    out, at = [], 0
    for x in range(LX):
        for ch in range(CHANNELS):
            n = REACH_Y + sign * CY[ch]
            out.append((ch, x, LY - n if sign > 0 else 0, n, at))
            at += n
    return out, -(-at // 8) * 8


def pack_x(sign):
    out, at = [], 0
    for ch in range(CHANNELS):
        n = REACH_X + sign * CX[ch]
        for x in range(LX - n, LX) if sign > 0 else range(n):
            out.append((ch, x, REACH_Y + CY[ch], REACH_Y - CY[ch], at))
            at += 2 * REACH_Y + LY
    return out, -(-at // 8) * 8


SPAN = 2 * REACH_Y + LY
Y_UP, Y_ROWS = pack_y(1)
Y_DOWN, _ = pack_y(-1)
X_RIGHT, X_ROWS = pack_x(1)
X_LEFT, _ = pack_x(-1)
Y_UP_AT = {(ch, x): (n, at) for ch, x, _, n, at in Y_UP}
Y_DOWN_AT = {(ch, x): (n, at) for ch, x, _, n, at in Y_DOWN}
X_RIGHT_AT = {(ch, x): at for ch, x, _, _, at in X_RIGHT}
X_LEFT_AT = {(ch, x): at for ch, x, _, _, at in X_LEFT}
RIGHT = [i for i in range(19) if CX[i] == 1]
LEFT = [i for i in range(19) if CX[i] == -1]
EDGE_ROWS = len(RIGHT) * LY


def collide(f, label, drive, phase):
    rho = f[0]
    for i in range(1, 19):
        rho = rho + f[i]
    j = []
    for axis in range(3):
        total = None
        for i in range(1, 19, 2):
            c = VELOCITY[i][axis]
            if c == 0:
                continue
            term = f[i] - f[i + 1] if c > 0 else f[i + 1] - f[i]
            total = term if total is None else total + term
        j.append(total)
    second = label == 1.0
    solid = label == 2.0
    omega = jnp.where(second, 1.1, 1.6)
    keep = 1.0 - omega
    strength = jnp.where(second, 0.6 * phase, phase)
    inverse = 1.0 / rho
    mix = [omega * j[axis] + strength * drive[axis] for axis in range(3)]
    base = omega * (rho - 1.5 * (j[0] * j[0] + j[1] * j[1] + j[2] * j[2]) * inverse)
    curve = 4.5 * omega * inverse

    def along(vector, c):
        total = None
        for axis in range(3):
            if c[axis] == 0:
                continue
            if total is None:
                total = vector[axis] if c[axis] > 0 else -vector[axis]
            else:
                total = total + vector[axis] if c[axis] > 0 else total - vector[axis]
        return total

    post = [None] * 19
    post[0] = jnp.where(solid, f[0], keep * f[0] + WEIGHTS[0] * base)
    for i in range(1, 19, 2):
        w = WEIGHTS[i]
        cj = along(j, VELOCITY[i])
        even = w * (base + curve * (cj * cj))
        odd = (3.0 * w) * along(mix, VELOCITY[i])
        post[i] = jnp.where(solid, f[i + 1], keep * f[i] + (even + odd))
        post[i + 1] = jnp.where(solid, f[i], keep * f[i + 1] + (even - odd))
    fluid = jnp.where(solid, 0.0, inverse)
    stress = [j[a] * j[b] * fluid for a, b in PAIRS]
    return post, stress


def first_kernel(pops_in, label_in, drive_in, cells, total, far, near, box, pops, label, drive, sems):
    copies = [
        pltpu.make_async_copy(source, target, sems.at[k])
        for k, (source, target) in enumerate(((pops_in, pops), (label_in, label), (drive_in, drive)))
    ]
    for copy in copies:
        copy.start()
    for copy in copies:
        copy.wait()
    up = lax.rem(lax.axis_index(GY), 2)
    down = 1 - up
    sums = [jnp.zeros((LY, NZ), jnp.float32)] * 6
    for x in range(LX):
        f = [pops[i, x] for i in range(19)]
        lab = label[x].astype(jnp.float32)
        force = [drive[axis, x] for axis in range(3)]
        post, stress = collide(f, lab, force, PHASES[0])
        for i in range(19):
            cells[i, x] = post[i]
        cells[19, x] = lab
        for axis in range(3):
            cells[20 + axis, x] = force[axis]
        sums = [sums[k] + stress[k] for k in range(6)]
    for k in range(6):
        total[k] = sums[k]
    for ch, x, row, n, at in Y_UP:
        box[up, at : at + n, :] = cells[ch, x, row : row + n, :]
    for ch, x, row, n, at in Y_DOWN:
        box[down, at : at + n, :] = cells[ch, x, row : row + n, :]
    near[...] = box[0]
    far[...] = box[1]


def second_kernel(cells, got_far, got_near, far, near, rows, box):
    odd_y = lax.rem(lax.axis_index(GY), 2)
    low_slot, high_slot = 1 - odd_y, odd_y
    right = lax.rem(lax.axis_index(GX), 2)
    rows[0] = got_near[...]
    rows[1] = got_far[...]
    for slot, entries in ((right, X_RIGHT), (1 - right, X_LEFT)):
        for ch, x, low, high, at in entries:
            n, source = Y_UP_AT[ch, x]
            box[slot, at : at + n, :] = rows[low_slot, source : source + n, :]
            box[slot, at + low : at + low + LY, :] = cells[ch, x]
            n, source = Y_DOWN_AT[ch, x]
            box[slot, at + low + LY : at + low + LY + n, :] = rows[high_slot, source : source + n, :]
    near[...] = box[0]
    far[...] = box[1]


PACK = 16
ROW0 = 8
WORK_ROWS = 24


def own_kernel(cells, got_far, got_near, packs, rows):
    odd_y = lax.rem(lax.axis_index(GY), 2)
    rows[0] = got_near[...]
    rows[1] = got_far[...]
    for ch in range(CHANNELS):
        for x in range(LX):
            low, source = Y_UP_AT[ch, x]
            packs[ch, x, 0:low, :] = rows[1 - odd_y, source : source + low, :]
            packs[ch, x, low : low + LY, :] = cells[ch, x]
            high, source = Y_DOWN_AT[ch, x]
            packs[ch, x, low + LY : low + LY + high, :] = rows[odd_y, source : source + high, :]


def spin(value, i):
    cz = VELOCITY[i][2]
    return pltpu.roll(value, cz % NZ, 1) if cz else value


def arrive(source, x, row, n):
    return [
        spin(source[i, x - CX[i], row - CY[i] : row - CY[i] + n, :], i) for i in range(19)
    ]


def third_kernel(
    cells, total, packs, x_far, x_near, post3, spread, edge_far, edge_near, cols, one, two, sums, box
):
    odd_x = lax.rem(lax.axis_index(GX), 2)
    left_slot, right_slot = 1 - odd_x, odd_x
    cols[0] = x_near[...]
    cols[1] = x_far[...]

    def packed(ch, x):
        if x < 0:
            at = X_RIGHT_AT[ch, x + LX]
            return cols[left_slot, at : at + SPAN, :]
        if x >= LX:
            at = X_LEFT_AT[ch, x - LX]
            return cols[right_slot, at : at + SPAN, :]
        return packs[ch, x, 0:SPAN, :]

    def add(first, second):
        return second if first is None else [a + b for a, b in zip(first, second)]

    last = [total[k] for k in range(6)]
    for step, source, target in ((1, None, one), (2, one, two), (3, two, post3)):
        near, wide = REACH_X + 1 - step, REACH_Y + 1 - step
        n = LY + 2 * wide
        to = 0 if step == 3 else ROW0 - wide
        kept = None
        for x in range(-near, LX + near):
            if step == 1:
                f = [spin(packed(i, x - CX[i]), i) for i in range(19)]
            else:
                f = arrive(source, x + near + 1, ROW0 - wide, n)
            at = REACH_Y - wide
            lab, *force = [packed(ch, x)[at : at + n] for ch in range(19, CHANNELS)]
            post, stress = collide(f, lab, force, PHASES[step])
            for i in range(19):
                target[i, x + near, to : to + n, :] = post[i]
            if 0 <= x < LX:
                kept = add(kept, stress)
        for k in range(6):
            sums[6 * step - 6 + k, 0:n, :] = kept[k]
        last = [last[k] + sums[6 * step - 6 + k, wide : wide + LY, :] for k in range(6)]
    stacked = jnp.concatenate(last, axis=0)
    r = lax.broadcasted_iota(jnp.int32, (16, 48), 0)
    c = lax.broadcasted_iota(jnp.int32, (16, 48), 1)
    chosen = jnp.logical_and((r & 7) == (c >> 3), (r >> 3) == ((c & 7) >> 2))
    left = jnp.where(chosen, 1.0, 0.0)
    halves = jnp.dot(left, stacked, precision=HIGHEST, preferred_element_type=jnp.float32)
    z = lax.broadcasted_iota(jnp.int32, (NZ, NZ), 0)
    lane = lax.broadcasted_iota(jnp.int32, (NZ, NZ), 1)
    mean = 1.0 / (STEPS * 64)
    slow = jnp.zeros((8, NZ), jnp.float32)
    for half in range(2):
        table = jnp.where(lane == (z >> 2) + half * SZ, mean, 0.0)
        slow = slow + jnp.dot(
            halves[half * 8 : half * 8 + 8],
            table,
            precision=HIGHEST,
            preferred_element_type=jnp.float32,
        )
    for d in range(spread.shape[0]):
        spread[d] = slow
    for slot, comps, x in ((odd_x, RIGHT, LX - 1), (1 - odd_x, LEFT, 0)):
        for k, i in enumerate(comps):
            box[slot, k * LY : k * LY + LY, :] = post3[i, x, 1 - CY[i] : 1 - CY[i] + LY, :]
    edge_near[...] = box[0]
    edge_far[...] = box[1]


def momentum_kernel(post3, x_far, x_near, out, cols):
    odd_x = lax.rem(lax.axis_index(GX), 2)
    cols[0] = x_near[...]
    cols[1] = x_far[...]
    for x in range(LX):
        f = [None]
        for i in range(1, 19):
            source = x - CX[i]
            if source < 0:
                at = RIGHT.index(i) * LY
                value = cols[1 - odd_x, at : at + LY, :]
            elif source >= LX:
                at = LEFT.index(i) * LY
                value = cols[odd_x, at : at + LY, :]
            else:
                value = post3[i, source, 1 - CY[i] : 1 - CY[i] + LY, :]
            f.append(spin(value, i))
        for axis in range(3):
            total = None
            for i in range(1, 19, 2):
                c = VELOCITY[i][axis]
                if c == 0:
                    continue
                term = f[i] - f[i + 1] if c > 0 else f[i + 1] - f[i]
                total = term if total is None else total + term
            out[axis, x] = total


TILES = 3


@functools.cache
def operator_table(sx, sy):
    waves = [2.0 * math.pi * np.fft.fftfreq(n) for n in (sx, sy, SZ)]
    k = np.meshgrid(*waves, indexing="ij")
    square = k[0] ** 2 + k[1] ** 2 + k[2] ** 2
    positive = square > 0
    safe = np.where(positive, square, 1.0)
    half = SZ // 2 + 1
    modes = sy * half
    lanes = TILES * NZ
    ky = np.repeat(np.arange(sy), half)
    kz = np.tile(np.arange(half), sy)
    weight = np.where((kz == 0) | (kz == SZ // 2), 1.0, 2.0) / (sy * SZ)
    gains = np.zeros((3, 6, sx, lanes))
    twists = np.zeros((3, 8, lanes))
    imaginary = []
    for a in range(3):
        for c in range(6):
            force = [
                -1j * sum(k[b] for b in range(3) if COMPONENT[first][b] == c) + 0.0 * k[0]
                for first in range(3)
            ]
            inner = k[0] * force[0] + k[1] * force[1] + k[2] * force[2]
            gain = np.where(positive, (force[a] - k[a] * inner / safe) / (SLOW_VISCOSITY * safe), 0.0)
            flipped = gain
            for axis in range(3):
                flipped = np.roll(np.flip(flipped, axis), 1, axis)
            gain = 0.5 * (gain + np.conj(flipped))
            line = weight * np.fft.ifft(gain, axis=0)[:, :, :half].reshape(sx, modes)
            odd_x = (int(a == 0) + sum(int(d == 0) for d in PAIRS[c])) % 2
            imaginary.append(not odd_x)
            gains[a, c, :, :modes] = line.real if odd_x else line.imag
            if odd_x:
                twists[a, c, :modes] = line.imag[0]
    gains = gains.reshape(3, 6, sx // GROUP, GROUP, TILES, NZ).transpose(0, 1, 4, 3, 2, 5)
    gains = np.concatenate([gains[:, :, :, :, -1:], gains], axis=4)
    twists = twists.reshape(3, 8, TILES, NZ).transpose(0, 2, 1, 3)
    y = np.repeat(np.arange(2), SZ)
    z = np.tile(np.arange(SZ), 2)
    angle = 2.0 * math.pi * (np.outer(y, ky) / sy + np.outer(z, kz) / SZ)
    forward = np.zeros((2, NZ, lanes))
    forward[0, :64, :modes] = np.cos(angle)
    forward[1, :64, :modes] = -np.sin(angle)
    forward = forward.reshape(2, NZ, TILES, NZ).transpose(0, 2, 1, 3)
    shift = 2.0 * math.pi * np.outer(2 * np.arange(sy // 2), ky) / sy
    turns = np.zeros((sy // 2, 2, lanes))
    turns[:, 0, :modes] = np.cos(shift)
    turns[:, 1, :modes] = np.sin(shift)
    turns = np.concatenate([turns.reshape(-1, NZ), np.zeros((-turns.size // NZ % 8, NZ))])
    sections = [gains.reshape(-1, NZ), twists.reshape(-1, NZ), turns, forward.reshape(-1, NZ)]
    starts = np.cumsum([0] + [len(section) for section in sections])
    table = np.concatenate(sections).astype(np.float32)
    return table, tuple(int(start) for start in starts[:4]), tuple(imaginary)


def solve_kernel(starts, imaginary, pairs, groups, blocks, table, out, part, hat, field):
    at_gain, at_twist, at_turn, at_forward = starts
    me = lax.axis_index("cy")
    mine = lax.rem(lax.axis_index(GX), GROUP)
    upper = lax.axis_index("zh")
    column = lax.axis_index("cx")
    columns = pairs // 2
    forward = jnp.concatenate(
        [table[at_forward + k * NZ : at_forward + (k + 1) * NZ, :] for k in range(2 * TILES)], axis=1
    )
    part[...] = jnp.dot(
        blocks[...].reshape(2 * GROUP * 8, NZ),
        forward,
        precision=HIGHEST,
        preferred_element_type=jnp.float32,
    ).reshape(2 * GROUP, 8, 2 * TILES * NZ)
    half = [table[at_turn + columns * (2 * TILES) + k : at_turn + columns * (2 * TILES) + k + 1, :] for k in range(TILES)]
    half = jnp.concatenate(half + half, axis=1)
    for r in range(GROUP):
        hat[r] = part[2 * r + upper] + half * part[2 * r + 1 - upper]

    sign = (1 - 2 * lax.rem(mine, 2)).astype(jnp.float32)
    for k in range(TILES):
        re_lanes = slice(k * NZ, (k + 1) * NZ)
        im_lanes = slice((TILES + k) * NZ, (TILES + k + 1) * NZ)
        all_re = hat[0, :, re_lanes]
        all_im = hat[0, :, im_lanes]
        for r in range(1, GROUP):
            all_re = all_re + hat[r, :, re_lanes] if r % 2 == 0 else all_re - hat[r, :, re_lanes]
            all_im = all_im + hat[r, :, im_lanes] if r % 2 == 0 else all_im - hat[r, :, im_lanes]
        re, im = [], []
        for a in range(3):
            at = at_twist + (a * TILES + k) * 8
            wave = sign * table[at : at + 8, :]
            first_re = -jnp.sum(wave * all_im, axis=0, keepdims=True)
            first_im = jnp.sum(wave * all_re, axis=0, keepdims=True)
            re.append(jnp.broadcast_to(first_re, (groups, NZ)))
            im.append(jnp.broadcast_to(first_im, (groups, NZ)))
        for r in range(GROUP):
            apart = mine + GROUP - r
            ahead = apart // GROUP
            row = (apart - GROUP * ahead) * (groups + 1) + ahead
            for c in range(6):
                hat_re = jnp.broadcast_to(hat[r, c : c + 1, re_lanes], (groups, NZ))
                hat_im = jnp.broadcast_to(hat[r, c : c + 1, im_lanes], (groups, NZ))
                for a in range(3):
                    at = at_gain + ((a * 6 + c) * TILES + k) * (GROUP * (groups + 1))
                    gain = table[pl.ds(at + row, groups), :]
                    if imaginary[a * 6 + c]:
                        re[a] = re[a] - gain * hat_im
                        im[a] = im[a] + gain * hat_re
                    else:
                        re[a] = re[a] + gain * hat_re
                        im[a] = im[a] + gain * hat_im
        for j in range(columns):
            d = lax.rem(pairs + j - column, pairs)
            cosine = table[pl.ds(at_turn + k + d * (2 * TILES), 1), :]
            sine = table[pl.ds(at_turn + TILES + k + d * (2 * TILES), 1), :]
            for a in range(3):
                at = (a * columns + j) * groups
                field[at : at + groups, re_lanes] = re[a] * cosine - im[a] * sine
                field[at : at + groups, im_lanes] = re[a] * sine + im[a] * cosine
    result = lax.dot_general(
        field[...],
        forward,
        (((1,), (1,)), ((), ())),
        precision=HIGHEST,
        preferred_element_type=jnp.float32,
    )
    for j in range(columns):
        first, second, third = [
            result[(a * columns + j) * groups : (a * columns + j + 1) * groups] for a in range(3)
        ]
        both = first + pltpu.roll(second, 64, 1)
        for q in range(groups):
            target = lax.rem(me + q, groups) * columns + j
            out[target, 0:1, :] = both[q : q + 1]
            out[target, 1:2, :] = third[q : q + 1]


def last_kernel(parts, out):
    total = jnp.sum(parts[...], axis=0)
    for a in range(3):
        row = total[a // 2 : a // 2 + 1, :]
        for y in range(2):
            lane = (a % 2) * 64 + y * SZ
            value = pltpu.roll(row, (NZ - lane) % NZ, 1) if lane else row
            out[a, 0, y : y + 1, :] = value[:, :SZ]


def call(body, outs, scratch, cost, limit=16, place=pltpu.VMEM, more=()):
    shapes = [jax.ShapeDtypeStruct(s, jnp.float32) for s in outs]
    spec = pl.BlockSpec(memory_space=pltpu.VMEM)

    def run(*args):
        return pl.pallas_call(
            body,
            out_shape=shapes,
            in_specs=[pl.BlockSpec(memory_space=place)] * len(args),
            out_specs=[spec] * len(shapes),
            scratch_shapes=[pltpu.VMEM(s, jnp.float32) for s in scratch] + list(more),
            compiler_params=pltpu.CompilerParams(vmem_limit_bytes=limit << 20),
            cost_estimate=pl.CostEstimate(flops=cost, bytes_accessed=cost, transcendentals=0),
        )(*args)

    return run


def swap(far, near, axis):
    count = lax.axis_size(axis)
    near_pairs = [(i, i ^ 1) for i in range(count)]
    far_pairs = [(i, (i + 1) % count if i % 2 else (i - 1) % count) for i in range(count)]
    return lax.ppermute(far, axis, far_pairs), lax.ppermute(near, axis, near_pairs)


def local(pops, label, drive):
    nx = lax.axis_size(GX)
    ny = lax.axis_size(GY)
    groups = lax.axis_size("cy")
    cells, total, far, near = call(
        first_kernel,
        [(CHANNELS, LX, LY, NZ), (6, LY, NZ), (Y_ROWS, NZ), (Y_ROWS, NZ)],
        [(2, Y_ROWS, NZ), pops.shape],
        2_000_000,
        place=pltpu.HBM,
        more=[
            pltpu.VMEM(label.shape, jnp.int32),
            pltpu.VMEM(drive.shape, jnp.float32),
            pltpu.SemaphoreType.DMA((3,)),
        ],
    )(*[pltpu.with_memory_space_constraint(value, pltpu.HBM) for value in (pops, label, drive)])
    y_far, y_near = swap(far, near, GY)
    far, near = call(
        second_kernel,
        [(X_ROWS, NZ), (X_ROWS, NZ)],
        [(2, Y_ROWS, NZ), (2, X_ROWS, NZ)],
        2_000_000,
    )(cells, y_far, y_near)
    x_far, x_near = swap(far, near, GX)
    (packs,) = call(
        own_kernel, [(CHANNELS, LX, PACK, NZ)], [(2, Y_ROWS, NZ)], 2_000_000
    )(cells, y_far, y_near)
    post3, spread, far, near = call(
        third_kernel,
        [(19, LX, PACK, NZ), (2 * GROUP, 8, NZ), (EDGE_ROWS, NZ), (EDGE_ROWS, NZ)],
        [
            (2, X_ROWS, NZ),
            (19, LX + 2 * REACH_X, WORK_ROWS, NZ),
            (19, LX + 2 * REACH_X - 2, WORK_ROWS, NZ),
            (18, 16, NZ),
            (2, EDGE_ROWS, NZ),
        ],
        20_000_000,
    )(cells, total, packs, x_far, x_near)
    blocks = lax.all_to_all(spread, ("zl", "core", "zh"), 0, 0, tiled=False)
    edge_far, edge_near = swap(far, near, GX)
    blocks, edge_far, edge_near = lax.optimization_barrier((blocks, edge_far, edge_near))
    (momentum,) = call(
        momentum_kernel, [(3, LX, LY, NZ)], [(2, EDGE_ROWS, NZ)], 1_000_000
    )(post3, edge_far, edge_near)
    table, starts, imaginary = operator_table(nx, 2 * ny)
    (parts,) = call(
        functools.partial(solve_kernel, starts, imaginary, ny, groups),
        [(groups * ny // 2, 2, NZ)],
        [
            (2 * GROUP, 8, 2 * TILES * NZ),
            (GROUP, 8, 2 * TILES * NZ),
            (3 * groups * ny // 2, 2 * TILES * NZ),
        ],
        10_000_000,
    )(blocks, table)
    parts = lax.all_to_all(parts, ("cy", "cx"), 0, 0, tiled=False)
    parts, momentum = lax.optimization_barrier((parts, momentum))
    (running,) = call(last_kernel, [(3, 1, 2, SZ)], [], 100_000)(parts)
    return momentum, running


def solution(mesh):
    nx, ny = mesh.devices.shape
    devices = mesh.devices.reshape(nx // GROUP, 4, 2, 2, ny // 2)
    mesh = jax.sharding.Mesh(devices, GX + GY)
    in_specs = (P(None, GX, GY, None), P(GX, GY, None), P(None, GX, GY, None))
    out_specs = (P(None, GX, GY, None), P(None, GX, GY, None))
    return jax.shard_map(local, mesh=mesh, in_specs=in_specs, out_specs=out_specs, check_vma=False)
```

```python
import functools
import math

import jax
import jax.numpy as jnp
import numpy as np
from jax import lax
from jax.experimental import pallas as pl
from jax.experimental.pallas import tpu as pltpu
from jax.sharding import PartitionSpec as P

NZ = 128
STEPS = 4
SZ = 32
LX = 4
LY = 8
VELOCITY = [
    [0, 0, 0],
    [1, 0, 0],
    [-1, 0, 0],
    [0, 1, 0],
    [0, -1, 0],
    [0, 0, 1],
    [0, 0, -1],
    [1, 1, 0],
    [-1, -1, 0],
    [1, -1, 0],
    [-1, 1, 0],
    [1, 0, 1],
    [-1, 0, -1],
    [1, 0, -1],
    [-1, 0, 1],
    [0, 1, 1],
    [0, -1, -1],
    [0, 1, -1],
    [0, -1, 1],
]
OPPOSITE = [0, 2, 1, 4, 3, 6, 5, 8, 7, 10, 9, 12, 11, 14, 13, 16, 15, 18, 17]
WEIGHTS = [1.0 / 3.0] + [1.0 / 18.0] * 6 + [1.0 / 36.0] * 12
PAIRS = [(0, 0), (1, 1), (2, 2), (0, 1), (0, 2), (1, 2)]
COMPONENT = [[0, 3, 4], [3, 1, 5], [4, 5, 2]]
SLOW_VISCOSITY = 0.0004
PHASES = [math.cos(2.0 * math.pi * (step + 0.5) / STEPS) for step in range(STEPS)]

CHANNELS = 23
CX = [v[0] for v in VELOCITY] + [0] * 4
CY = [v[1] for v in VELOCITY] + [0] * 4
HIGHEST = lax.Precision.HIGHEST
GX = ("cy", "zl", "core")
GY = ("zh", "cx")
GROUP = 8


REACH_X = STEPS - 2
REACH_Y = STEPS - 1


def pack_y(sign):
    out, at = [], 0
    for x in range(LX):
        for ch in range(CHANNELS):
            n = REACH_Y + sign * CY[ch]
            out.append((ch, x, LY - n if sign > 0 else 0, n, at))
            at += n
    return out, -(-at // 8) * 8


def pack_x(sign):
    out, at = [], 0
    for ch in range(CHANNELS):
        n = REACH_X + sign * CX[ch]
        for x in range(LX - n, LX) if sign > 0 else range(n):
            out.append((ch, x, REACH_Y + CY[ch], REACH_Y - CY[ch], at))
            at += 2 * REACH_Y + LY
    return out, -(-at // 8) * 8


SPAN = 2 * REACH_Y + LY
Y_UP, Y_ROWS = pack_y(1)
Y_DOWN, _ = pack_y(-1)
X_RIGHT, X_ROWS = pack_x(1)
X_LEFT, _ = pack_x(-1)
Y_UP_AT = {(ch, x): (n, at) for ch, x, _, n, at in Y_UP}
Y_DOWN_AT = {(ch, x): (n, at) for ch, x, _, n, at in Y_DOWN}
X_RIGHT_AT = {(ch, x): at for ch, x, _, _, at in X_RIGHT}
X_LEFT_AT = {(ch, x): at for ch, x, _, _, at in X_LEFT}
RIGHT = [i for i in range(19) if CX[i] == 1]
LEFT = [i for i in range(19) if CX[i] == -1]
EDGE_ROWS = len(RIGHT) * LY


def collide(f, label, drive, phase):
    rho = f[0]
    for i in range(1, 19):
        rho = rho + f[i]
    j = []
    for axis in range(3):
        total = None
        for i in range(1, 19, 2):
            c = VELOCITY[i][axis]
            if c == 0:
                continue
            term = f[i] - f[i + 1] if c > 0 else f[i + 1] - f[i]
            total = term if total is None else total + term
        j.append(total)
    second = label == 1.0
    solid = label == 2.0
    omega = jnp.where(second, 1.1, 1.6)
    keep = 1.0 - omega
    strength = jnp.where(second, 0.6 * phase, phase)
    inverse = 1.0 / rho
    mix = [omega * j[axis] + strength * drive[axis] for axis in range(3)]
    base = omega * (rho - 1.5 * (j[0] * j[0] + j[1] * j[1] + j[2] * j[2]) * inverse)
    curve = 4.5 * omega * inverse

    def along(vector, c):
        total = None
        for axis in range(3):
            if c[axis] == 0:
                continue
            if total is None:
                total = vector[axis] if c[axis] > 0 else -vector[axis]
            else:
                total = total + vector[axis] if c[axis] > 0 else total - vector[axis]
        return total

    post = [None] * 19
    post[0] = jnp.where(solid, f[0], keep * f[0] + WEIGHTS[0] * base)
    for i in range(1, 19, 2):
        w = WEIGHTS[i]
        cj = along(j, VELOCITY[i])
        even = w * (base + curve * (cj * cj))
        odd = (3.0 * w) * along(mix, VELOCITY[i])
        post[i] = jnp.where(solid, f[i + 1], keep * f[i] + (even + odd))
        post[i + 1] = jnp.where(solid, f[i], keep * f[i + 1] + (even - odd))
    fluid = jnp.where(solid, 0.0, inverse)
    stress = [j[a] * j[b] * fluid for a, b in PAIRS]
    return post, stress


def first_kernel(pops_in, label_in, drive_in, cells, total, far, near, box, pops, label, drive, sems):
    copies = [
        pltpu.make_async_copy(source, target, sems.at[k])
        for k, (source, target) in enumerate(((pops_in, pops), (label_in, label), (drive_in, drive)))
    ]
    for copy in copies:
        copy.start()
    for copy in copies:
        copy.wait()
    up = lax.rem(lax.axis_index(GY), 2)
    down = 1 - up
    sums = [jnp.zeros((LY, NZ), jnp.float32)] * 6
    for x in range(LX):
        f = [pops[i, x] for i in range(19)]
        lab = label[x].astype(jnp.float32)
        force = [drive[axis, x] for axis in range(3)]
        post, stress = collide(f, lab, force, PHASES[0])
        for i in range(19):
            cells[i, x] = post[i]
        cells[19, x] = lab
        for axis in range(3):
            cells[20 + axis, x] = force[axis]
        sums = [sums[k] + stress[k] for k in range(6)]
    for k in range(6):
        total[k] = sums[k]
    for ch, x, row, n, at in Y_UP:
        box[up, at : at + n, :] = cells[ch, x, row : row + n, :]
    for ch, x, row, n, at in Y_DOWN:
        box[down, at : at + n, :] = cells[ch, x, row : row + n, :]
    near[...] = box[0]
    far[...] = box[1]


def second_kernel(cells, got_far, got_near, far, near, rows, box):
    odd_y = lax.rem(lax.axis_index(GY), 2)
    low_slot, high_slot = 1 - odd_y, odd_y
    right = lax.rem(lax.axis_index(GX), 2)
    rows[0] = got_near[...]
    rows[1] = got_far[...]
    for slot, entries in ((right, X_RIGHT), (1 - right, X_LEFT)):
        for ch, x, low, high, at in entries:
            n, source = Y_UP_AT[ch, x]
            box[slot, at : at + n, :] = rows[low_slot, source : source + n, :]
            box[slot, at + low : at + low + LY, :] = cells[ch, x]
            n, source = Y_DOWN_AT[ch, x]
            box[slot, at + low + LY : at + low + LY + n, :] = rows[high_slot, source : source + n, :]
    near[...] = box[0]
    far[...] = box[1]


PACK = 16
ROW0 = 8
WORK_ROWS = 24


def own_kernel(cells, got_far, got_near, packs, rows):
    odd_y = lax.rem(lax.axis_index(GY), 2)
    rows[0] = got_near[...]
    rows[1] = got_far[...]
    for ch in range(CHANNELS):
        for x in range(LX):
            low, source = Y_UP_AT[ch, x]
            packs[ch, x, 0:low, :] = rows[1 - odd_y, source : source + low, :]
            packs[ch, x, low : low + LY, :] = cells[ch, x]
            high, source = Y_DOWN_AT[ch, x]
            packs[ch, x, low + LY : low + LY + high, :] = rows[odd_y, source : source + high, :]


def spin(value, i):
    cz = VELOCITY[i][2]
    return pltpu.roll(value, cz % NZ, 1) if cz else value


def arrive(source, x, row, n):
    return [
        spin(source[i, x - CX[i], row - CY[i] : row - CY[i] + n, :], i) for i in range(19)
    ]


def third_kernel(
    cells, total, packs, x_far, x_near, post3, spread, edge_far, edge_near, cols, one, two, sums, box
):
    odd_x = lax.rem(lax.axis_index(GX), 2)
    left_slot, right_slot = 1 - odd_x, odd_x
    cols[0] = x_near[...]
    cols[1] = x_far[...]

    def packed(ch, x):
        if x < 0:
            at = X_RIGHT_AT[ch, x + LX]
            return cols[left_slot, at : at + SPAN, :]
        if x >= LX:
            at = X_LEFT_AT[ch, x - LX]
            return cols[right_slot, at : at + SPAN, :]
        return packs[ch, x, 0:SPAN, :]

    def add(first, second):
        return second if first is None else [a + b for a, b in zip(first, second)]

    last = [total[k] for k in range(6)]
    for step, source, target in ((1, None, one), (2, one, two), (3, two, post3)):
        near, wide = REACH_X + 1 - step, REACH_Y + 1 - step
        n = LY + 2 * wide
        to = 0 if step == 3 else ROW0 - wide
        kept = None
        for x in range(-near, LX + near):
            if step == 1:
                f = [spin(packed(i, x - CX[i]), i) for i in range(19)]
            else:
                f = arrive(source, x + near + 1, ROW0 - wide, n)
            at = REACH_Y - wide
            lab, *force = [packed(ch, x)[at : at + n] for ch in range(19, CHANNELS)]
            post, stress = collide(f, lab, force, PHASES[step])
            for i in range(19):
                target[i, x + near, to : to + n, :] = post[i]
            if 0 <= x < LX:
                kept = add(kept, stress)
        for k in range(6):
            sums[6 * step - 6 + k, 0:n, :] = kept[k]
        last = [last[k] + sums[6 * step - 6 + k, wide : wide + LY, :] for k in range(6)]
    stacked = jnp.concatenate(last, axis=0)
    r = lax.broadcasted_iota(jnp.int32, (16, 48), 0)
    c = lax.broadcasted_iota(jnp.int32, (16, 48), 1)
    chosen = jnp.logical_and((r & 7) == (c >> 3), (r >> 3) == ((c & 7) >> 2))
    left = jnp.where(chosen, 1.0, 0.0)
    halves = jnp.dot(left, stacked, precision=HIGHEST, preferred_element_type=jnp.float32)
    z = lax.broadcasted_iota(jnp.int32, (2 * NZ, NZ), 0)
    lane = lax.broadcasted_iota(jnp.int32, (2 * NZ, NZ), 1)
    table = jnp.where(lane == z >> 2, 1.0 / (STEPS * 64), 0.0)
    slow = jnp.dot(
        jnp.concatenate([halves[0:8], halves[8:16]], axis=1),
        table,
        precision=HIGHEST,
        preferred_element_type=jnp.float32,
    )
    for d in range(spread.shape[0]):
        spread[d] = slow
    for slot, comps, x in ((odd_x, RIGHT, LX - 1), (1 - odd_x, LEFT, 0)):
        for k, i in enumerate(comps):
            box[slot, k * LY : k * LY + LY, :] = post3[i, x, 1 - CY[i] : 1 - CY[i] + LY, :]
    edge_near[...] = box[0]
    edge_far[...] = box[1]


def momentum_of(post3, x_far, x_near, out, cols):
    odd_x = lax.rem(lax.axis_index(GX), 2)
    cols[0] = x_near[...]
    cols[1] = x_far[...]
    for x in range(LX):
        f = [None]
        for i in range(1, 19):
            source = x - CX[i]
            if source < 0:
                at = RIGHT.index(i) * LY
                value = cols[1 - odd_x, at : at + LY, :]
            elif source >= LX:
                at = LEFT.index(i) * LY
                value = cols[odd_x, at : at + LY, :]
            else:
                value = post3[i, source, 1 - CY[i] : 1 - CY[i] + LY, :]
            f.append(spin(value, i))
        for axis in range(3):
            total = None
            for i in range(1, 19, 2):
                c = VELOCITY[i][axis]
                if c == 0:
                    continue
                term = f[i] - f[i + 1] if c > 0 else f[i + 1] - f[i]
                total = term if total is None else total + term
            out[axis, x] = total


TILES = 3


@functools.cache
def operator_table(sx, sy):
    waves = [2.0 * math.pi * np.fft.fftfreq(n) for n in (sx, sy, SZ)]
    k = np.meshgrid(*waves, indexing="ij")
    square = k[0] ** 2 + k[1] ** 2 + k[2] ** 2
    positive = square > 0
    safe = np.where(positive, square, 1.0)
    half = SZ // 2 + 1
    modes = sy * half
    lanes = TILES * NZ
    ky = np.repeat(np.arange(sy), half)
    kz = np.tile(np.arange(half), sy)
    weight = np.where((kz == 0) | (kz == SZ // 2), 1.0, 2.0) / (sy * SZ)
    gains = np.zeros((3, 6, sx, lanes))
    twists = np.zeros((3, 8, lanes))
    imaginary = []
    for a in range(3):
        for c in range(6):
            force = [
                -1j * sum(k[b] for b in range(3) if COMPONENT[first][b] == c) + 0.0 * k[0]
                for first in range(3)
            ]
            inner = k[0] * force[0] + k[1] * force[1] + k[2] * force[2]
            gain = np.where(positive, (force[a] - k[a] * inner / safe) / (SLOW_VISCOSITY * safe), 0.0)
            flipped = gain
            for axis in range(3):
                flipped = np.roll(np.flip(flipped, axis), 1, axis)
            gain = 0.5 * (gain + np.conj(flipped))
            line = weight * np.fft.ifft(gain, axis=0)[:, :, :half].reshape(sx, modes)
            odd_x = (int(a == 0) + sum(int(d == 0) for d in PAIRS[c])) % 2
            imaginary.append(not odd_x)
            gains[a, c, :, :modes] = line.real if odd_x else line.imag
            if odd_x:
                twists[a, c, :modes] = line.imag[0]
    gains = gains.reshape(3, 6, sx // GROUP, GROUP, TILES, NZ).transpose(0, 1, 4, 3, 2, 5)
    gains = np.concatenate([gains[:, :, :, :, -1:], gains], axis=4)
    twists = twists.reshape(3, 8, TILES, NZ).transpose(0, 2, 1, 3)
    y = np.repeat(np.arange(2), SZ)
    z = np.tile(np.arange(SZ), 2)
    angle = 2.0 * math.pi * (np.outer(y, ky) / sy + np.outer(z, kz) / SZ)
    forward = np.zeros((2, NZ, lanes))
    forward[0, :64, :modes] = np.cos(angle)
    forward[1, :64, :modes] = -np.sin(angle)
    forward = forward.reshape(2, NZ, TILES, NZ).transpose(0, 2, 1, 3)
    shift = 2.0 * math.pi * np.outer(2 * np.arange(sy // 2), ky) / sy
    turns = np.zeros((sy // 2, 2, lanes))
    turns[:, 0, :modes] = np.cos(shift)
    turns[:, 1, :modes] = np.sin(shift)
    turns = np.concatenate([turns.reshape(-1, NZ), np.zeros((-turns.size // NZ % 8, NZ))])
    sections = [gains.reshape(-1, NZ), twists.reshape(-1, NZ), turns, forward.reshape(-1, NZ)]
    starts = np.cumsum([0] + [len(section) for section in sections])
    table = np.concatenate(sections).astype(np.float32)
    return table, tuple(int(start) for start in starts[:4]), tuple(imaginary)


def solve_kernel(
    starts,
    imaginary,
    pairs,
    groups,
    blocks,
    table,
    post3,
    x_far,
    x_near,
    out,
    momentum,
    part,
    hat,
    field,
    cols,
):
    momentum_of(post3, x_far, x_near, momentum, cols)
    at_gain, at_twist, at_turn, at_forward = starts
    me = lax.axis_index("cy")
    mine = lax.rem(lax.axis_index(GX), GROUP)
    upper = lax.axis_index("zh")
    column = lax.axis_index("cx")
    columns = pairs // 2
    forward = jnp.concatenate(
        [table[at_forward + k * NZ : at_forward + (k + 1) * NZ, :] for k in range(2 * TILES)], axis=1
    )
    part[...] = jnp.dot(
        blocks[...].reshape(2 * GROUP * 8, NZ),
        forward,
        precision=HIGHEST,
        preferred_element_type=jnp.float32,
    ).reshape(2 * GROUP, 8, 2 * TILES * NZ)
    half = [table[at_turn + columns * (2 * TILES) + k : at_turn + columns * (2 * TILES) + k + 1, :] for k in range(TILES)]
    half = jnp.concatenate(half + half, axis=1)
    for r in range(GROUP):
        hat[r] = part[2 * r + upper] + half * part[2 * r + 1 - upper]

    sign = (1 - 2 * lax.rem(mine, 2)).astype(jnp.float32)
    for k in range(TILES):
        re_lanes = slice(k * NZ, (k + 1) * NZ)
        im_lanes = slice((TILES + k) * NZ, (TILES + k + 1) * NZ)
        all_re = hat[0, :, re_lanes]
        all_im = hat[0, :, im_lanes]
        for r in range(1, GROUP):
            all_re = all_re + hat[r, :, re_lanes] if r % 2 == 0 else all_re - hat[r, :, re_lanes]
            all_im = all_im + hat[r, :, im_lanes] if r % 2 == 0 else all_im - hat[r, :, im_lanes]
        re, im = [], []
        for a in range(3):
            at = at_twist + (a * TILES + k) * 8
            wave = sign * table[at : at + 8, :]
            first_re = -jnp.sum(wave * all_im, axis=0, keepdims=True)
            first_im = jnp.sum(wave * all_re, axis=0, keepdims=True)
            re.append(jnp.broadcast_to(first_re, (groups, NZ)))
            im.append(jnp.broadcast_to(first_im, (groups, NZ)))
        for r in range(GROUP):
            apart = mine + GROUP - r
            ahead = apart // GROUP
            row = (apart - GROUP * ahead) * (groups + 1) + ahead
            for c in range(6):
                hat_re = jnp.broadcast_to(hat[r, c : c + 1, re_lanes], (groups, NZ))
                hat_im = jnp.broadcast_to(hat[r, c : c + 1, im_lanes], (groups, NZ))
                for a in range(3):
                    at = at_gain + ((a * 6 + c) * TILES + k) * (GROUP * (groups + 1))
                    gain = table[pl.ds(at + row, groups), :]
                    if imaginary[a * 6 + c]:
                        re[a] = re[a] - gain * hat_im
                        im[a] = im[a] + gain * hat_re
                    else:
                        re[a] = re[a] + gain * hat_re
                        im[a] = im[a] + gain * hat_im
        for j in range(columns):
            d = lax.rem(pairs + j - column, pairs)
            cosine = table[pl.ds(at_turn + k + d * (2 * TILES), 1), :]
            sine = table[pl.ds(at_turn + TILES + k + d * (2 * TILES), 1), :]
            for a in range(3):
                at = (a * columns + j) * groups
                field[at : at + groups, re_lanes] = re[a] * cosine - im[a] * sine
                field[at : at + groups, im_lanes] = re[a] * sine + im[a] * cosine
    result = lax.dot_general(
        field[...],
        forward,
        (((1,), (1,)), ((), ())),
        precision=HIGHEST,
        preferred_element_type=jnp.float32,
    )
    for j in range(columns):
        first, second, third = [
            result[(a * columns + j) * groups : (a * columns + j + 1) * groups] for a in range(3)
        ]
        both = first + pltpu.roll(second, 64, 1)
        for q in range(groups):
            target = lax.rem(me + q, groups) * columns + j
            out[target, 0:1, :] = both[q : q + 1]
            out[target, 1:2, :] = third[q : q + 1]


def last_kernel(parts, out):
    total = jnp.sum(parts[...], axis=0)
    for a in range(3):
        row = total[a // 2 : a // 2 + 1, :]
        for y in range(2):
            lane = (a % 2) * 64 + y * SZ
            value = pltpu.roll(row, (NZ - lane) % NZ, 1) if lane else row
            out[a, 0, y : y + 1, :] = value[:, :SZ]


def call(body, outs, scratch, cost, limit=16, place=pltpu.VMEM, more=()):
    shapes = [jax.ShapeDtypeStruct(s, jnp.float32) for s in outs]
    spec = pl.BlockSpec(memory_space=pltpu.VMEM)

    def run(*args):
        return pl.pallas_call(
            body,
            out_shape=shapes,
            in_specs=[pl.BlockSpec(memory_space=place)] * len(args),
            out_specs=[spec] * len(shapes),
            scratch_shapes=[pltpu.VMEM(s, jnp.float32) for s in scratch] + list(more),
            compiler_params=pltpu.CompilerParams(vmem_limit_bytes=limit << 20),
            cost_estimate=pl.CostEstimate(flops=cost, bytes_accessed=cost, transcendentals=0),
        )(*args)

    return run


def swap(far, near, axis):
    count = lax.axis_size(axis)
    near_pairs = [(i, i ^ 1) for i in range(count)]
    far_pairs = [(i, (i + 1) % count if i % 2 else (i - 1) % count) for i in range(count)]
    return lax.ppermute(far, axis, far_pairs), lax.ppermute(near, axis, near_pairs)


def local(pops, label, drive):
    nx = lax.axis_size(GX)
    ny = lax.axis_size(GY)
    groups = lax.axis_size("cy")
    cells, total, far, near = call(
        first_kernel,
        [(CHANNELS, LX, LY, NZ), (6, LY, NZ), (Y_ROWS, NZ), (Y_ROWS, NZ)],
        [(2, Y_ROWS, NZ), pops.shape],
        2_000_000,
        place=pltpu.HBM,
        more=[
            pltpu.VMEM(label.shape, jnp.int32),
            pltpu.VMEM(drive.shape, jnp.float32),
            pltpu.SemaphoreType.DMA((3,)),
        ],
    )(*[pltpu.with_memory_space_constraint(value, pltpu.HBM) for value in (pops, label, drive)])
    y_far, y_near = swap(far, near, GY)
    far, near = call(
        second_kernel,
        [(X_ROWS, NZ), (X_ROWS, NZ)],
        [(2, Y_ROWS, NZ), (2, X_ROWS, NZ)],
        2_000_000,
    )(cells, y_far, y_near)
    x_far, x_near = swap(far, near, GX)
    (packs,) = call(
        own_kernel, [(CHANNELS, LX, PACK, NZ)], [(2, Y_ROWS, NZ)], 2_000_000
    )(cells, y_far, y_near)
    post3, spread, far, near = call(
        third_kernel,
        [(19, LX, PACK, NZ), (2 * GROUP, 8, NZ), (EDGE_ROWS, NZ), (EDGE_ROWS, NZ)],
        [
            (2, X_ROWS, NZ),
            (19, LX + 2 * REACH_X, WORK_ROWS, NZ),
            (19, LX + 2 * REACH_X - 2, WORK_ROWS, NZ),
            (18, 16, NZ),
            (2, EDGE_ROWS, NZ),
        ],
        20_000_000,
    )(cells, total, packs, x_far, x_near)
    blocks = lax.all_to_all(spread, ("zl", "core", "zh"), 0, 0, tiled=False)
    edge_far, edge_near = swap(far, near, GX)
    blocks, edge_far, edge_near = lax.optimization_barrier((blocks, edge_far, edge_near))
    table, starts, imaginary = operator_table(nx, 2 * ny)
    parts, momentum = call(
        functools.partial(solve_kernel, starts, imaginary, ny, groups),
        [(groups * ny // 2, 2, NZ), (3, LX, LY, NZ)],
        [
            (2 * GROUP, 8, 2 * TILES * NZ),
            (GROUP, 8, 2 * TILES * NZ),
            (3 * groups * ny // 2, 2 * TILES * NZ),
            (2, EDGE_ROWS, NZ),
        ],
        10_000_000,
    )(blocks, table, post3, edge_far, edge_near)
    parts = lax.all_to_all(parts, ("cy", "cx"), 0, 0, tiled=False)
    (running,) = call(last_kernel, [(3, 1, 2, SZ)], [], 100_000)(parts)
    return momentum, running


def solution(mesh):
    nx, ny = mesh.devices.shape
    devices = mesh.devices.reshape(nx // GROUP, 4, 2, 2, ny // 2)
    mesh = jax.sharding.Mesh(devices, GX + GY)
    in_specs = (P(None, GX, GY, None), P(GX, GY, None), P(None, GX, GY, None))
    out_specs = (P(None, GX, GY, None), P(None, GX, GY, None))
    return jax.shard_map(local, mesh=mesh, in_specs=in_specs, out_specs=out_specs, check_vma=False)
```

```python
import functools
import math

import jax
import jax.numpy as jnp
import numpy as np
from jax import lax
from jax.experimental import pallas as pl
from jax.experimental.pallas import tpu as pltpu
from jax.sharding import PartitionSpec as P

NZ = 128
STEPS = 4
SZ = 32
LX = 4
LY = 8
VELOCITY = [
    [0, 0, 0],
    [1, 0, 0],
    [-1, 0, 0],
    [0, 1, 0],
    [0, -1, 0],
    [0, 0, 1],
    [0, 0, -1],
    [1, 1, 0],
    [-1, -1, 0],
    [1, -1, 0],
    [-1, 1, 0],
    [1, 0, 1],
    [-1, 0, -1],
    [1, 0, -1],
    [-1, 0, 1],
    [0, 1, 1],
    [0, -1, -1],
    [0, 1, -1],
    [0, -1, 1],
]
OPPOSITE = [0, 2, 1, 4, 3, 6, 5, 8, 7, 10, 9, 12, 11, 14, 13, 16, 15, 18, 17]
WEIGHTS = [1.0 / 3.0] + [1.0 / 18.0] * 6 + [1.0 / 36.0] * 12
PAIRS = [(0, 0), (1, 1), (2, 2), (0, 1), (0, 2), (1, 2)]
COMPONENT = [[0, 3, 4], [3, 1, 5], [4, 5, 2]]
SLOW_VISCOSITY = 0.0004
PHASES = [math.cos(2.0 * math.pi * (step + 0.5) / STEPS) for step in range(STEPS)]

CHANNELS = 23
CX = [v[0] for v in VELOCITY] + [0] * 4
CY = [v[1] for v in VELOCITY] + [0] * 4
HIGHEST = lax.Precision.HIGHEST
GX = ("cy", "zl", "core")
GY = ("zh", "cx")
GROUP = 8


REACH_X = STEPS - 2
REACH_Y = STEPS - 1


def pack_y(sign):
    out, at = [], 0
    for x in range(LX):
        for ch in range(CHANNELS):
            n = REACH_Y + sign * CY[ch]
            out.append((ch, x, LY - n if sign > 0 else 0, n, at))
            at += n
    return out, -(-at // 8) * 8


def pack_x(sign):
    out, at = [], 0
    for ch in range(CHANNELS):
        n = REACH_X + sign * CX[ch]
        for x in range(LX - n, LX) if sign > 0 else range(n):
            out.append((ch, x, REACH_Y + CY[ch], REACH_Y - CY[ch], at))
            at += 2 * REACH_Y + LY
    return out, -(-at // 8) * 8


SPAN = 2 * REACH_Y + LY
Y_UP, Y_ROWS = pack_y(1)
Y_DOWN, _ = pack_y(-1)
X_RIGHT, X_ROWS = pack_x(1)
X_LEFT, _ = pack_x(-1)
Y_UP_AT = {(ch, x): (n, at) for ch, x, _, n, at in Y_UP}
Y_DOWN_AT = {(ch, x): (n, at) for ch, x, _, n, at in Y_DOWN}
X_RIGHT_AT = {(ch, x): at for ch, x, _, _, at in X_RIGHT}
X_LEFT_AT = {(ch, x): at for ch, x, _, _, at in X_LEFT}
RIGHT = [i for i in range(19) if CX[i] == 1]
LEFT = [i for i in range(19) if CX[i] == -1]
EDGE_ROWS = len(RIGHT) * LY


def collide(f, label, drive, phase):
    rho = f[0]
    for i in range(1, 19):
        rho = rho + f[i]
    j = []
    for axis in range(3):
        total = None
        for i in range(1, 19, 2):
            c = VELOCITY[i][axis]
            if c == 0:
                continue
            term = f[i] - f[i + 1] if c > 0 else f[i + 1] - f[i]
            total = term if total is None else total + term
        j.append(total)
    second = label == 1.0
    solid = label == 2.0
    omega = jnp.where(second, 1.1, 1.6)
    keep = 1.0 - omega
    strength = jnp.where(second, 0.6 * phase, phase)
    inverse = 1.0 / rho
    mix = [omega * j[axis] + strength * drive[axis] for axis in range(3)]
    base = omega * (rho - 1.5 * (j[0] * j[0] + j[1] * j[1] + j[2] * j[2]) * inverse)
    curve = 4.5 * omega * inverse

    def along(vector, c):
        total = None
        for axis in range(3):
            if c[axis] == 0:
                continue
            if total is None:
                total = vector[axis] if c[axis] > 0 else -vector[axis]
            else:
                total = total + vector[axis] if c[axis] > 0 else total - vector[axis]
        return total

    post = [None] * 19
    post[0] = jnp.where(solid, f[0], keep * f[0] + WEIGHTS[0] * base)
    for i in range(1, 19, 2):
        w = WEIGHTS[i]
        cj = along(j, VELOCITY[i])
        even = w * (base + curve * (cj * cj))
        odd = (3.0 * w) * along(mix, VELOCITY[i])
        post[i] = jnp.where(solid, f[i + 1], keep * f[i] + (even + odd))
        post[i + 1] = jnp.where(solid, f[i], keep * f[i + 1] + (even - odd))
    fluid = jnp.where(solid, 0.0, inverse)
    stress = [j[a] * j[b] * fluid for a, b in PAIRS]
    return post, stress


def first_kernel(pops_in, label_in, drive_in, cells, total, far, near, box, pops, label, drive, sems):
    copies = [
        pltpu.make_async_copy(source, target, sems.at[k])
        for k, (source, target) in enumerate(((pops_in, pops), (label_in, label), (drive_in, drive)))
    ]
    for copy in copies:
        copy.start()
    for copy in copies:
        copy.wait()
    up = lax.rem(lax.axis_index(GY), 2)
    down = 1 - up
    sums = [jnp.zeros((LY, NZ), jnp.float32)] * 6
    for x in range(LX):
        f = [pops[i, x] for i in range(19)]
        lab = label[x].astype(jnp.float32)
        force = [drive[axis, x] for axis in range(3)]
        post, stress = collide(f, lab, force, PHASES[0])
        for i in range(19):
            cells[i, x] = post[i]
        cells[19, x] = lab
        for axis in range(3):
            cells[20 + axis, x] = force[axis]
        sums = [sums[k] + stress[k] for k in range(6)]
    for k in range(6):
        total[k] = sums[k]
    for ch, x, row, n, at in Y_UP:
        box[up, at : at + n, :] = cells[ch, x, row : row + n, :]
    for ch, x, row, n, at in Y_DOWN:
        box[down, at : at + n, :] = cells[ch, x, row : row + n, :]
    near[...] = box[0]
    far[...] = box[1]


def second_kernel(cells, got_far, got_near, far, near, rows, box):
    odd_y = lax.rem(lax.axis_index(GY), 2)
    low_slot, high_slot = 1 - odd_y, odd_y
    right = lax.rem(lax.axis_index(GX), 2)
    rows[0] = got_near[...]
    rows[1] = got_far[...]
    for slot, entries in ((right, X_RIGHT), (1 - right, X_LEFT)):
        for ch, x, low, high, at in entries:
            n, source = Y_UP_AT[ch, x]
            box[slot, at : at + n, :] = rows[low_slot, source : source + n, :]
            box[slot, at + low : at + low + LY, :] = cells[ch, x]
            n, source = Y_DOWN_AT[ch, x]
            box[slot, at + low + LY : at + low + LY + n, :] = rows[high_slot, source : source + n, :]
    near[...] = box[0]
    far[...] = box[1]


PACK = 16
ROW0 = 8
WORK_ROWS = 24


def own_kernel(cells, got_far, got_near, packs, rows):
    odd_y = lax.rem(lax.axis_index(GY), 2)
    rows[0] = got_near[...]
    rows[1] = got_far[...]
    for ch in range(CHANNELS):
        for x in range(LX):
            low, source = Y_UP_AT[ch, x]
            packs[ch, x, 0:low, :] = rows[1 - odd_y, source : source + low, :]
            packs[ch, x, low : low + LY, :] = cells[ch, x]
            high, source = Y_DOWN_AT[ch, x]
            packs[ch, x, low + LY : low + LY + high, :] = rows[odd_y, source : source + high, :]


def spin(value, i):
    cz = VELOCITY[i][2]
    return pltpu.roll(value, cz % NZ, 1) if cz else value


def arrive(source, x, row, n):
    return [
        spin(source[i, x - CX[i], row - CY[i] : row - CY[i] + n, :], i) for i in range(19)
    ]


def third_kernel(
    cells, total, packs, x_far, x_near, post3, spread, edge_far, edge_near, cols, one, two, sums, box
):
    odd_x = lax.rem(lax.axis_index(GX), 2)
    left_slot, right_slot = 1 - odd_x, odd_x
    cols[0] = x_near[...]
    cols[1] = x_far[...]

    def packed(ch, x):
        if x < 0:
            at = X_RIGHT_AT[ch, x + LX]
            return cols[left_slot, at : at + SPAN, :]
        if x >= LX:
            at = X_LEFT_AT[ch, x - LX]
            return cols[right_slot, at : at + SPAN, :]
        return packs[ch, x, 0:SPAN, :]

    def add(first, second):
        return second if first is None else [a + b for a, b in zip(first, second)]

    last = [total[k] for k in range(6)]
    for step, source, target in ((1, None, one), (2, one, two), (3, two, post3)):
        near, wide = REACH_X + 1 - step, REACH_Y + 1 - step
        n = LY + 2 * wide
        to = 0 if step == 3 else ROW0 - wide
        kept = None
        for x in range(-near, LX + near):
            if step == 1:
                f = [spin(packed(i, x - CX[i]), i) for i in range(19)]
            else:
                f = arrive(source, x + near + 1, ROW0 - wide, n)
            at = REACH_Y - wide
            lab, *force = [packed(ch, x)[at : at + n] for ch in range(19, CHANNELS)]
            post, stress = collide(f, lab, force, PHASES[step])
            for i in range(19):
                target[i, x + near, to : to + n, :] = post[i]
            if 0 <= x < LX:
                kept = add(kept, stress)
        for k in range(6):
            sums[6 * step - 6 + k, 0:n, :] = kept[k]
        last = [last[k] + sums[6 * step - 6 + k, wide : wide + LY, :] for k in range(6)]
    stacked = jnp.concatenate(last, axis=0)
    r = lax.broadcasted_iota(jnp.int32, (16, 48), 0)
    c = lax.broadcasted_iota(jnp.int32, (16, 48), 1)
    chosen = jnp.logical_and((r & 7) == (c >> 3), (r >> 3) == ((c & 7) >> 2))
    left = jnp.where(chosen, 1.0, 0.0)
    halves = jnp.dot(left, stacked, precision=HIGHEST, preferred_element_type=jnp.float32)
    z = lax.broadcasted_iota(jnp.int32, (2 * NZ, NZ), 0)
    lane = lax.broadcasted_iota(jnp.int32, (2 * NZ, NZ), 1)
    table = jnp.where(lane == z >> 2, 1.0 / (STEPS * 64), 0.0)
    slow = jnp.dot(
        jnp.concatenate([halves[0:8], halves[8:16]], axis=1),
        table,
        precision=HIGHEST,
        preferred_element_type=jnp.float32,
    )
    for d in range(spread.shape[0]):
        spread[d] = slow
    for slot, comps, x in ((odd_x, RIGHT, LX - 1), (1 - odd_x, LEFT, 0)):
        for k, i in enumerate(comps):
            box[slot, k * LY : k * LY + LY, :] = post3[i, x, 1 - CY[i] : 1 - CY[i] + LY, :]
    edge_near[...] = box[0]
    edge_far[...] = box[1]


def momentum_kernel(post3, x_far, x_near, out, cols):
    odd_x = lax.rem(lax.axis_index(GX), 2)
    cols[0] = x_near[...]
    cols[1] = x_far[...]
    for x in range(LX):
        f = [None]
        for i in range(1, 19):
            source = x - CX[i]
            if source < 0:
                at = RIGHT.index(i) * LY
                value = cols[1 - odd_x, at : at + LY, :]
            elif source >= LX:
                at = LEFT.index(i) * LY
                value = cols[odd_x, at : at + LY, :]
            else:
                value = post3[i, source, 1 - CY[i] : 1 - CY[i] + LY, :]
            f.append(spin(value, i))
        for axis in range(3):
            total = None
            for i in range(1, 19, 2):
                c = VELOCITY[i][axis]
                if c == 0:
                    continue
                term = f[i] - f[i + 1] if c > 0 else f[i + 1] - f[i]
                total = term if total is None else total + term
            out[axis, x] = total


TILES = 3


@functools.cache
def operator_table(sx, sy):
    waves = [2.0 * math.pi * np.fft.fftfreq(n) for n in (sx, sy, SZ)]
    k = np.meshgrid(*waves, indexing="ij")
    square = k[0] ** 2 + k[1] ** 2 + k[2] ** 2
    positive = square > 0
    safe = np.where(positive, square, 1.0)
    half = SZ // 2 + 1
    modes = sy * half
    lanes = TILES * NZ
    ky = np.repeat(np.arange(sy), half)
    kz = np.tile(np.arange(half), sy)
    weight = np.where((kz == 0) | (kz == SZ // 2), 1.0, 2.0) / (sy * SZ)
    gains = np.zeros((3, 6, sx, lanes))
    twists = np.zeros((3, 8, lanes))
    imaginary = []
    for a in range(3):
        for c in range(6):
            force = [
                -1j * sum(k[b] for b in range(3) if COMPONENT[first][b] == c) + 0.0 * k[0]
                for first in range(3)
            ]
            inner = k[0] * force[0] + k[1] * force[1] + k[2] * force[2]
            gain = np.where(positive, (force[a] - k[a] * inner / safe) / (SLOW_VISCOSITY * safe), 0.0)
            flipped = gain
            for axis in range(3):
                flipped = np.roll(np.flip(flipped, axis), 1, axis)
            gain = 0.5 * (gain + np.conj(flipped))
            line = weight * np.fft.ifft(gain, axis=0)[:, :, :half].reshape(sx, modes)
            odd_x = (int(a == 0) + sum(int(d == 0) for d in PAIRS[c])) % 2
            imaginary.append(not odd_x)
            gains[a, c, :, :modes] = line.real if odd_x else line.imag
            if odd_x:
                twists[a, c, :modes] = line.imag[0]
    gains = gains.reshape(3, 6, sx // GROUP, GROUP, TILES, NZ).transpose(0, 1, 4, 3, 2, 5)
    gains = np.concatenate([gains[:, :, :, :, -1:], gains], axis=4)
    twists = twists.reshape(3, 8, TILES, NZ).transpose(0, 2, 1, 3)
    y = np.repeat(np.arange(2), SZ)
    z = np.tile(np.arange(SZ), 2)
    angle = 2.0 * math.pi * (np.outer(y, ky) / sy + np.outer(z, kz) / SZ)
    forward = np.zeros((2, NZ, lanes))
    forward[0, :64, :modes] = np.cos(angle)
    forward[1, :64, :modes] = -np.sin(angle)
    forward = forward.reshape(2, NZ, TILES, NZ).transpose(0, 2, 1, 3)
    shift = 2.0 * math.pi * np.outer(2 * np.arange(sy // 2), ky) / sy
    turns = np.zeros((sy // 2, 2, lanes))
    turns[:, 0, :modes] = np.cos(shift)
    turns[:, 1, :modes] = np.sin(shift)
    turns = np.concatenate([turns.reshape(-1, NZ), np.zeros((-turns.size // NZ % 8, NZ))])
    sections = [gains.reshape(-1, NZ), twists.reshape(-1, NZ), turns, forward.reshape(-1, NZ)]
    starts = np.cumsum([0] + [len(section) for section in sections])
    table = np.concatenate(sections).astype(np.float32)
    return table, tuple(int(start) for start in starts[:4]), tuple(imaginary)


def solve_kernel(starts, imaginary, pairs, groups, blocks, table, out, part, hat, field):
    at_gain, at_twist, at_turn, at_forward = starts
    me = lax.axis_index("cy")
    mine = lax.rem(lax.axis_index(GX), GROUP)
    upper = lax.axis_index("zh")
    column = lax.axis_index("cx")
    columns = pairs // 2
    forward = jnp.concatenate(
        [table[at_forward + k * NZ : at_forward + (k + 1) * NZ, :] for k in range(2 * TILES)], axis=1
    )
    part[...] = jnp.dot(
        blocks[...].reshape(2 * GROUP * 8, NZ),
        forward,
        precision=HIGHEST,
        preferred_element_type=jnp.float32,
    ).reshape(2 * GROUP, 8, 2 * TILES * NZ)
    half = [table[at_turn + columns * (2 * TILES) + k : at_turn + columns * (2 * TILES) + k + 1, :] for k in range(TILES)]
    half = jnp.concatenate(half + half, axis=1)
    for r in range(GROUP):
        hat[r] = part[2 * r + upper] + half * part[2 * r + 1 - upper]

    sign = (1 - 2 * lax.rem(mine, 2)).astype(jnp.float32)
    for k in range(TILES):
        re_lanes = slice(k * NZ, (k + 1) * NZ)
        im_lanes = slice((TILES + k) * NZ, (TILES + k + 1) * NZ)
        all_re = hat[0, :, re_lanes]
        all_im = hat[0, :, im_lanes]
        for r in range(1, GROUP):
            all_re = all_re + hat[r, :, re_lanes] if r % 2 == 0 else all_re - hat[r, :, re_lanes]
            all_im = all_im + hat[r, :, im_lanes] if r % 2 == 0 else all_im - hat[r, :, im_lanes]
        re, im = [], []
        for a in range(3):
            at = at_twist + (a * TILES + k) * 8
            wave = sign * table[at : at + 8, :]
            first_re = -jnp.sum(wave * all_im, axis=0, keepdims=True)
            first_im = jnp.sum(wave * all_re, axis=0, keepdims=True)
            re.append(jnp.broadcast_to(first_re, (groups, NZ)))
            im.append(jnp.broadcast_to(first_im, (groups, NZ)))
        for r in range(GROUP):
            apart = mine + GROUP - r
            ahead = apart // GROUP
            row = (apart - GROUP * ahead) * (groups + 1) + ahead
            for c in range(6):
                hat_re = jnp.broadcast_to(hat[r, c : c + 1, re_lanes], (groups, NZ))
                hat_im = jnp.broadcast_to(hat[r, c : c + 1, im_lanes], (groups, NZ))
                for a in range(3):
                    at = at_gain + ((a * 6 + c) * TILES + k) * (GROUP * (groups + 1))
                    gain = table[pl.ds(at + row, groups), :]
                    if imaginary[a * 6 + c]:
                        re[a] = re[a] - gain * hat_im
                        im[a] = im[a] + gain * hat_re
                    else:
                        re[a] = re[a] + gain * hat_re
                        im[a] = im[a] + gain * hat_im
        for j in range(columns):
            d = lax.rem(pairs + j - column, pairs)
            cosine = table[pl.ds(at_turn + k + d * (2 * TILES), 1), :]
            sine = table[pl.ds(at_turn + TILES + k + d * (2 * TILES), 1), :]
            for a in range(3):
                at = (a * columns + j) * groups
                field[at : at + groups, re_lanes] = re[a] * cosine - im[a] * sine
                field[at : at + groups, im_lanes] = re[a] * sine + im[a] * cosine
    result = lax.dot_general(
        field[...],
        forward,
        (((1,), (1,)), ((), ())),
        precision=HIGHEST,
        preferred_element_type=jnp.float32,
    )
    for j in range(columns):
        first, second, third = [
            result[(a * columns + j) * groups : (a * columns + j + 1) * groups] for a in range(3)
        ]
        both = first + pltpu.roll(second, 64, 1)
        for q in range(groups):
            target = lax.rem(me + q, groups) * columns + j
            out[target, 0:1, :] = both[q : q + 1]
            out[target, 1:2, :] = third[q : q + 1]


def last_kernel(parts, out):
    total = jnp.sum(parts[...], axis=0)
    for a in range(3):
        row = total[a // 2 : a // 2 + 1, :]
        for y in range(2):
            lane = (a % 2) * 64 + y * SZ
            value = pltpu.roll(row, (NZ - lane) % NZ, 1) if lane else row
            out[a, 0, y : y + 1, :] = value[:, :SZ]


def call(body, outs, scratch, cost, limit=16, place=pltpu.VMEM, more=()):
    shapes = [jax.ShapeDtypeStruct(s, jnp.float32) for s in outs]
    spec = pl.BlockSpec(memory_space=pltpu.VMEM)

    def run(*args):
        return pl.pallas_call(
            body,
            out_shape=shapes,
            in_specs=[pl.BlockSpec(memory_space=place)] * len(args),
            out_specs=[spec] * len(shapes),
            scratch_shapes=[pltpu.VMEM(s, jnp.float32) for s in scratch] + list(more),
            compiler_params=pltpu.CompilerParams(vmem_limit_bytes=limit << 20),
            cost_estimate=pl.CostEstimate(flops=cost, bytes_accessed=cost, transcendentals=0),
        )(*args)

    return run


def swap(far, near, axis):
    count = lax.axis_size(axis)
    near_pairs = [(i, i ^ 1) for i in range(count)]
    far_pairs = [(i, (i + 1) % count if i % 2 else (i - 1) % count) for i in range(count)]
    return lax.ppermute(far, axis, far_pairs), lax.ppermute(near, axis, near_pairs)


def local(pops, label, drive):
    nx = lax.axis_size(GX)
    ny = lax.axis_size(GY)
    groups = lax.axis_size("cy")
    cells, total, far, near = call(
        first_kernel,
        [(CHANNELS, LX, LY, NZ), (6, LY, NZ), (Y_ROWS, NZ), (Y_ROWS, NZ)],
        [(2, Y_ROWS, NZ), pops.shape],
        2_000_000,
        place=pltpu.HBM,
        more=[
            pltpu.VMEM(label.shape, jnp.int32),
            pltpu.VMEM(drive.shape, jnp.float32),
            pltpu.SemaphoreType.DMA((3,)),
        ],
    )(*[pltpu.with_memory_space_constraint(value, pltpu.HBM) for value in (pops, label, drive)])
    y_far, y_near = swap(far, near, GY)
    far, near = call(
        second_kernel,
        [(X_ROWS, NZ), (X_ROWS, NZ)],
        [(2, Y_ROWS, NZ), (2, X_ROWS, NZ)],
        2_000_000,
    )(cells, y_far, y_near)
    x_far, x_near = swap(far, near, GX)
    (packs,) = call(
        own_kernel, [(CHANNELS, LX, PACK, NZ)], [(2, Y_ROWS, NZ)], 2_000_000
    )(cells, y_far, y_near)
    post3, spread, far, near = call(
        third_kernel,
        [(19, LX, PACK, NZ), (2 * GROUP, 8, NZ), (EDGE_ROWS, NZ), (EDGE_ROWS, NZ)],
        [
            (2, X_ROWS, NZ),
            (19, LX + 2 * REACH_X, WORK_ROWS, NZ),
            (19, LX + 2 * REACH_X - 2, WORK_ROWS, NZ),
            (18, 16, NZ),
            (2, EDGE_ROWS, NZ),
        ],
        20_000_000,
    )(cells, total, packs, x_far, x_near)
    blocks = lax.all_to_all(spread, ("zl", "core", "zh"), 0, 0, tiled=False)
    edge_far, edge_near = swap(far, near, GX)
    (momentum,) = call(
        momentum_kernel, [(3, LX, LY, NZ)], [(2, EDGE_ROWS, NZ)], 1_000_000
    )(post3, edge_far, edge_near)
    table, starts, imaginary = operator_table(nx, 2 * ny)
    (parts,) = call(
        functools.partial(solve_kernel, starts, imaginary, ny, groups),
        [(groups * ny // 2, 2, NZ)],
        [
            (2 * GROUP, 8, 2 * TILES * NZ),
            (GROUP, 8, 2 * TILES * NZ),
            (3 * groups * ny // 2, 2 * TILES * NZ),
        ],
        10_000_000,
    )(blocks, table)
    parts = lax.all_to_all(parts, ("cy", "cx"), 0, 0, tiled=False)
    parts, momentum = lax.optimization_barrier((parts, momentum))
    (running,) = call(last_kernel, [(3, 1, 2, SZ)], [], 100_000)(parts)
    return momentum, running


def solution(mesh):
    nx, ny = mesh.devices.shape
    devices = mesh.devices.reshape(nx // GROUP, 4, 2, 2, ny // 2)
    mesh = jax.sharding.Mesh(devices, GX + GY)
    in_specs = (P(None, GX, GY, None), P(GX, GY, None), P(None, GX, GY, None))
    out_specs = (P(None, GX, GY, None), P(None, GX, GY, None))
    return jax.shard_map(local, mesh=mesh, in_specs=in_specs, out_specs=out_specs, check_vma=False)
```

```python
import functools
import math

import jax
import jax.numpy as jnp
import numpy as np
from jax import lax
from jax.experimental import pallas as pl
from jax.experimental.pallas import tpu as pltpu
from jax.sharding import PartitionSpec as P

NZ = 128
STEPS = 4
SZ = 32
LX = 4
LY = 8
VELOCITY = [
    [0, 0, 0],
    [1, 0, 0],
    [-1, 0, 0],
    [0, 1, 0],
    [0, -1, 0],
    [0, 0, 1],
    [0, 0, -1],
    [1, 1, 0],
    [-1, -1, 0],
    [1, -1, 0],
    [-1, 1, 0],
    [1, 0, 1],
    [-1, 0, -1],
    [1, 0, -1],
    [-1, 0, 1],
    [0, 1, 1],
    [0, -1, -1],
    [0, 1, -1],
    [0, -1, 1],
]
OPPOSITE = [0, 2, 1, 4, 3, 6, 5, 8, 7, 10, 9, 12, 11, 14, 13, 16, 15, 18, 17]
WEIGHTS = [1.0 / 3.0] + [1.0 / 18.0] * 6 + [1.0 / 36.0] * 12
PAIRS = [(0, 0), (1, 1), (2, 2), (0, 1), (0, 2), (1, 2)]
COMPONENT = [[0, 3, 4], [3, 1, 5], [4, 5, 2]]
SLOW_VISCOSITY = 0.0004
PHASES = [math.cos(2.0 * math.pi * (step + 0.5) / STEPS) for step in range(STEPS)]

CHANNELS = 23
CX = [v[0] for v in VELOCITY] + [0] * 4
CY = [v[1] for v in VELOCITY] + [0] * 4
HIGHEST = lax.Precision.HIGHEST
GX = ("cy", "zl", "core")
GY = ("zh", "cx")
GROUP = 8


REACH_X = STEPS - 1
REACH_Y = STEPS - 1


def pack_y(sign):
    out, at = [], 0
    for x in range(LX):
        for ch in range(CHANNELS):
            n = REACH_Y + sign * CY[ch]
            out.append((ch, x, LY - n if sign > 0 else 0, n, at))
            at += n
    return out, -(-at // 8) * 8


def pack_x(sign):
    out, at = [], 0
    for ch in range(CHANNELS):
        n = REACH_X + sign * CX[ch]
        for x in range(LX - n, LX) if sign > 0 else range(n):
            out.append((ch, x, REACH_Y + CY[ch], REACH_Y - CY[ch], at))
            at += 2 * REACH_Y + LY
    return out, -(-at // 8) * 8


SPAN = 2 * REACH_Y + LY
Y_UP, Y_ROWS = pack_y(1)
Y_DOWN, _ = pack_y(-1)
X_RIGHT, X_ROWS = pack_x(1)
X_LEFT, _ = pack_x(-1)
Y_UP_AT = {(ch, x): (n, at) for ch, x, _, n, at in Y_UP}
Y_DOWN_AT = {(ch, x): (n, at) for ch, x, _, n, at in Y_DOWN}
X_RIGHT_AT = {(ch, x): at for ch, x, _, _, at in X_RIGHT}
X_LEFT_AT = {(ch, x): at for ch, x, _, _, at in X_LEFT}


def collide(f, label, drive, phase):
    rho = f[0]
    for i in range(1, 19):
        rho = rho + f[i]
    j = []
    for axis in range(3):
        total = None
        for i in range(1, 19, 2):
            c = VELOCITY[i][axis]
            if c == 0:
                continue
            term = f[i] - f[i + 1] if c > 0 else f[i + 1] - f[i]
            total = term if total is None else total + term
        j.append(total)
    second = label == 1.0
    solid = label == 2.0
    omega = jnp.where(second, 1.1, 1.6)
    keep = 1.0 - omega
    strength = jnp.where(second, 0.6 * phase, phase)
    inverse = 1.0 / rho
    mix = [omega * j[axis] + strength * drive[axis] for axis in range(3)]
    base = omega * (rho - 1.5 * (j[0] * j[0] + j[1] * j[1] + j[2] * j[2]) * inverse)
    curve = 4.5 * omega * inverse

    def along(vector, c):
        total = None
        for axis in range(3):
            if c[axis] == 0:
                continue
            if total is None:
                total = vector[axis] if c[axis] > 0 else -vector[axis]
            else:
                total = total + vector[axis] if c[axis] > 0 else total - vector[axis]
        return total

    post = [None] * 19
    post[0] = jnp.where(solid, f[0], keep * f[0] + WEIGHTS[0] * base)
    for i in range(1, 19, 2):
        w = WEIGHTS[i]
        cj = along(j, VELOCITY[i])
        even = w * (base + curve * (cj * cj))
        odd = (3.0 * w) * along(mix, VELOCITY[i])
        post[i] = jnp.where(solid, f[i + 1], keep * f[i] + (even + odd))
        post[i + 1] = jnp.where(solid, f[i], keep * f[i + 1] + (even - odd))
    fluid = jnp.where(solid, 0.0, inverse)
    stress = [j[a] * j[b] * fluid for a, b in PAIRS]
    return post, stress


def first_kernel(pops_in, label_in, drive_in, cells, total, far, near, box, pops, label, drive, sems):
    copies = [
        pltpu.make_async_copy(source, target, sems.at[k])
        for k, (source, target) in enumerate(((pops_in, pops), (label_in, label), (drive_in, drive)))
    ]
    for copy in copies:
        copy.start()
    for copy in copies:
        copy.wait()
    up = lax.rem(lax.axis_index(GY), 2)
    down = 1 - up
    sums = [jnp.zeros((LY, NZ), jnp.float32)] * 6
    for x in range(LX):
        f = [pops[i, x] for i in range(19)]
        lab = label[x].astype(jnp.float32)
        force = [drive[axis, x] for axis in range(3)]
        post, stress = collide(f, lab, force, PHASES[0])
        for i in range(19):
            cells[i, x] = post[i]
        cells[19, x] = lab
        for axis in range(3):
            cells[20 + axis, x] = force[axis]
        sums = [sums[k] + stress[k] for k in range(6)]
    for k in range(6):
        total[k] = sums[k]
    for ch, x, row, n, at in Y_UP:
        box[up, at : at + n, :] = cells[ch, x, row : row + n, :]
    for ch, x, row, n, at in Y_DOWN:
        box[down, at : at + n, :] = cells[ch, x, row : row + n, :]
    near[...] = box[0]
    far[...] = box[1]


def second_kernel(cells, got_far, got_near, far, near, rows, box):
    odd_y = lax.rem(lax.axis_index(GY), 2)
    low_slot, high_slot = 1 - odd_y, odd_y
    right = lax.rem(lax.axis_index(GX), 2)
    rows[0] = got_near[...]
    rows[1] = got_far[...]
    for slot, entries in ((right, X_RIGHT), (1 - right, X_LEFT)):
        for ch, x, low, high, at in entries:
            n, source = Y_UP_AT[ch, x]
            box[slot, at : at + n, :] = rows[low_slot, source : source + n, :]
            box[slot, at + low : at + low + LY, :] = cells[ch, x]
            n, source = Y_DOWN_AT[ch, x]
            box[slot, at + low + LY : at + low + LY + n, :] = rows[high_slot, source : source + n, :]
    near[...] = box[0]
    far[...] = box[1]


PACK = 16
ROW0 = 8
WORK_ROWS = 24


def own_kernel(cells, got_far, got_near, packs, rows):
    odd_y = lax.rem(lax.axis_index(GY), 2)
    rows[0] = got_near[...]
    rows[1] = got_far[...]
    for ch in range(CHANNELS):
        for x in range(LX):
            low, source = Y_UP_AT[ch, x]
            packs[ch, x, 0:low, :] = rows[1 - odd_y, source : source + low, :]
            packs[ch, x, low : low + LY, :] = cells[ch, x]
            high, source = Y_DOWN_AT[ch, x]
            packs[ch, x, low + LY : low + LY + high, :] = rows[odd_y, source : source + high, :]


def spin(value, i):
    cz = VELOCITY[i][2]
    return pltpu.roll(value, cz % NZ, 1) if cz else value


def arrive(source, x, row, n):
    return [
        spin(source[i, x - CX[i], row - CY[i] : row - CY[i] + n, :], i) for i in range(19)
    ]


def third_kernel(
    cells, total, packs, x_far, x_near, post3, spread, cols, one, two, sums
):
    odd_x = lax.rem(lax.axis_index(GX), 2)
    left_slot, right_slot = 1 - odd_x, odd_x
    cols[0] = x_near[...]
    cols[1] = x_far[...]

    def packed(ch, x):
        if x < 0:
            at = X_RIGHT_AT[ch, x + LX]
            return cols[left_slot, at : at + SPAN, :]
        if x >= LX:
            at = X_LEFT_AT[ch, x - LX]
            return cols[right_slot, at : at + SPAN, :]
        return packs[ch, x, 0:SPAN, :]

    def add(first, second):
        return second if first is None else [a + b for a, b in zip(first, second)]

    last = [total[k] for k in range(6)]
    for step, source, target in ((1, None, one), (2, one, two), (3, two, post3)):
        near, wide = REACH_X + 1 - step, REACH_Y + 1 - step
        n = LY + 2 * wide
        to = 0 if step == 3 else ROW0 - wide
        kept = None
        for x in range(-near, LX + near):
            if step == 1:
                f = [spin(packed(i, x - CX[i]), i) for i in range(19)]
            else:
                f = arrive(source, x + near + 1, ROW0 - wide, n)
            at = REACH_Y - wide
            lab, *force = [packed(ch, x)[at : at + n] for ch in range(19, CHANNELS)]
            post, stress = collide(f, lab, force, PHASES[step])
            for i in range(19):
                target[i, x + near, to : to + n, :] = post[i]
            if 0 <= x < LX:
                kept = add(kept, stress)
        for k in range(6):
            sums[6 * step - 6 + k, 0:n, :] = kept[k]
        last = [last[k] + sums[6 * step - 6 + k, wide : wide + LY, :] for k in range(6)]
    stacked = jnp.concatenate(last, axis=0)
    r = lax.broadcasted_iota(jnp.int32, (16, 48), 0)
    c = lax.broadcasted_iota(jnp.int32, (16, 48), 1)
    chosen = jnp.logical_and((r & 7) == (c >> 3), (r >> 3) == ((c & 7) >> 2))
    left = jnp.where(chosen, 1.0, 0.0)
    halves = jnp.dot(left, stacked, precision=HIGHEST, preferred_element_type=jnp.float32)
    z = lax.broadcasted_iota(jnp.int32, (2 * NZ, NZ), 0)
    lane = lax.broadcasted_iota(jnp.int32, (2 * NZ, NZ), 1)
    table = jnp.where(lane == z >> 2, 1.0 / (STEPS * 64), 0.0)
    slow = jnp.dot(
        jnp.concatenate([halves[0:8], halves[8:16]], axis=1),
        table,
        precision=HIGHEST,
        preferred_element_type=jnp.float32,
    )
    for d in range(spread.shape[0]):
        spread[d] = slow


def momentum_of(post3, out):
    for x in range(LX):
        f = [None] + [
            spin(post3[i, x + 1 - CX[i], 1 - CY[i] : 1 - CY[i] + LY, :], i) for i in range(1, 19)
        ]
        for axis in range(3):
            total = None
            for i in range(1, 19, 2):
                c = VELOCITY[i][axis]
                if c == 0:
                    continue
                term = f[i] - f[i + 1] if c > 0 else f[i + 1] - f[i]
                total = term if total is None else total + term
            out[axis, x] = total


TILES = 3


@functools.cache
def operator_table(sx, sy):
    waves = [2.0 * math.pi * np.fft.fftfreq(n) for n in (sx, sy, SZ)]
    k = np.meshgrid(*waves, indexing="ij")
    square = k[0] ** 2 + k[1] ** 2 + k[2] ** 2
    positive = square > 0
    safe = np.where(positive, square, 1.0)
    half = SZ // 2 + 1
    modes = sy * half
    lanes = TILES * NZ
    ky = np.repeat(np.arange(sy), half)
    kz = np.tile(np.arange(half), sy)
    weight = np.where((kz == 0) | (kz == SZ // 2), 1.0, 2.0) / (sy * SZ)
    gains = np.zeros((3, 6, sx, lanes))
    twists = np.zeros((3, 8, lanes))
    imaginary = []
    for a in range(3):
        for c in range(6):
            force = [
                -1j * sum(k[b] for b in range(3) if COMPONENT[first][b] == c) + 0.0 * k[0]
                for first in range(3)
            ]
            inner = k[0] * force[0] + k[1] * force[1] + k[2] * force[2]
            gain = np.where(positive, (force[a] - k[a] * inner / safe) / (SLOW_VISCOSITY * safe), 0.0)
            flipped = gain
            for axis in range(3):
                flipped = np.roll(np.flip(flipped, axis), 1, axis)
            gain = 0.5 * (gain + np.conj(flipped))
            line = weight * np.fft.ifft(gain, axis=0)[:, :, :half].reshape(sx, modes)
            odd_x = (int(a == 0) + sum(int(d == 0) for d in PAIRS[c])) % 2
            imaginary.append(not odd_x)
            gains[a, c, :, :modes] = line.real if odd_x else line.imag
            if odd_x:
                twists[a, c, :modes] = line.imag[0]
    gains = gains.reshape(3, 6, sx // GROUP, GROUP, TILES, NZ).transpose(0, 1, 4, 3, 2, 5)
    gains = np.concatenate([gains[:, :, :, :, -1:], gains], axis=4)
    twists = twists.reshape(3, 8, TILES, NZ).transpose(0, 2, 1, 3)
    y = np.repeat(np.arange(2), SZ)
    z = np.tile(np.arange(SZ), 2)
    angle = 2.0 * math.pi * (np.outer(y, ky) / sy + np.outer(z, kz) / SZ)
    forward = np.zeros((2, NZ, lanes))
    forward[0, :64, :modes] = np.cos(angle)
    forward[1, :64, :modes] = -np.sin(angle)
    forward = forward.reshape(2, NZ, TILES, NZ).transpose(0, 2, 1, 3)
    shift = 2.0 * math.pi * np.outer(2 * np.arange(sy // 2), ky) / sy
    turns = np.zeros((sy // 2, 2, lanes))
    turns[:, 0, :modes] = np.cos(shift)
    turns[:, 1, :modes] = np.sin(shift)
    turns = np.concatenate([turns.reshape(-1, NZ), np.zeros((-turns.size // NZ % 8, NZ))])
    sections = [gains.reshape(-1, NZ), twists.reshape(-1, NZ), turns, forward.reshape(-1, NZ)]
    starts = np.cumsum([0] + [len(section) for section in sections])
    table = np.concatenate(sections).astype(np.float32)
    return table, tuple(int(start) for start in starts[:4]), tuple(imaginary)


def solve_kernel(
    starts, imaginary, pairs, groups, blocks, table, post3, out, momentum, part, hat, field
):
    momentum_of(post3, momentum)
    at_gain, at_twist, at_turn, at_forward = starts
    me = lax.axis_index("cy")
    mine = lax.rem(lax.axis_index(GX), GROUP)
    upper = lax.axis_index("zh")
    column = lax.axis_index("cx")
    columns = pairs // 2
    forward = jnp.concatenate(
        [table[at_forward + k * NZ : at_forward + (k + 1) * NZ, :] for k in range(2 * TILES)], axis=1
    )
    part[...] = jnp.dot(
        blocks[...].reshape(2 * GROUP * 8, NZ),
        forward,
        precision=HIGHEST,
        preferred_element_type=jnp.float32,
    ).reshape(2 * GROUP, 8, 2 * TILES * NZ)
    half = [table[at_turn + columns * (2 * TILES) + k : at_turn + columns * (2 * TILES) + k + 1, :] for k in range(TILES)]
    half = jnp.concatenate(half + half, axis=1)
    for r in range(GROUP):
        hat[r] = part[2 * r + upper] + half * part[2 * r + 1 - upper]

    sign = (1 - 2 * lax.rem(mine, 2)).astype(jnp.float32)
    for k in range(TILES):
        re_lanes = slice(k * NZ, (k + 1) * NZ)
        im_lanes = slice((TILES + k) * NZ, (TILES + k + 1) * NZ)
        all_re = hat[0, :, re_lanes]
        all_im = hat[0, :, im_lanes]
        for r in range(1, GROUP):
            all_re = all_re + hat[r, :, re_lanes] if r % 2 == 0 else all_re - hat[r, :, re_lanes]
            all_im = all_im + hat[r, :, im_lanes] if r % 2 == 0 else all_im - hat[r, :, im_lanes]
        re, im = [], []
        for a in range(3):
            at = at_twist + (a * TILES + k) * 8
            wave = sign * table[at : at + 8, :]
            first_re = -jnp.sum(wave * all_im, axis=0, keepdims=True)
            first_im = jnp.sum(wave * all_re, axis=0, keepdims=True)
            re.append(jnp.broadcast_to(first_re, (groups, NZ)))
            im.append(jnp.broadcast_to(first_im, (groups, NZ)))
        for r in range(GROUP):
            apart = mine + GROUP - r
            ahead = apart // GROUP
            row = (apart - GROUP * ahead) * (groups + 1) + ahead
            for c in range(6):
                hat_re = jnp.broadcast_to(hat[r, c : c + 1, re_lanes], (groups, NZ))
                hat_im = jnp.broadcast_to(hat[r, c : c + 1, im_lanes], (groups, NZ))
                for a in range(3):
                    at = at_gain + ((a * 6 + c) * TILES + k) * (GROUP * (groups + 1))
                    gain = table[pl.ds(at + row, groups), :]
                    if imaginary[a * 6 + c]:
                        re[a] = re[a] - gain * hat_im
                        im[a] = im[a] + gain * hat_re
                    else:
                        re[a] = re[a] + gain * hat_re
                        im[a] = im[a] + gain * hat_im
        for j in range(columns):
            d = lax.rem(pairs + j - column, pairs)
            cosine = table[pl.ds(at_turn + k + d * (2 * TILES), 1), :]
            sine = table[pl.ds(at_turn + TILES + k + d * (2 * TILES), 1), :]
            for a in range(3):
                at = (a * columns + j) * groups
                field[at : at + groups, re_lanes] = re[a] * cosine - im[a] * sine
                field[at : at + groups, im_lanes] = re[a] * sine + im[a] * cosine
    result = lax.dot_general(
        field[...],
        forward,
        (((1,), (1,)), ((), ())),
        precision=HIGHEST,
        preferred_element_type=jnp.float32,
    )
    for j in range(columns):
        first, second, third = [
            result[(a * columns + j) * groups : (a * columns + j + 1) * groups] for a in range(3)
        ]
        both = first + pltpu.roll(second, 64, 1)
        for q in range(groups):
            target = lax.rem(me + q, groups) * columns + j
            out[target, 0:1, :] = both[q : q + 1]
            out[target, 1:2, :] = third[q : q + 1]


def last_kernel(parts, out):
    total = jnp.sum(parts[...], axis=0)
    for a in range(3):
        row = total[a // 2 : a // 2 + 1, :]
        for y in range(2):
            lane = (a % 2) * 64 + y * SZ
            value = pltpu.roll(row, (NZ - lane) % NZ, 1) if lane else row
            out[a, 0, y : y + 1, :] = value[:, :SZ]


def call(body, outs, scratch, cost, limit=16, place=pltpu.VMEM, more=()):
    shapes = [jax.ShapeDtypeStruct(s, jnp.float32) for s in outs]
    spec = pl.BlockSpec(memory_space=pltpu.VMEM)

    def run(*args):
        return pl.pallas_call(
            body,
            out_shape=shapes,
            in_specs=[pl.BlockSpec(memory_space=place)] * len(args),
            out_specs=[spec] * len(shapes),
            scratch_shapes=[pltpu.VMEM(s, jnp.float32) for s in scratch] + list(more),
            compiler_params=pltpu.CompilerParams(vmem_limit_bytes=limit << 20),
            cost_estimate=pl.CostEstimate(flops=cost, bytes_accessed=cost, transcendentals=0),
        )(*args)

    return run


def swap(far, near, axis):
    count = lax.axis_size(axis)
    near_pairs = [(i, i ^ 1) for i in range(count)]
    far_pairs = [(i, (i + 1) % count if i % 2 else (i - 1) % count) for i in range(count)]
    return lax.ppermute(far, axis, far_pairs), lax.ppermute(near, axis, near_pairs)


def local(pops, label, drive):
    nx = lax.axis_size(GX)
    ny = lax.axis_size(GY)
    groups = lax.axis_size("cy")
    cells, total, far, near = call(
        first_kernel,
        [(CHANNELS, LX, LY, NZ), (6, LY, NZ), (Y_ROWS, NZ), (Y_ROWS, NZ)],
        [(2, Y_ROWS, NZ), pops.shape],
        2_000_000,
        place=pltpu.HBM,
        more=[
            pltpu.VMEM(label.shape, jnp.int32),
            pltpu.VMEM(drive.shape, jnp.float32),
            pltpu.SemaphoreType.DMA((3,)),
        ],
    )(*[pltpu.with_memory_space_constraint(value, pltpu.HBM) for value in (pops, label, drive)])
    y_far, y_near = swap(far, near, GY)
    far, near = call(
        second_kernel,
        [(X_ROWS, NZ), (X_ROWS, NZ)],
        [(2, Y_ROWS, NZ), (2, X_ROWS, NZ)],
        2_000_000,
    )(cells, y_far, y_near)
    x_far, x_near = swap(far, near, GX)
    (packs,) = call(
        own_kernel, [(CHANNELS, LX, PACK, NZ)], [(2, Y_ROWS, NZ)], 2_000_000
    )(cells, y_far, y_near)
    post3, spread = call(
        third_kernel,
        [(19, LX + 2, PACK, NZ), (2 * GROUP, 8, NZ)],
        [
            (2, X_ROWS, NZ),
            (19, LX + 2 * REACH_X, WORK_ROWS, NZ),
            (19, LX + 2 * REACH_X - 2, WORK_ROWS, NZ),
            (18, 16, NZ),
        ],
        20_000_000,
    )(cells, total, packs, x_far, x_near)
    blocks = lax.all_to_all(spread, ("zl", "core", "zh"), 0, 0, tiled=False)
    table, starts, imaginary = operator_table(nx, 2 * ny)
    parts, momentum = call(
        functools.partial(solve_kernel, starts, imaginary, ny, groups),
        [(groups * ny // 2, 2, NZ), (3, LX, LY, NZ)],
        [
            (2 * GROUP, 8, 2 * TILES * NZ),
            (GROUP, 8, 2 * TILES * NZ),
            (3 * groups * ny // 2, 2 * TILES * NZ),
        ],
        10_000_000,
    )(blocks, table, post3)
    parts = lax.all_to_all(parts, ("cy", "cx"), 0, 0, tiled=False)
    (running,) = call(last_kernel, [(3, 1, 2, SZ)], [], 100_000)(parts)
    return momentum, running


def solution(mesh):
    nx, ny = mesh.devices.shape
    devices = mesh.devices.reshape(nx // GROUP, 4, 2, 2, ny // 2)
    mesh = jax.sharding.Mesh(devices, GX + GY)
    in_specs = (P(None, GX, GY, None), P(GX, GY, None), P(None, GX, GY, None))
    out_specs = (P(None, GX, GY, None), P(None, GX, GY, None))
    return jax.shard_map(local, mesh=mesh, in_specs=in_specs, out_specs=out_specs, check_vma=False)
```

```python
import functools
import math

import jax
import jax.numpy as jnp
import numpy as np
from jax import lax
from jax.experimental import pallas as pl
from jax.experimental.pallas import tpu as pltpu
from jax.sharding import PartitionSpec as P

NZ = 128
STEPS = 4
SZ = 32
LX = 4
LY = 8
VELOCITY = [
    [0, 0, 0],
    [1, 0, 0],
    [-1, 0, 0],
    [0, 1, 0],
    [0, -1, 0],
    [0, 0, 1],
    [0, 0, -1],
    [1, 1, 0],
    [-1, -1, 0],
    [1, -1, 0],
    [-1, 1, 0],
    [1, 0, 1],
    [-1, 0, -1],
    [1, 0, -1],
    [-1, 0, 1],
    [0, 1, 1],
    [0, -1, -1],
    [0, 1, -1],
    [0, -1, 1],
]
OPPOSITE = [0, 2, 1, 4, 3, 6, 5, 8, 7, 10, 9, 12, 11, 14, 13, 16, 15, 18, 17]
WEIGHTS = [1.0 / 3.0] + [1.0 / 18.0] * 6 + [1.0 / 36.0] * 12
PAIRS = [(0, 0), (1, 1), (2, 2), (0, 1), (0, 2), (1, 2)]
COMPONENT = [[0, 3, 4], [3, 1, 5], [4, 5, 2]]
SLOW_VISCOSITY = 0.0004
PHASES = [math.cos(2.0 * math.pi * (step + 0.5) / STEPS) for step in range(STEPS)]

CHANNELS = 23
CX = [v[0] for v in VELOCITY] + [0] * 4
CY = [v[1] for v in VELOCITY] + [0] * 4
HIGHEST = lax.Precision.HIGHEST
GX = ("cy", "zl", "core")
GY = ("zh", "cx")
GROUP = 8


REACH_X = STEPS - 2
REACH_Y = STEPS - 1


def pack_y(sign):
    out, at = [], 0
    for x in range(LX):
        for ch in range(CHANNELS):
            n = REACH_Y + sign * CY[ch]
            out.append((ch, x, LY - n if sign > 0 else 0, n, at))
            at += n
    return out, -(-at // 8) * 8


def pack_x(sign):
    out, at = [], 0
    for ch in range(CHANNELS):
        n = REACH_X + sign * CX[ch]
        for x in range(LX - n, LX) if sign > 0 else range(n):
            out.append((ch, x, REACH_Y + CY[ch], REACH_Y - CY[ch], at))
            at += 2 * REACH_Y + LY
    return out, at


SPAN = 2 * REACH_Y + LY
Y_UP, Y_ROWS = pack_y(1)
Y_DOWN, _ = pack_y(-1)
X_RIGHT, NEXT_AT = pack_x(1)
X_LEFT, _ = pack_x(-1)
Y_UP_AT = {(ch, x): (n, at) for ch, x, _, n, at in Y_UP}
Y_DOWN_AT = {(ch, x): (n, at) for ch, x, _, n, at in Y_DOWN}
X_RIGHT_AT = {(ch, x): at for ch, x, _, _, at in X_RIGHT}
X_LEFT_AT = {(ch, x): at for ch, x, _, _, at in X_LEFT}
RIGHT = [i for i in range(19) if CX[i] == 1]
LEFT = [i for i in range(19) if CX[i] == -1]
NEXT = SPAN - 2
X_ROWS = -(-(NEXT_AT + NEXT * len(RIGHT)) // 8) * 8


def collide(f, label, drive, phase):
    rho = f[0]
    for i in range(1, 19):
        rho = rho + f[i]
    j = []
    for axis in range(3):
        total = None
        for i in range(1, 19, 2):
            c = VELOCITY[i][axis]
            if c == 0:
                continue
            term = f[i] - f[i + 1] if c > 0 else f[i + 1] - f[i]
            total = term if total is None else total + term
        j.append(total)
    second = label == 1.0
    solid = label == 2.0
    omega = jnp.where(second, 1.1, 1.6)
    keep = 1.0 - omega
    strength = jnp.where(second, 0.6 * phase, phase)
    inverse = 1.0 / rho
    mix = [omega * j[axis] + strength * drive[axis] for axis in range(3)]
    base = omega * (rho - 1.5 * (j[0] * j[0] + j[1] * j[1] + j[2] * j[2]) * inverse)
    curve = 4.5 * omega * inverse

    def along(vector, c):
        total = None
        for axis in range(3):
            if c[axis] == 0:
                continue
            if total is None:
                total = vector[axis] if c[axis] > 0 else -vector[axis]
            else:
                total = total + vector[axis] if c[axis] > 0 else total - vector[axis]
        return total

    post = [None] * 19
    post[0] = jnp.where(solid, f[0], keep * f[0] + WEIGHTS[0] * base)
    for i in range(1, 19, 2):
        w = WEIGHTS[i]
        cj = along(j, VELOCITY[i])
        even = w * (base + curve * (cj * cj))
        odd = (3.0 * w) * along(mix, VELOCITY[i])
        post[i] = jnp.where(solid, f[i + 1], keep * f[i] + (even + odd))
        post[i + 1] = jnp.where(solid, f[i], keep * f[i + 1] + (even - odd))
    fluid = jnp.where(solid, 0.0, inverse)
    stress = [j[a] * j[b] * fluid for a, b in PAIRS]
    return post, stress


def first_kernel(pops_in, label_in, drive_in, cells, total, far, near, box, pops, label, drive, sems):
    copies = [
        pltpu.make_async_copy(source, target, sems.at[k])
        for k, (source, target) in enumerate(((pops_in, pops), (label_in, label), (drive_in, drive)))
    ]
    for copy in copies:
        copy.start()
    for copy in copies:
        copy.wait()
    up = lax.rem(lax.axis_index(GY), 2)
    down = 1 - up
    sums = [jnp.zeros((LY, NZ), jnp.float32)] * 6
    for x in range(LX):
        f = [pops[i, x] for i in range(19)]
        lab = label[x].astype(jnp.float32)
        force = [drive[axis, x] for axis in range(3)]
        post, stress = collide(f, lab, force, PHASES[0])
        for i in range(19):
            cells[i, x] = post[i]
        cells[19, x] = lab
        for axis in range(3):
            cells[20 + axis, x] = force[axis]
        sums = [sums[k] + stress[k] for k in range(6)]
    for k in range(6):
        total[k] = sums[k]
    for ch, x, row, n, at in Y_UP:
        box[up, at : at + n, :] = cells[ch, x, row : row + n, :]
    for ch, x, row, n, at in Y_DOWN:
        box[down, at : at + n, :] = cells[ch, x, row : row + n, :]
    near[...] = box[0]
    far[...] = box[1]


PACK = 16
ROW0 = 8
WORK_ROWS = 24


def spin(value, i):
    cz = VELOCITY[i][2]
    return pltpu.roll(value, cz % NZ, 1) if cz else value


def arrive(source, x, row, n):
    return [
        spin(source[i, x - CX[i], row - CY[i] : row - CY[i] + n, :], i) for i in range(19)
    ]


def second_kernel(cells, got_far, got_near, far, near, packs, rows, box):
    odd_y = lax.rem(lax.axis_index(GY), 2)
    right = lax.rem(lax.axis_index(GX), 2)
    rows[0] = got_near[...]
    rows[1] = got_far[...]
    for ch in range(CHANNELS):
        for x in range(LX):
            low, source = Y_UP_AT[ch, x]
            packs[ch, x, 0:low, :] = rows[1 - odd_y, source : source + low, :]
            packs[ch, x, low : low + LY, :] = cells[ch, x]
            high, source = Y_DOWN_AT[ch, x]
            packs[ch, x, low + LY : low + LY + high, :] = rows[odd_y, source : source + high, :]
    for slot, entries, comps, x in (
        (right, X_RIGHT, RIGHT, LX - 1 - REACH_X),
        (1 - right, X_LEFT, LEFT, REACH_X),
    ):
        for ch, layer, _, _, at in entries:
            box[slot, at : at + SPAN, :] = packs[ch, layer, 0:SPAN, :]
        f = [spin(packs[i, x - CX[i], 0:SPAN, :], i) for i in range(19)]
        lab, *force = [packs[ch, x, 0:SPAN, :] for ch in range(19, CHANNELS)]
        post, _ = collide(f, lab, force, PHASES[1])
        for k, i in enumerate(comps):
            at = NEXT_AT + k * NEXT
            box[slot, at : at + NEXT, :] = post[i][1 - CY[i] : 1 - CY[i] + NEXT]
    near[...] = box[0]
    far[...] = box[1]


def third_kernel(
    cells, total, packs, x_far, x_near, post3, spread, cols, one, two, sums
):
    odd_x = lax.rem(lax.axis_index(GX), 2)
    left_slot, right_slot = 1 - odd_x, odd_x
    cols[0] = x_near[...]
    cols[1] = x_far[...]

    def packed(ch, x):
        if x < 0:
            at = X_RIGHT_AT[ch, x + LX]
            return cols[left_slot, at : at + SPAN, :]
        if x >= LX:
            at = X_LEFT_AT[ch, x - LX]
            return cols[right_slot, at : at + SPAN, :]
        return packs[ch, x, 0:SPAN, :]

    def add(first, second):
        return second if first is None else [a + b for a, b in zip(first, second)]

    for slot, comps, x in ((left_slot, RIGHT, 0), (right_slot, LEFT, LX + 2 * REACH_X + 1)):
        for k, i in enumerate(comps):
            at = NEXT_AT + k * NEXT
            low = ROW0 - (REACH_Y - 1) - CY[i]
            one[i, x, low : low + NEXT, :] = cols[slot, at : at + NEXT, :]
    last = [total[k] for k in range(6)]
    for step, source, target, near, before, after in (
        (1, None, one, REACH_X, 0, REACH_X + 1),
        (2, one, two, REACH_X, REACH_X + 1, REACH_X),
        (3, two, post3, REACH_X - 1, REACH_X, REACH_X - 1),
    ):
        wide = REACH_Y + 1 - step
        n = LY + 2 * wide
        to = 0 if step == 3 else ROW0 - wide
        kept = None
        for x in range(-near, LX + near):
            if step == 1:
                f = [spin(packed(i, x - CX[i]), i) for i in range(19)]
            else:
                f = arrive(source, x + before, ROW0 - wide, n)
            at = REACH_Y - wide
            lab, *force = [packed(ch, x)[at : at + n] for ch in range(19, CHANNELS)]
            post, stress = collide(f, lab, force, PHASES[step])
            for i in range(19):
                target[i, x + after, to : to + n, :] = post[i]
            if 0 <= x < LX:
                kept = add(kept, stress)
        for k in range(6):
            sums[6 * step - 6 + k, 0:n, :] = kept[k]
        last = [last[k] + sums[6 * step - 6 + k, wide : wide + LY, :] for k in range(6)]
    stacked = jnp.concatenate(last, axis=0)
    r = lax.broadcasted_iota(jnp.int32, (16, 48), 0)
    c = lax.broadcasted_iota(jnp.int32, (16, 48), 1)
    chosen = jnp.logical_and((r & 7) == (c >> 3), (r >> 3) == ((c & 7) >> 2))
    left = jnp.where(chosen, 1.0, 0.0)
    halves = jnp.dot(left, stacked, precision=HIGHEST, preferred_element_type=jnp.float32)
    z = lax.broadcasted_iota(jnp.int32, (2 * NZ, NZ), 0)
    lane = lax.broadcasted_iota(jnp.int32, (2 * NZ, NZ), 1)
    table = jnp.where(lane == z >> 2, 1.0 / (STEPS * 64), 0.0)
    slow = jnp.dot(
        jnp.concatenate([halves[0:8], halves[8:16]], axis=1),
        table,
        precision=HIGHEST,
        preferred_element_type=jnp.float32,
    )
    for d in range(spread.shape[0]):
        spread[d] = slow


def momentum_of(post3, out):
    for x in range(LX):
        f = [None] + [
            spin(post3[i, x + 1 - CX[i], 1 - CY[i] : 1 - CY[i] + LY, :], i) for i in range(1, 19)
        ]
        for axis in range(3):
            total = None
            for i in range(1, 19, 2):
                c = VELOCITY[i][axis]
                if c == 0:
                    continue
                term = f[i] - f[i + 1] if c > 0 else f[i + 1] - f[i]
                total = term if total is None else total + term
            out[axis, x] = total


TILES = 3


@functools.cache
def operator_table(sx, sy):
    waves = [2.0 * math.pi * np.fft.fftfreq(n) for n in (sx, sy, SZ)]
    k = np.meshgrid(*waves, indexing="ij")
    square = k[0] ** 2 + k[1] ** 2 + k[2] ** 2
    positive = square > 0
    safe = np.where(positive, square, 1.0)
    half = SZ // 2 + 1
    modes = sy * half
    lanes = TILES * NZ
    ky = np.repeat(np.arange(sy), half)
    kz = np.tile(np.arange(half), sy)
    weight = np.where((kz == 0) | (kz == SZ // 2), 1.0, 2.0) / (sy * SZ)
    gains = np.zeros((3, 6, sx, lanes))
    twists = np.zeros((3, 8, lanes))
    imaginary = []
    for a in range(3):
        for c in range(6):
            force = [
                -1j * sum(k[b] for b in range(3) if COMPONENT[first][b] == c) + 0.0 * k[0]
                for first in range(3)
            ]
            inner = k[0] * force[0] + k[1] * force[1] + k[2] * force[2]
            gain = np.where(positive, (force[a] - k[a] * inner / safe) / (SLOW_VISCOSITY * safe), 0.0)
            flipped = gain
            for axis in range(3):
                flipped = np.roll(np.flip(flipped, axis), 1, axis)
            gain = 0.5 * (gain + np.conj(flipped))
            line = weight * np.fft.ifft(gain, axis=0)[:, :, :half].reshape(sx, modes)
            odd_x = (int(a == 0) + sum(int(d == 0) for d in PAIRS[c])) % 2
            imaginary.append(not odd_x)
            gains[a, c, :, :modes] = line.real if odd_x else line.imag
            if odd_x:
                twists[a, c, :modes] = line.imag[0]
    gains = gains.reshape(3, 6, sx // GROUP, GROUP, TILES, NZ).transpose(0, 1, 4, 3, 2, 5)
    gains = np.concatenate([gains[:, :, :, :, -1:], gains], axis=4)
    twists = twists.reshape(3, 8, TILES, NZ).transpose(0, 2, 1, 3)
    y = np.repeat(np.arange(2), SZ)
    z = np.tile(np.arange(SZ), 2)
    angle = 2.0 * math.pi * (np.outer(y, ky) / sy + np.outer(z, kz) / SZ)
    forward = np.zeros((2, NZ, lanes))
    forward[0, :64, :modes] = np.cos(angle)
    forward[1, :64, :modes] = -np.sin(angle)
    forward = forward.reshape(2, NZ, TILES, NZ).transpose(0, 2, 1, 3)
    shift = 2.0 * math.pi * np.outer(2 * np.arange(sy // 2), ky) / sy
    turns = np.zeros((sy // 2, 2, lanes))
    turns[:, 0, :modes] = np.cos(shift)
    turns[:, 1, :modes] = np.sin(shift)
    turns = np.concatenate([turns.reshape(-1, NZ), np.zeros((-turns.size // NZ % 8, NZ))])
    sections = [gains.reshape(-1, NZ), twists.reshape(-1, NZ), turns, forward.reshape(-1, NZ)]
    starts = np.cumsum([0] + [len(section) for section in sections])
    table = np.concatenate(sections).astype(np.float32)
    return table, tuple(int(start) for start in starts[:4]), tuple(imaginary)


def solve_kernel(
    starts, imaginary, pairs, groups, blocks, table, post3, out, momentum, part, hat, field
):
    momentum_of(post3, momentum)
    at_gain, at_twist, at_turn, at_forward = starts
    me = lax.axis_index("cy")
    mine = lax.rem(lax.axis_index(GX), GROUP)
    upper = lax.axis_index("zh")
    column = lax.axis_index("cx")
    columns = pairs // 2
    forward = jnp.concatenate(
        [table[at_forward + k * NZ : at_forward + (k + 1) * NZ, :] for k in range(2 * TILES)], axis=1
    )
    part[...] = jnp.dot(
        blocks[...].reshape(2 * GROUP * 8, NZ),
        forward,
        precision=HIGHEST,
        preferred_element_type=jnp.float32,
    ).reshape(2 * GROUP, 8, 2 * TILES * NZ)
    half = [table[at_turn + columns * (2 * TILES) + k : at_turn + columns * (2 * TILES) + k + 1, :] for k in range(TILES)]
    half = jnp.concatenate(half + half, axis=1)
    for r in range(GROUP):
        hat[r] = part[2 * r + upper] + half * part[2 * r + 1 - upper]

    sign = (1 - 2 * lax.rem(mine, 2)).astype(jnp.float32)
    for k in range(TILES):
        re_lanes = slice(k * NZ, (k + 1) * NZ)
        im_lanes = slice((TILES + k) * NZ, (TILES + k + 1) * NZ)
        all_re = hat[0, :, re_lanes]
        all_im = hat[0, :, im_lanes]
        for r in range(1, GROUP):
            all_re = all_re + hat[r, :, re_lanes] if r % 2 == 0 else all_re - hat[r, :, re_lanes]
            all_im = all_im + hat[r, :, im_lanes] if r % 2 == 0 else all_im - hat[r, :, im_lanes]
        re, im = [], []
        for a in range(3):
            at = at_twist + (a * TILES + k) * 8
            wave = sign * table[at : at + 8, :]
            first_re = -jnp.sum(wave * all_im, axis=0, keepdims=True)
            first_im = jnp.sum(wave * all_re, axis=0, keepdims=True)
            re.append(jnp.broadcast_to(first_re, (groups, NZ)))
            im.append(jnp.broadcast_to(first_im, (groups, NZ)))
        for r in range(GROUP):
            apart = mine + GROUP - r
            ahead = apart // GROUP
            row = (apart - GROUP * ahead) * (groups + 1) + ahead
            for c in range(6):
                hat_re = jnp.broadcast_to(hat[r, c : c + 1, re_lanes], (groups, NZ))
                hat_im = jnp.broadcast_to(hat[r, c : c + 1, im_lanes], (groups, NZ))
                for a in range(3):
                    at = at_gain + ((a * 6 + c) * TILES + k) * (GROUP * (groups + 1))
                    gain = table[pl.ds(at + row, groups), :]
                    if imaginary[a * 6 + c]:
                        re[a] = re[a] - gain * hat_im
                        im[a] = im[a] + gain * hat_re
                    else:
                        re[a] = re[a] + gain * hat_re
                        im[a] = im[a] + gain * hat_im
        for j in range(columns):
            d = lax.rem(pairs + j - column, pairs)
            cosine = table[pl.ds(at_turn + k + d * (2 * TILES), 1), :]
            sine = table[pl.ds(at_turn + TILES + k + d * (2 * TILES), 1), :]
            for a in range(3):
                at = (a * columns + j) * groups
                field[at : at + groups, re_lanes] = re[a] * cosine - im[a] * sine
                field[at : at + groups, im_lanes] = re[a] * sine + im[a] * cosine
    result = lax.dot_general(
        field[...],
        forward,
        (((1,), (1,)), ((), ())),
        precision=HIGHEST,
        preferred_element_type=jnp.float32,
    )
    for j in range(columns):
        first, second, third = [
            result[(a * columns + j) * groups : (a * columns + j + 1) * groups] for a in range(3)
        ]
        both = first + pltpu.roll(second, 64, 1)
        for q in range(groups):
            target = lax.rem(me + q, groups) * columns + j
            out[target, 0:1, :] = both[q : q + 1]
            out[target, 1:2, :] = third[q : q + 1]


def last_kernel(parts, out):
    total = jnp.sum(parts[...], axis=0)
    for a in range(3):
        row = total[a // 2 : a // 2 + 1, :]
        for y in range(2):
            lane = (a % 2) * 64 + y * SZ
            value = pltpu.roll(row, (NZ - lane) % NZ, 1) if lane else row
            out[a, 0, y : y + 1, :] = value[:, :SZ]


def call(body, outs, scratch, cost, limit=16, place=pltpu.VMEM, more=()):
    shapes = [jax.ShapeDtypeStruct(s, jnp.float32) for s in outs]
    spec = pl.BlockSpec(memory_space=pltpu.VMEM)

    def run(*args):
        return pl.pallas_call(
            body,
            out_shape=shapes,
            in_specs=[pl.BlockSpec(memory_space=place)] * len(args),
            out_specs=[spec] * len(shapes),
            scratch_shapes=[pltpu.VMEM(s, jnp.float32) for s in scratch] + list(more),
            compiler_params=pltpu.CompilerParams(vmem_limit_bytes=limit << 20),
            cost_estimate=pl.CostEstimate(flops=cost, bytes_accessed=cost, transcendentals=0),
        )(*args)

    return run


def swap(far, near, axis):
    count = lax.axis_size(axis)
    near_pairs = [(i, i ^ 1) for i in range(count)]
    far_pairs = [(i, (i + 1) % count if i % 2 else (i - 1) % count) for i in range(count)]
    return lax.ppermute(far, axis, far_pairs), lax.ppermute(near, axis, near_pairs)


def local(pops, label, drive):
    nx = lax.axis_size(GX)
    ny = lax.axis_size(GY)
    groups = lax.axis_size("cy")
    cells, total, far, near = call(
        first_kernel,
        [(CHANNELS, LX, LY, NZ), (6, LY, NZ), (Y_ROWS, NZ), (Y_ROWS, NZ)],
        [(2, Y_ROWS, NZ), pops.shape],
        2_000_000,
        place=pltpu.HBM,
        more=[
            pltpu.VMEM(label.shape, jnp.int32),
            pltpu.VMEM(drive.shape, jnp.float32),
            pltpu.SemaphoreType.DMA((3,)),
        ],
    )(*[pltpu.with_memory_space_constraint(value, pltpu.HBM) for value in (pops, label, drive)])
    y_far, y_near = swap(far, near, GY)
    far, near, packs = call(
        second_kernel,
        [(X_ROWS, NZ), (X_ROWS, NZ), (CHANNELS, LX, PACK, NZ)],
        [(2, Y_ROWS, NZ), (2, X_ROWS, NZ)],
        2_000_000,
    )(cells, y_far, y_near)
    x_far, x_near = swap(far, near, GX)
    post3, spread = call(
        third_kernel,
        [(19, LX + 2, PACK, NZ), (2 * GROUP, 8, NZ)],
        [
            (2, X_ROWS, NZ),
            (19, LX + 2 * REACH_X + 2, WORK_ROWS, NZ),
            (19, LX + 2 * REACH_X, WORK_ROWS, NZ),
            (18, 16, NZ),
        ],
        20_000_000,
    )(cells, total, packs, x_far, x_near)
    blocks = lax.all_to_all(spread, ("zl", "core", "zh"), 0, 0, tiled=False)
    table, starts, imaginary = operator_table(nx, 2 * ny)
    parts, momentum = call(
        functools.partial(solve_kernel, starts, imaginary, ny, groups),
        [(groups * ny // 2, 2, NZ), (3, LX, LY, NZ)],
        [
            (2 * GROUP, 8, 2 * TILES * NZ),
            (GROUP, 8, 2 * TILES * NZ),
            (3 * groups * ny // 2, 2 * TILES * NZ),
        ],
        10_000_000,
    )(blocks, table, post3)
    parts = lax.all_to_all(parts, ("cy", "cx"), 0, 0, tiled=False)
    (running,) = call(last_kernel, [(3, 1, 2, SZ)], [], 100_000)(parts)
    return momentum, running


def solution(mesh):
    nx, ny = mesh.devices.shape
    devices = mesh.devices.reshape(nx // GROUP, 4, 2, 2, ny // 2)
    mesh = jax.sharding.Mesh(devices, GX + GY)
    in_specs = (P(None, GX, GY, None), P(GX, GY, None), P(None, GX, GY, None))
    out_specs = (P(None, GX, GY, None), P(None, GX, GY, None))
    return jax.shard_map(local, mesh=mesh, in_specs=in_specs, out_specs=out_specs, check_vma=False)
```

```python
import functools
import math

import jax
import jax.numpy as jnp
import numpy as np
from jax import lax
from jax.experimental import pallas as pl
from jax.experimental.pallas import tpu as pltpu
from jax.sharding import PartitionSpec as P

NZ = 128
STEPS = 4
SZ = 32
LX = 4
LY = 8
VELOCITY = [
    [0, 0, 0],
    [1, 0, 0],
    [-1, 0, 0],
    [0, 1, 0],
    [0, -1, 0],
    [0, 0, 1],
    [0, 0, -1],
    [1, 1, 0],
    [-1, -1, 0],
    [1, -1, 0],
    [-1, 1, 0],
    [1, 0, 1],
    [-1, 0, -1],
    [1, 0, -1],
    [-1, 0, 1],
    [0, 1, 1],
    [0, -1, -1],
    [0, 1, -1],
    [0, -1, 1],
]
OPPOSITE = [0, 2, 1, 4, 3, 6, 5, 8, 7, 10, 9, 12, 11, 14, 13, 16, 15, 18, 17]
WEIGHTS = [1.0 / 3.0] + [1.0 / 18.0] * 6 + [1.0 / 36.0] * 12
PAIRS = [(0, 0), (1, 1), (2, 2), (0, 1), (0, 2), (1, 2)]
COMPONENT = [[0, 3, 4], [3, 1, 5], [4, 5, 2]]
SLOW_VISCOSITY = 0.0004
PHASES = [math.cos(2.0 * math.pi * (step + 0.5) / STEPS) for step in range(STEPS)]

CHANNELS = 23
CX = [v[0] for v in VELOCITY] + [0] * 4
CY = [v[1] for v in VELOCITY] + [0] * 4
HIGHEST = lax.Precision.HIGHEST
GX = ("cy", "zl", "core")
GY = ("zh", "cx")
GROUP = 8


REACH_X = STEPS - 2
REACH_Y = STEPS - 1


def pack_y(sign):
    out, at = [], 0
    for x in range(LX):
        for ch in range(CHANNELS):
            n = REACH_Y + sign * CY[ch]
            out.append((ch, x, LY - n if sign > 0 else 0, n, at))
            at += n
    return out, -(-at // 8) * 8


def pack_x(sign):
    out, at = [], 0
    for ch in range(CHANNELS):
        n = REACH_X - 1 + sign * CX[ch] if ch < 19 else REACH_X
        for x in range(LX - n, LX) if sign > 0 else range(n):
            out.append((ch, x, REACH_Y + CY[ch], REACH_Y - CY[ch], at))
            at += 2 * REACH_Y + LY
    return out, at


SPAN = 2 * REACH_Y + LY
Y_UP, Y_ROWS = pack_y(1)
Y_DOWN, _ = pack_y(-1)
X_RIGHT, NEXT_AT = pack_x(1)
X_LEFT, _ = pack_x(-1)
Y_UP_AT = {(ch, x): (n, at) for ch, x, _, n, at in Y_UP}
Y_DOWN_AT = {(ch, x): (n, at) for ch, x, _, n, at in Y_DOWN}
X_RIGHT_AT = {(ch, x): at for ch, x, _, _, at in X_RIGHT}
X_LEFT_AT = {(ch, x): at for ch, x, _, _, at in X_LEFT}
NEXT = SPAN - 2
INNER = (1, 2)


def pack_next(sign):
    out, at = [], NEXT_AT
    for depth, x in enumerate(INNER[::-1] if sign > 0 else INNER):
        for i in range(19):
            if sign * CX[i] >= depth:
                out.append((i, x, at))
                at += NEXT
    return out, -(-at // 8) * 8


NEXT_RIGHT, X_ROWS = pack_next(1)
NEXT_LEFT, _ = pack_next(-1)


def collide(f, label, drive, phase):
    rho = f[0]
    for i in range(1, 19):
        rho = rho + f[i]
    j = []
    for axis in range(3):
        total = None
        for i in range(1, 19, 2):
            c = VELOCITY[i][axis]
            if c == 0:
                continue
            term = f[i] - f[i + 1] if c > 0 else f[i + 1] - f[i]
            total = term if total is None else total + term
        j.append(total)
    second = label == 1.0
    solid = label == 2.0
    omega = jnp.where(second, 1.1, 1.6)
    keep = 1.0 - omega
    strength = jnp.where(second, 0.6 * phase, phase)
    inverse = 1.0 / rho
    mix = [omega * j[axis] + strength * drive[axis] for axis in range(3)]
    base = omega * (rho - 1.5 * (j[0] * j[0] + j[1] * j[1] + j[2] * j[2]) * inverse)
    curve = 4.5 * omega * inverse

    def along(vector, c):
        total = None
        for axis in range(3):
            if c[axis] == 0:
                continue
            if total is None:
                total = vector[axis] if c[axis] > 0 else -vector[axis]
            else:
                total = total + vector[axis] if c[axis] > 0 else total - vector[axis]
        return total

    post = [None] * 19
    post[0] = jnp.where(solid, f[0], keep * f[0] + WEIGHTS[0] * base)
    for i in range(1, 19, 2):
        w = WEIGHTS[i]
        cj = along(j, VELOCITY[i])
        even = w * (base + curve * (cj * cj))
        odd = (3.0 * w) * along(mix, VELOCITY[i])
        post[i] = jnp.where(solid, f[i + 1], keep * f[i] + (even + odd))
        post[i + 1] = jnp.where(solid, f[i], keep * f[i + 1] + (even - odd))
    fluid = jnp.where(solid, 0.0, inverse)
    stress = [j[a] * j[b] * fluid for a, b in PAIRS]
    return post, stress


def first_kernel(pops_in, label_in, drive_in, cells, total, far, near, box, pops, label, drive, sems):
    copies = [
        pltpu.make_async_copy(source, target, sems.at[k])
        for k, (source, target) in enumerate(((pops_in, pops), (label_in, label), (drive_in, drive)))
    ]
    for copy in copies:
        copy.start()
    for copy in copies:
        copy.wait()
    up = lax.rem(lax.axis_index(GY), 2)
    down = 1 - up
    sums = [jnp.zeros((LY, NZ), jnp.float32)] * 6
    for x in range(LX):
        f = [pops[i, x] for i in range(19)]
        lab = label[x].astype(jnp.float32)
        force = [drive[axis, x] for axis in range(3)]
        post, stress = collide(f, lab, force, PHASES[0])
        for i in range(19):
            cells[i, x] = post[i]
        cells[19, x] = lab
        for axis in range(3):
            cells[20 + axis, x] = force[axis]
        sums = [sums[k] + stress[k] for k in range(6)]
    for k in range(6):
        total[k] = sums[k]
    for ch, x, row, n, at in Y_UP:
        box[up, at : at + n, :] = cells[ch, x, row : row + n, :]
    for ch, x, row, n, at in Y_DOWN:
        box[down, at : at + n, :] = cells[ch, x, row : row + n, :]
    near[...] = box[0]
    far[...] = box[1]


PACK = 16
ROW0 = 8
WORK_ROWS = 24


def spin(value, i):
    cz = VELOCITY[i][2]
    return pltpu.roll(value, cz % NZ, 1) if cz else value


def arrive(source, x, row, n):
    return [
        spin(source[i, x - CX[i], row - CY[i] : row - CY[i] + n, :], i) for i in range(19)
    ]


def second_kernel(cells, got_far, got_near, far, near, packs, rows, box):
    odd_y = lax.rem(lax.axis_index(GY), 2)
    right = lax.rem(lax.axis_index(GX), 2)
    rows[0] = got_near[...]
    rows[1] = got_far[...]
    for ch in range(CHANNELS):
        for x in range(LX):
            low, source = Y_UP_AT[ch, x]
            packs[ch, x, 0:low, :] = rows[1 - odd_y, source : source + low, :]
            packs[ch, x, low : low + LY, :] = cells[ch, x]
            high, source = Y_DOWN_AT[ch, x]
            packs[ch, x, low + LY : low + LY + high, :] = rows[odd_y, source : source + high, :]
    after = {}
    for x in INNER:
        f = [spin(packs[i, x - CX[i], 0:SPAN, :], i) for i in range(19)]
        lab, *force = [packs[ch, x, 0:SPAN, :] for ch in range(19, CHANNELS)]
        after[x], _ = collide(f, lab, force, PHASES[1])
    for slot, entries, following in ((right, X_RIGHT, NEXT_RIGHT), (1 - right, X_LEFT, NEXT_LEFT)):
        for ch, x, _, _, at in entries:
            box[slot, at : at + SPAN, :] = packs[ch, x, 0:SPAN, :]
        for i, x, at in following:
            box[slot, at : at + NEXT, :] = after[x][i][1 - CY[i] : 1 - CY[i] + NEXT]
    near[...] = box[0]
    far[...] = box[1]


def third_kernel(
    cells, total, packs, x_far, x_near, post3, spread, cols, one, two, sums
):
    odd_x = lax.rem(lax.axis_index(GX), 2)
    left_slot, right_slot = 1 - odd_x, odd_x
    cols[0] = x_near[...]
    cols[1] = x_far[...]

    def packed(ch, x):
        if x < 0:
            at = X_RIGHT_AT[ch, x + LX]
            return cols[left_slot, at : at + SPAN, :]
        if x >= LX:
            at = X_LEFT_AT[ch, x - LX]
            return cols[right_slot, at : at + SPAN, :]
        return packs[ch, x, 0:SPAN, :]

    def add(first, second):
        return second if first is None else [a + b for a, b in zip(first, second)]

    for slot, following, shift in ((left_slot, NEXT_RIGHT, -LX), (right_slot, NEXT_LEFT, LX)):
        for i, x, at in following:
            low = ROW0 - (REACH_Y - 1) - CY[i]
            one[i, x + shift + REACH_X + 1, low : low + NEXT, :] = cols[slot, at : at + NEXT, :]
    last = [total[k] for k in range(6)]
    for step, source, target, near, before, after in (
        (1, None, one, REACH_X - 1, 0, REACH_X + 1),
        (2, one, two, REACH_X, REACH_X + 1, REACH_X),
        (3, two, post3, REACH_X - 1, REACH_X, REACH_X - 1),
    ):
        wide = REACH_Y + 1 - step
        n = LY + 2 * wide
        to = 0 if step == 3 else ROW0 - wide
        kept = None
        for x in range(-near, LX + near):
            if step == 1:
                f = [spin(packed(i, x - CX[i]), i) for i in range(19)]
            else:
                f = arrive(source, x + before, ROW0 - wide, n)
            at = REACH_Y - wide
            lab, *force = [packed(ch, x)[at : at + n] for ch in range(19, CHANNELS)]
            post, stress = collide(f, lab, force, PHASES[step])
            for i in range(19):
                target[i, x + after, to : to + n, :] = post[i]
            if 0 <= x < LX:
                kept = add(kept, stress)
        for k in range(6):
            sums[6 * step - 6 + k, 0:n, :] = kept[k]
        last = [last[k] + sums[6 * step - 6 + k, wide : wide + LY, :] for k in range(6)]
    stacked = jnp.concatenate(last, axis=0)
    r = lax.broadcasted_iota(jnp.int32, (16, 48), 0)
    c = lax.broadcasted_iota(jnp.int32, (16, 48), 1)
    chosen = jnp.logical_and((r & 7) == (c >> 3), (r >> 3) == ((c & 7) >> 2))
    left = jnp.where(chosen, 1.0, 0.0)
    halves = jnp.dot(left, stacked, precision=HIGHEST, preferred_element_type=jnp.float32)
    z = lax.broadcasted_iota(jnp.int32, (2 * NZ, NZ), 0)
    lane = lax.broadcasted_iota(jnp.int32, (2 * NZ, NZ), 1)
    table = jnp.where(lane == z >> 2, 1.0 / (STEPS * 64), 0.0)
    slow = jnp.dot(
        jnp.concatenate([halves[0:8], halves[8:16]], axis=1),
        table,
        precision=HIGHEST,
        preferred_element_type=jnp.float32,
    )
    for d in range(spread.shape[0]):
        spread[d] = slow


def momentum_of(post3, out):
    for x in range(LX):
        f = [None] + [
            spin(post3[i, x + 1 - CX[i], 1 - CY[i] : 1 - CY[i] + LY, :], i) for i in range(1, 19)
        ]
        for axis in range(3):
            total = None
            for i in range(1, 19, 2):
                c = VELOCITY[i][axis]
                if c == 0:
                    continue
                term = f[i] - f[i + 1] if c > 0 else f[i + 1] - f[i]
                total = term if total is None else total + term
            out[axis, x] = total


TILES = 3


@functools.cache
def operator_table(sx, sy):
    waves = [2.0 * math.pi * np.fft.fftfreq(n) for n in (sx, sy, SZ)]
    k = np.meshgrid(*waves, indexing="ij")
    square = k[0] ** 2 + k[1] ** 2 + k[2] ** 2
    positive = square > 0
    safe = np.where(positive, square, 1.0)
    half = SZ // 2 + 1
    modes = sy * half
    lanes = TILES * NZ
    ky = np.repeat(np.arange(sy), half)
    kz = np.tile(np.arange(half), sy)
    weight = np.where((kz == 0) | (kz == SZ // 2), 1.0, 2.0) / (sy * SZ)
    gains = np.zeros((3, 6, sx, lanes))
    twists = np.zeros((3, 8, lanes))
    imaginary = []
    for a in range(3):
        for c in range(6):
            force = [
                -1j * sum(k[b] for b in range(3) if COMPONENT[first][b] == c) + 0.0 * k[0]
                for first in range(3)
            ]
            inner = k[0] * force[0] + k[1] * force[1] + k[2] * force[2]
            gain = np.where(positive, (force[a] - k[a] * inner / safe) / (SLOW_VISCOSITY * safe), 0.0)
            flipped = gain
            for axis in range(3):
                flipped = np.roll(np.flip(flipped, axis), 1, axis)
            gain = 0.5 * (gain + np.conj(flipped))
            line = weight * np.fft.ifft(gain, axis=0)[:, :, :half].reshape(sx, modes)
            odd_x = (int(a == 0) + sum(int(d == 0) for d in PAIRS[c])) % 2
            imaginary.append(not odd_x)
            gains[a, c, :, :modes] = line.real if odd_x else line.imag
            if odd_x:
                twists[a, c, :modes] = line.imag[0]
    gains = gains.reshape(3, 6, sx // GROUP, GROUP, TILES, NZ).transpose(0, 1, 4, 3, 2, 5)
    gains = np.concatenate([gains[:, :, :, :, -1:], gains], axis=4)
    twists = twists.reshape(3, 8, TILES, NZ).transpose(0, 2, 1, 3)
    y = np.repeat(np.arange(2), SZ)
    z = np.tile(np.arange(SZ), 2)
    angle = 2.0 * math.pi * (np.outer(y, ky) / sy + np.outer(z, kz) / SZ)
    forward = np.zeros((2, NZ, lanes))
    forward[0, :64, :modes] = np.cos(angle)
    forward[1, :64, :modes] = -np.sin(angle)
    forward = forward.reshape(2, NZ, TILES, NZ).transpose(0, 2, 1, 3)
    shift = 2.0 * math.pi * np.outer(2 * np.arange(sy // 2), ky) / sy
    turns = np.zeros((sy // 2, 2, lanes))
    turns[:, 0, :modes] = np.cos(shift)
    turns[:, 1, :modes] = np.sin(shift)
    turns = np.concatenate([turns.reshape(-1, NZ), np.zeros((-turns.size // NZ % 8, NZ))])
    sections = [gains.reshape(-1, NZ), twists.reshape(-1, NZ), turns, forward.reshape(-1, NZ)]
    starts = np.cumsum([0] + [len(section) for section in sections])
    table = np.concatenate(sections).astype(np.float32)
    return table, tuple(int(start) for start in starts[:4]), tuple(imaginary)


def solve_kernel(
    starts, imaginary, pairs, groups, blocks, table, post3, out, momentum, part, hat, field
):
    momentum_of(post3, momentum)
    at_gain, at_twist, at_turn, at_forward = starts
    me = lax.axis_index("cy")
    mine = lax.rem(lax.axis_index(GX), GROUP)
    upper = lax.axis_index("zh")
    column = lax.axis_index("cx")
    columns = pairs // 2
    forward = jnp.concatenate(
        [table[at_forward + k * NZ : at_forward + (k + 1) * NZ, :] for k in range(2 * TILES)], axis=1
    )
    part[...] = jnp.dot(
        blocks[...].reshape(2 * GROUP * 8, NZ),
        forward,
        precision=HIGHEST,
        preferred_element_type=jnp.float32,
    ).reshape(2 * GROUP, 8, 2 * TILES * NZ)
    half = [table[at_turn + columns * (2 * TILES) + k : at_turn + columns * (2 * TILES) + k + 1, :] for k in range(TILES)]
    half = jnp.concatenate(half + half, axis=1)
    for r in range(GROUP):
        hat[r] = part[2 * r + upper] + half * part[2 * r + 1 - upper]

    sign = (1 - 2 * lax.rem(mine, 2)).astype(jnp.float32)
    for k in range(TILES):
        re_lanes = slice(k * NZ, (k + 1) * NZ)
        im_lanes = slice((TILES + k) * NZ, (TILES + k + 1) * NZ)
        all_re = hat[0, :, re_lanes]
        all_im = hat[0, :, im_lanes]
        for r in range(1, GROUP):
            all_re = all_re + hat[r, :, re_lanes] if r % 2 == 0 else all_re - hat[r, :, re_lanes]
            all_im = all_im + hat[r, :, im_lanes] if r % 2 == 0 else all_im - hat[r, :, im_lanes]
        re, im = [], []
        for a in range(3):
            at = at_twist + (a * TILES + k) * 8
            wave = sign * table[at : at + 8, :]
            first_re = -jnp.sum(wave * all_im, axis=0, keepdims=True)
            first_im = jnp.sum(wave * all_re, axis=0, keepdims=True)
            re.append(jnp.broadcast_to(first_re, (groups, NZ)))
            im.append(jnp.broadcast_to(first_im, (groups, NZ)))
        for r in range(GROUP):
            apart = mine + GROUP - r
            ahead = apart // GROUP
            row = (apart - GROUP * ahead) * (groups + 1) + ahead
            for c in range(6):
                hat_re = jnp.broadcast_to(hat[r, c : c + 1, re_lanes], (groups, NZ))
                hat_im = jnp.broadcast_to(hat[r, c : c + 1, im_lanes], (groups, NZ))
                for a in range(3):
                    at = at_gain + ((a * 6 + c) * TILES + k) * (GROUP * (groups + 1))
                    gain = table[pl.ds(at + row, groups), :]
                    if imaginary[a * 6 + c]:
                        re[a] = re[a] - gain * hat_im
                        im[a] = im[a] + gain * hat_re
                    else:
                        re[a] = re[a] + gain * hat_re
                        im[a] = im[a] + gain * hat_im
        for j in range(columns):
            d = lax.rem(pairs + j - column, pairs)
            cosine = table[pl.ds(at_turn + k + d * (2 * TILES), 1), :]
            sine = table[pl.ds(at_turn + TILES + k + d * (2 * TILES), 1), :]
            for a in range(3):
                at = (a * columns + j) * groups
                field[at : at + groups, re_lanes] = re[a] * cosine - im[a] * sine
                field[at : at + groups, im_lanes] = re[a] * sine + im[a] * cosine
    result = lax.dot_general(
        field[...],
        forward,
        (((1,), (1,)), ((), ())),
        precision=HIGHEST,
        preferred_element_type=jnp.float32,
    )
    for j in range(columns):
        first, second, third = [
            result[(a * columns + j) * groups : (a * columns + j + 1) * groups] for a in range(3)
        ]
        both = first + pltpu.roll(second, 64, 1)
        for q in range(groups):
            target = lax.rem(me + q, groups) * columns + j
            out[target, 0:1, :] = both[q : q + 1]
            out[target, 1:2, :] = third[q : q + 1]


def last_kernel(parts, out):
    total = jnp.sum(parts[...], axis=0)
    for a in range(3):
        row = total[a // 2 : a // 2 + 1, :]
        for y in range(2):
            lane = (a % 2) * 64 + y * SZ
            value = pltpu.roll(row, (NZ - lane) % NZ, 1) if lane else row
            out[a, 0, y : y + 1, :] = value[:, :SZ]


def call(body, outs, scratch, cost, limit=16, place=pltpu.VMEM, more=()):
    shapes = [jax.ShapeDtypeStruct(s, jnp.float32) for s in outs]
    spec = pl.BlockSpec(memory_space=pltpu.VMEM)

    def run(*args):
        return pl.pallas_call(
            body,
            out_shape=shapes,
            in_specs=[pl.BlockSpec(memory_space=place)] * len(args),
            out_specs=[spec] * len(shapes),
            scratch_shapes=[pltpu.VMEM(s, jnp.float32) for s in scratch] + list(more),
            compiler_params=pltpu.CompilerParams(vmem_limit_bytes=limit << 20),
            cost_estimate=pl.CostEstimate(flops=cost, bytes_accessed=cost, transcendentals=0),
        )(*args)

    return run


def swap(far, near, axis):
    count = lax.axis_size(axis)
    near_pairs = [(i, i ^ 1) for i in range(count)]
    far_pairs = [(i, (i + 1) % count if i % 2 else (i - 1) % count) for i in range(count)]
    return lax.ppermute(far, axis, far_pairs), lax.ppermute(near, axis, near_pairs)


def local(pops, label, drive):
    nx = lax.axis_size(GX)
    ny = lax.axis_size(GY)
    groups = lax.axis_size("cy")
    cells, total, far, near = call(
        first_kernel,
        [(CHANNELS, LX, LY, NZ), (6, LY, NZ), (Y_ROWS, NZ), (Y_ROWS, NZ)],
        [(2, Y_ROWS, NZ), pops.shape],
        2_000_000,
        place=pltpu.HBM,
        more=[
            pltpu.VMEM(label.shape, jnp.int32),
            pltpu.VMEM(drive.shape, jnp.float32),
            pltpu.SemaphoreType.DMA((3,)),
        ],
    )(*[pltpu.with_memory_space_constraint(value, pltpu.HBM) for value in (pops, label, drive)])
    y_far, y_near = swap(far, near, GY)
    far, near, packs = call(
        second_kernel,
        [(X_ROWS, NZ), (X_ROWS, NZ), (CHANNELS, LX, PACK, NZ)],
        [(2, Y_ROWS, NZ), (2, X_ROWS, NZ)],
        2_000_000,
    )(cells, y_far, y_near)
    x_far, x_near = swap(far, near, GX)
    post3, spread = call(
        third_kernel,
        [(19, LX + 2, PACK, NZ), (2 * GROUP, 8, NZ)],
        [
            (2, X_ROWS, NZ),
            (19, LX + 2 * REACH_X + 2, WORK_ROWS, NZ),
            (19, LX + 2 * REACH_X, WORK_ROWS, NZ),
            (18, 16, NZ),
        ],
        20_000_000,
    )(cells, total, packs, x_far, x_near)
    blocks = lax.all_to_all(spread, ("zl", "core", "zh"), 0, 0, tiled=False)
    table, starts, imaginary = operator_table(nx, 2 * ny)
    parts, momentum = call(
        functools.partial(solve_kernel, starts, imaginary, ny, groups),
        [(groups * ny // 2, 2, NZ), (3, LX, LY, NZ)],
        [
            (2 * GROUP, 8, 2 * TILES * NZ),
            (GROUP, 8, 2 * TILES * NZ),
            (3 * groups * ny // 2, 2 * TILES * NZ),
        ],
        10_000_000,
    )(blocks, table, post3)
    parts = lax.all_to_all(parts, ("cy", "cx"), 0, 0, tiled=False)
    (running,) = call(last_kernel, [(3, 1, 2, SZ)], [], 100_000)(parts)
    return momentum, running


def solution(mesh):
    nx, ny = mesh.devices.shape
    devices = mesh.devices.reshape(nx // GROUP, 4, 2, 2, ny // 2)
    mesh = jax.sharding.Mesh(devices, GX + GY)
    in_specs = (P(None, GX, GY, None), P(GX, GY, None), P(None, GX, GY, None))
    out_specs = (P(None, GX, GY, None), P(None, GX, GY, None))
    return jax.shard_map(local, mesh=mesh, in_specs=in_specs, out_specs=out_specs, check_vma=False)
```
